128 devices in a mesh: exp: 8 (over z, core), tile: 16 (over y, x).
Axes of the slice: x: 4, y: 4, z: 4, core: 2. Of those that a mesh axis runs over, the one named last changes fastest.
Arguments:
- exposure: bfloat16 [8, 4096, 4096], P('exp', 'tile'), may hold values from -6 to 6
- row_taps: bfloat16 [3, 21], replicated, may hold values from -1.25 to 1.25
- column_taps: bfloat16 [3, 21], replicated, may hold values from -1.25 to 1.25
- basis_coef: float32 [8, 3], P('exp'), may hold values from -2.5 to 2.5
- warp_rows: bfloat16 [64, 128, 128], replicated, may hold values from -0.3 to 1.2
- warp_columns: bfloat16 [64, 128, 128], replicated, may hold values from -0.3 to 1.2
- warp_id: int32 [8, 16, 64], replicated, may hold values from 0 to 63
- route_device: int32 [8, 16, 64], replicated, may hold values from 0 to 127, as said below
- route_slot: int32 [8, 16, 64], replicated, may hold values from 0 to 63
- weight: float32 [8, 16], replicated, may hold values from 0.3 to 3
Outputs:
- coadd_patch: float32 [8192, 16384], P('exp', 'tile')
- difference: float32 [8, 4096, 4096], P('exp', 'tile')
The draws below stay inside these ranges and needn't reach their ends.
Inputs may be any that keep to these rules, and one draw needn't show every extreme that they name: `route_device`: the blocks of one device (its exposures of its tile, in order) name any one device at most 2 times, and some device is named exactly 2 times by the blocks of every device.
All inputs are finite; a program needn't handle non-finite values.
Results may differ from the reference program's by a relative error of at most 0.0058.
Values may be sent and summed in bfloat16 or wider, within the bound.
No kernel may reach another device: no remote copies, remote signals or barrier semaphores. Data moves between devices by JAX's collectives and lax.ppermute only.
A program may use at most 128 MiB of HBM per device.

```python
import math
import jax
import jax.numpy as jnp
from jax import lax

BLOCK = 128
COLS = 4096
TILE_ROWS = 256
EXP_DEV = 1
TAPS = 21
HALF = 10
BASES = 3
WARPS = 64
SLOT_ROWS = 8
SLOT_COLS = 8
EXPOSURES = 8
HEIGHT = 4096
BLOCKS_TILE = 64
SLOTS = 64
CAP = 2
N_EXP = 8
N_TILE = 16


def lanczos_bank(key):
    shift_key, noise_key, dense_key = jax.random.split(key, 3)
    offsets = jax.random.uniform(shift_key, (WARPS,), minval=0.15, maxval=0.45)
    jitter = jax.random.uniform(noise_key, (WARPS, BLOCK, BLOCK), minval=0.9, maxval=1.1)
    dense_part = jnp.clip(0.04 * jax.random.normal(dense_key, (WARPS, BLOCK, BLOCK)), -0.1, 0.1)
    column_lag = (jnp.arange(BLOCK)[None, :] - jnp.arange(BLOCK)[:, None]).astype(jnp.float32)
    argument = column_lag[None, :, :] - offsets[:, None, None]
    kernel = jnp.sinc(argument) * jnp.sinc(argument / 3.0)
    inside = ((column_lag >= -2.0) & (column_lag <= 3.0)).astype(jnp.float32)
    return (kernel * inside[None, :, :] * jitter + dense_part).astype(jnp.bfloat16)


def draw_warp_rows(key, part):
    return lanczos_bank(jax.random.fold_in(key, 101))


def draw_warp_columns(key, part):
    return lanczos_bank(jax.random.fold_in(key, 202))


def draw_route_device(key, part):
    devices = N_EXP * N_TILE
    per_device = EXP_DEV * BLOCKS_TILE
    capacity = CAP
    keys_all = jax.random.split(jax.random.fold_in(key, 303), 5)
    hot_device = jax.random.randint(keys_all[0], (), 0, devices)
    others = jax.random.permutation(keys_all[1], devices - 1)
    remaining = per_device - capacity
    least_group = max(1, (remaining + devices - 2) // (devices - 1))
    group_size = jax.random.randint(keys_all[2], (devices, 1), least_group, capacity + 1)
    start_group = jax.random.randint(keys_all[3], (devices, 1), 0, devices - 1)
    orders = jax.vmap(lambda one_key: jax.random.permutation(one_key, per_device))(jax.random.split(keys_all[4], devices))
    later = jnp.maximum(orders - capacity, 0)
    group_index = (start_group + later // group_size) % (devices - 1)
    other_device = (hot_device + 1 + others[group_index]) % devices
    target = jnp.where(orders < capacity, hot_device, other_device).astype(jnp.int32)
    target = target.reshape(N_EXP, N_TILE, EXP_DEV, BLOCKS_TILE).transpose(0, 2, 1, 3)
    return target.reshape(EXP_DEV * N_EXP, N_TILE, BLOCKS_TILE)


def with_ends(result, stream_key, least, largest):
    extent = result.shape
    index_at = [jax.random.randint(jax.random.fold_in(stream_key, axis), (), 0, extent[axis]) for axis in range(len(extent))]
    result = result.at[tuple(index_at)].set(least)
    longest = extent.index(max(extent))
    index_at[longest] = (index_at[longest] + 1) % extent[longest]
    return result.at[tuple(index_at)].set(largest)


def block_scale(own_key, dims, cuts, least, high):
    def one(axis_at, blocks):
        steps = jax.random.uniform(jax.random.fold_in(jax.random.fold_in(own_key, 6), axis_at), (blocks,), jnp.float32, least / len(cuts), high / len(cuts))
        return jnp.repeat(jnp.exp(steps), dims[axis_at] // blocks).reshape((-1,) + (1,) * (len(dims) - axis_at - 1))

    factor_of = one(*cuts[0])
    for cut in cuts[1:]:
        factor_of = factor_of * one(*cut)
    return factor_of


def scatter_about(key, dims, spread, most, cuts=(), dtype=jnp.bfloat16):
    array = spread * jax.random.normal(key, dims, jnp.float32)
    if cuts:
        array = array * block_scale(key, dims, cuts, -0.22, 0.18)
    return jnp.clip(array, -most, most).astype(dtype)


def setup_inputs(seed: int = 0) -> dict:
    streams_of = jax.random.split(jax.random.key(seed), 11)
    exposure = scatter_about(streams_of[0], (EXPOSURES, HEIGHT, COLS), 1.0, 6.0, ((0, 8), (1, 16)))
    row_taps = scatter_about(streams_of[1], (BASES, TAPS), TAPS ** -0.5, 1.25)
    column_taps = scatter_about(streams_of[2], (BASES, TAPS), TAPS ** -0.5, 1.25)
    basis_coef = scatter_about(streams_of[3], (EXPOSURES, BASES), 0.6, 2.5, ((0, 8),), jnp.float32)
    warp_rows = draw_warp_rows(jax.random.fold_in(streams_of[10], 71), 0)
    warp_columns = draw_warp_columns(jax.random.fold_in(streams_of[10], 71), 0)
    warp_id = with_ends(jax.random.randint(streams_of[6], (EXPOSURES, N_TILE, BLOCKS_TILE), 0, WARPS), jax.random.fold_in(streams_of[6], 1), 0, WARPS - 1).astype(jnp.int32)
    route_device = draw_route_device(jax.random.fold_in(streams_of[10], 71), 0)
    route_slot = with_ends(jax.random.randint(streams_of[8], (EXPOSURES, N_TILE, BLOCKS_TILE), 0, SLOTS), jax.random.fold_in(streams_of[8], 1), 0, SLOTS - 1).astype(jnp.int32)
    weight = jnp.clip(jnp.exp(jax.random.uniform(streams_of[9], (EXPOSURES, N_TILE), jnp.float32, math.log(0.3), math.log(3.0))), 0.3, 3.0)
    return {"exposure": exposure, "row_taps": row_taps, "column_taps": column_taps, "basis_coef": basis_coef, "warp_rows": warp_rows, "warp_columns": warp_columns, "warp_id": warp_id, "route_device": route_device, "route_slot": route_slot, "weight": weight}


def shifted_sum(picture, tap_values, axis_index):
    padded = jnp.pad(picture, ((HALF, HALF), (0, 0)) if axis_index == 0 else ((0, 0), (HALF, HALF)))
    summed = jnp.zeros_like(picture)
    length = picture.shape[axis_index]
    for tap_index in range(TAPS):
        window = lax.slice_in_dim(padded, tap_index, tap_index + length, axis=axis_index)
        summed = summed + tap_values[tap_index] * window
    return summed


def match_kernel(picture, row_taps, column_taps, coef_row):
    values = picture.astype(jnp.float32)
    summed = jnp.zeros_like(values)
    for basis_idx in range(BASES):
        row_pass = (coef_row[basis_idx] * shifted_sum(values, row_taps[basis_idx].astype(jnp.float32), 0)).astype(jnp.bfloat16)
        row_pass = lax.optimization_barrier(row_pass).astype(jnp.float32)
        summed = summed + shifted_sum(row_pass, column_taps[basis_idx].astype(jnp.float32), 1)
    return summed


def reference(exposure, row_taps, column_taps, basis_coef, warp_rows, warp_columns, warp_id, route_device, route_slot, weight):
    row_blocks = TILE_ROWS // BLOCK
    col_blocks = COLS // BLOCK
    devices = N_EXP * N_TILE
    row_warps = warp_rows.astype(jnp.float32)
    col_warps = warp_columns.astype(jnp.float32)

    def forward(inputs):
        picture, coef_row, idents, tile_weight = inputs
        matched = match_kernel(picture, row_taps, column_taps, coef_row).astype(jnp.bfloat16)
        matched = lax.optimization_barrier(matched).astype(jnp.float32)
        pieces = matched.reshape(N_TILE, row_blocks, BLOCK, col_blocks, BLOCK).transpose(0, 1, 3, 2, 4)
        pieces = pieces.reshape(N_TILE * BLOCKS_TILE, BLOCK, BLOCK)
        flat_ids = idents.reshape(-1)
        first_pass = jnp.einsum("bij,bjc->bic", row_warps[flat_ids], pieces).astype(jnp.bfloat16)
        first_pass = lax.optimization_barrier(first_pass).astype(jnp.float32)
        second_pass = jnp.einsum("bic,bkc->bik", first_pass, col_warps[flat_ids])
        block_weight = jnp.repeat(tile_weight, BLOCKS_TILE)
        return (block_weight[:, None, None] * second_pass).astype(jnp.bfloat16)

    weighted = lax.map(forward, (exposure, basis_coef, warp_id, weight))
    weighted = lax.optimization_barrier(weighted)
    target_slot = (route_device * SLOTS + route_slot).reshape(-1).astype(jnp.int32)
    flat_weight = jnp.repeat(weight.reshape(-1), BLOCKS_TILE)
    numerator = jax.ops.segment_sum(weighted.reshape(-1, BLOCK * BLOCK).astype(jnp.float32), target_slot, num_segments=devices * SLOTS)
    denominator = jax.ops.segment_sum(flat_weight, target_slot, num_segments=devices * SLOTS)
    coadd_slots = numerator / jnp.maximum(denominator, 1.0)[:, None]
    coadd_patch = coadd_slots.reshape(N_EXP, N_TILE, SLOT_ROWS, SLOT_COLS, BLOCK, BLOCK).transpose(0, 2, 4, 1, 3, 5)
    coadd_patch = coadd_patch.reshape(N_EXP * SLOT_ROWS * BLOCK, N_TILE * SLOT_COLS * BLOCK)
    templates = coadd_slots.astype(jnp.bfloat16)[target_slot].reshape(EXPOSURES, N_TILE * BLOCKS_TILE, BLOCK, BLOCK)

    def backward(inputs):
        picture, coef_row, idents, pieces = inputs
        flat_ids = idents.reshape(-1)
        pieces = lax.optimization_barrier(pieces).astype(jnp.float32)
        first_pass = jnp.einsum("bji,bjc->bic", row_warps[flat_ids], pieces).astype(jnp.bfloat16)
        first_pass = lax.optimization_barrier(first_pass).astype(jnp.float32)
        unwarped = jnp.einsum("bic,bck->bik", first_pass, col_warps[flat_ids]).astype(jnp.bfloat16)
        template_image = unwarped.reshape(N_TILE, row_blocks, col_blocks, BLOCK, BLOCK).transpose(0, 1, 3, 2, 4)
        template_image = lax.optimization_barrier(template_image.reshape(HEIGHT, COLS))
        return picture.astype(jnp.float32) - match_kernel(template_image, row_taps, column_taps, coef_row)

    difference = lax.map(backward, (exposure, basis_coef, warp_id, templates))
    return coadd_patch, difference
```

```python
import functools

import jax
import jax.numpy as jnp
from jax import lax
from jax.experimental import pallas as pl
from jax.experimental.pallas import tpu as pltpu
from jax.sharding import PartitionSpec as P

BLOCK = 128
HALF = 10
RIM = 16
CHUNK = 256
SLOT_ROWS = 8
SLOT_COLS = 8
LANES = 4
VMEM_BYTES = 60 * 1024 * 1024
VMEM = pl.BlockSpec(memory_space=pltpu.VMEM)
SMEM = pl.BlockSpec(memory_space=pltpu.SMEM)


def band_matrices(tap_values, depth, width, start, axis):
    grid = (
        lax.broadcasted_iota(jnp.int32, (depth, width), 0)
        - lax.broadcasted_iota(jnp.int32, (depth, width), 1)
        - start
    )
    bands = []
    for taps in tap_values.astype(jnp.float32):
        band = jnp.zeros((depth, width), jnp.float32)
        for tap_index in range(tap_values.shape[1]):
            band = jnp.where(grid == tap_index, taps[tap_index], band)
        bands.append(band.T if axis == 0 else band)
    return jnp.stack(bands).astype(jnp.bfloat16)


def rims(block):
    count = lax.axis_size("tile")
    forward = [(i, i + 1) for i in range(count - 1)]
    backward = [(target, source) for source, target in forward]
    above = lax.ppermute(block[block.shape[0] - RIM :], "tile", forward)
    below = lax.ppermute(block[:RIM], "tile", backward)
    return above, below


def row_step(step, chunks, coef_ref, above_ref, image_ref, below_ref, rows_ref, pass_ref):
    tile_rows = image_ref.shape[0]
    live = (step < chunks).astype(jnp.float32)
    for part in range(tile_rows // BLOCK):
        low = part * BLOCK - RIM
        high = (part + 1) * BLOCK + RIM
        pieces = [image_ref[max(low, 0) : min(high, tile_rows), :]]
        if low < 0:
            pieces.insert(0, above_ref[...])
        if high > tile_rows:
            pieces.append(below_ref[...])
        window = jnp.concatenate(pieces, axis=0)
        summed = jnp.dot(rows_ref[...], window, preferred_element_type=jnp.float32)
        for base in range(pass_ref.shape[0]):
            pass_ref[base, part * BLOCK : (part + 1) * BLOCK, pl.ds(BLOCK + step * CHUNK, CHUNK)] = (
                (coef_ref[0, base] * live) * summed[base * BLOCK : (base + 1) * BLOCK]
            ).astype(jnp.bfloat16)


def column_step(chunk, columns_ref, pass_ref):
    window = pl.ds(pl.multiple_of(chunk * CHUNK, CHUNK), CHUNK + 2 * BLOCK)
    summed = jnp.dot(pass_ref[0, :, window], columns_ref[0], preferred_element_type=jnp.float32)
    for base in range(1, pass_ref.shape[0]):
        summed = summed + jnp.dot(
            pass_ref[base, :, window], columns_ref[base], preferred_element_type=jnp.float32
        )
    return summed


def forward_kernel(
    ident_ref,
    weight_ref,
    coef_ref,
    above_ref,
    image_ref,
    below_ref,
    rows_ref,
    columns_ref,
    warp_rows_ref,
    warp_columns_ref,
    out_ref,
    pass_ref,
    turned_ref,
    *,
    chunks,
):
    step = pl.program_id(0)
    parts = image_ref.shape[0] // BLOCK
    side = CHUNK // BLOCK
    per_tile = parts * chunks * side

    @pl.when(step == 0)
    def _():
        pass_ref[:, :, :BLOCK] = jnp.zeros((pass_ref.shape[0], pass_ref.shape[1], BLOCK), jnp.bfloat16)

    chunk = jnp.maximum(step - 2, 0)
    matched = column_step(chunk, columns_ref, pass_ref).astype(jnp.bfloat16)
    for part in range(parts):
        for inner in range(side):
            index = part * (chunks * side) + chunk * side + inner
            ident = ident_ref[0, index]
            piece = matched[part * BLOCK : (part + 1) * BLOCK, inner * BLOCK : (inner + 1) * BLOCK]
            first = jnp.dot(
                warp_rows_ref[ident], piece, preferred_element_type=jnp.float32
            ).astype(jnp.bfloat16)
            second = lax.dot_general(
                first,
                warp_columns_ref[ident],
                (((1,), (1,)), ((), ())),
                preferred_element_type=jnp.float32,
            )
            turned_ref[pl.ds(index, BLOCK, stride=per_tile), :] = weight_ref[0, 0] * second
    row_step(step, chunks, coef_ref, above_ref, image_ref, below_ref, rows_ref, pass_ref)

    @pl.when(step == chunks + 1)
    def _():
        @pl.loop(0, BLOCK)
        def _(row):
            at = pl.ds(pl.multiple_of(row * per_tile, per_tile), per_tile)
            out_ref[at, :] = turned_ref[at, :].astype(jnp.bfloat16)


def forward(ident, weight, coef, above, image, below, rows, columns, warp_rows, warp_columns):
    tile_rows, width = image.shape
    chunks = width // CHUNK
    bases = columns.shape[0]
    items = tile_rows * width // BLOCK

    def at_column(step):
        return (0, jnp.minimum(step, chunks - 1))

    return pl.pallas_call(
        functools.partial(forward_kernel, chunks=chunks),
        out_shape=jax.ShapeDtypeStruct((items, BLOCK), jnp.bfloat16),
        grid=(chunks + 2,),
        in_specs=[
            SMEM,
            SMEM,
            SMEM,
            pl.BlockSpec((RIM, CHUNK), at_column),
            pl.BlockSpec((tile_rows, CHUNK), at_column),
            pl.BlockSpec((RIM, CHUNK), at_column),
            VMEM,
            VMEM,
            VMEM,
            VMEM,
        ],
        out_specs=pl.BlockSpec((items, BLOCK), lambda step: (0, 0)),
        scratch_shapes=[
            pltpu.VMEM((bases, tile_rows, BLOCK + (chunks + 2) * CHUNK), jnp.bfloat16),
            pltpu.VMEM((items, BLOCK), jnp.float32),
        ],
        compiler_params=pltpu.CompilerParams(
            dimension_semantics=("arbitrary",), vmem_limit_bytes=VMEM_BYTES
        ),
        name="match_warp",
    )(ident, weight, coef, above, image, below, rows, columns, warp_rows, warp_columns)


def slots_kernel(slot_ref, arrived_ref, total_ref, template_ref, coadd_ref, wide_ref, *sums):
    sources, per_tile = slot_ref.shape

    @pl.loop(0, sources)
    def _(source):
        at = pl.ds(pl.multiple_of(source * per_tile, per_tile), per_tile)
        wide_ref[at, :] = arrived_ref[at, :].astype(jnp.float32)
        for sum_ref in sums:
            sum_ref[at, :] = jnp.zeros((per_tile, BLOCK), jnp.float32)

    @pl.loop(0, sources)
    def _(source):
        for first in range(0, per_tile, len(sums)):
            slots = [slot_ref[source, first + lane] for lane in range(len(sums))]
            values = [
                sum_ref[pl.ds(slot, 1), :] + wide_ref[pl.ds(source * per_tile + first + lane, 1), :]
                for lane, (slot, sum_ref) in enumerate(zip(slots, sums))
            ]
            for slot, sum_ref, value in zip(slots, sums, values):
                sum_ref[pl.ds(slot, 1), :] = value

    @pl.loop(0, sources)
    def _(source):
        at = pl.ds(pl.multiple_of(source * per_tile, per_tile), per_tile)
        numerator = sums[0][at, :]
        for sum_ref in sums[1:]:
            numerator = numerator + sum_ref[at, :]
        value = numerator / jnp.maximum(total_ref[at, :], 1.0)
        sums[0][at, :] = value
        coadd_ref[at, :] = value.astype(jnp.bfloat16)

    @pl.loop(0, sources)
    def _(source):
        for item in range(per_tile):
            slot = slot_ref[source, item]
            wide_ref[pl.ds(source * per_tile + item, 1), :] = sums[0][pl.ds(slot, 1), :]

    @pl.loop(0, sources)
    def _(source):
        at = pl.ds(pl.multiple_of(source * per_tile, per_tile), per_tile)
        template_ref[at, :] = wide_ref[at, :].astype(jnp.bfloat16)


def slot_values(slots, arrived, total):
    shape = jax.ShapeDtypeStruct(arrived.shape, jnp.bfloat16)
    wide = pltpu.VMEM(arrived.shape, jnp.float32)
    return pl.pallas_call(
        slots_kernel,
        out_shape=(shape, shape),
        in_specs=[SMEM, VMEM, VMEM],
        out_specs=(VMEM, VMEM),
        scratch_shapes=[wide] * (1 + LANES),
        compiler_params=pltpu.CompilerParams(vmem_limit_bytes=VMEM_BYTES),
        name="slot_values",
    )(slots, arrived, total)


def unwarp_kernel(ident_ref, returned_ref, warp_rows_ref, warp_columns_ref, out_ref, wide_ref):
    per_tile = ident_ref.shape[1]
    across = out_ref.shape[1] // BLOCK

    @pl.loop(0, BLOCK)
    def _(row):
        at = pl.ds(pl.multiple_of(row * per_tile, per_tile), per_tile)
        wide_ref[at, :] = returned_ref[at, :].astype(jnp.float32)

    parts = out_ref.shape[0] // BLOCK

    @pl.loop(0, across // 2)
    def _(pair):
        for part in range(parts):
            for inner in range(2):
                column = pair * 2 + inner
                index = part * across + column
                ident = ident_ref[0, index]
                template = wide_ref[pl.ds(index, BLOCK, stride=per_tile), :].astype(jnp.bfloat16)
                first = lax.dot_general(
                    warp_rows_ref[ident],
                    template,
                    (((0,), (0,)), ((), ())),
                    preferred_element_type=jnp.float32,
                ).astype(jnp.bfloat16)
                out_ref[
                    part * BLOCK : (part + 1) * BLOCK,
                    pl.ds(pl.multiple_of(column * BLOCK, BLOCK), BLOCK),
                ] = jnp.dot(
                    first, warp_columns_ref[ident], preferred_element_type=jnp.float32
                ).astype(jnp.bfloat16)


def unwarp(ident, returned, warp_rows, warp_columns, tile_rows, width):
    return pl.pallas_call(
        unwarp_kernel,
        out_shape=jax.ShapeDtypeStruct((tile_rows, width), jnp.bfloat16),
        in_specs=[SMEM, VMEM, VMEM, VMEM],
        out_specs=VMEM,
        scratch_shapes=[pltpu.VMEM(returned.shape, jnp.float32)],
        compiler_params=pltpu.CompilerParams(vmem_limit_bytes=VMEM_BYTES),
        name="unwarp",
    )(ident, returned, warp_rows, warp_columns)


def subtract_kernel(
    coef_ref,
    above_ref,
    image_ref,
    below_ref,
    exposure_ref,
    rows_ref,
    columns_ref,
    out_ref,
    pass_ref,
    *,
    chunks,
):
    step = pl.program_id(0)

    @pl.when(step == 0)
    def _():
        pass_ref[:, :, :BLOCK] = jnp.zeros((pass_ref.shape[0], pass_ref.shape[1], BLOCK), jnp.bfloat16)

    chunk = jnp.maximum(step - 2, 0)
    out_ref[...] = exposure_ref[...].astype(jnp.float32) - column_step(chunk, columns_ref, pass_ref)
    row_step(step, chunks, coef_ref, above_ref, image_ref, below_ref, rows_ref, pass_ref)


def subtract(coef, above, image, below, exposure, rows, columns):
    tile_rows, width = image.shape
    chunks = width // CHUNK
    bases = columns.shape[0]

    def at_column(step):
        return (0, jnp.minimum(step, chunks - 1))

    def behind(step):
        return (0, jnp.maximum(step - 2, 0))

    return pl.pallas_call(
        functools.partial(subtract_kernel, chunks=chunks),
        out_shape=jax.ShapeDtypeStruct((tile_rows, width), jnp.float32),
        grid=(chunks + 2,),
        in_specs=[
            SMEM,
            pl.BlockSpec((RIM, CHUNK), at_column),
            pl.BlockSpec((tile_rows, CHUNK), at_column),
            pl.BlockSpec((RIM, CHUNK), at_column),
            pl.BlockSpec((tile_rows, CHUNK), behind),
            VMEM,
            VMEM,
        ],
        out_specs=pl.BlockSpec((tile_rows, CHUNK), behind),
        scratch_shapes=[
            pltpu.VMEM((bases, tile_rows, BLOCK + (chunks + 2) * CHUNK), jnp.bfloat16)
        ],
        compiler_params=pltpu.CompilerParams(
            dimension_semantics=("arbitrary",), vmem_limit_bytes=VMEM_BYTES
        ),
        name="match_subtract",
    )(coef, above, image, below, exposure, rows, columns)


def patch_kernel(rows_ref, out_ref, wide_ref):
    slots = SLOT_ROWS * SLOT_COLS

    @pl.loop(0, BLOCK)
    def _(row):
        at = pl.ds(pl.multiple_of(row * slots, slots), slots)
        wide_ref[at, :] = rows_ref[at, :].astype(jnp.float32)

    @pl.loop(0, SLOT_ROWS)
    def _(down):
        for across in range(SLOT_COLS):
            out_ref[
                pl.ds(pl.multiple_of(down * BLOCK, BLOCK), BLOCK),
                across * BLOCK : (across + 1) * BLOCK,
            ] = wide_ref[pl.ds(down * SLOT_COLS + across, BLOCK, stride=slots), :]


def patch(rows):
    return pl.pallas_call(
        patch_kernel,
        out_shape=jax.ShapeDtypeStruct((SLOT_ROWS * BLOCK, SLOT_COLS * BLOCK), jnp.float32),
        in_specs=[VMEM],
        out_specs=VMEM,
        scratch_shapes=[pltpu.VMEM(rows.shape, jnp.float32)],
        compiler_params=pltpu.CompilerParams(vmem_limit_bytes=VMEM_BYTES),
        name="patch",
    )(rows)


def exchange(rows, devices):
    shaped = rows.reshape(devices, -1, BLOCK)
    moved = lax.all_to_all(shaped, ("exp", "tile"), split_axis=0, concat_axis=0, tiled=True)
    return moved.reshape(rows.shape)


def shards(
    exposure,
    row_taps,
    column_taps,
    basis_coef,
    warp_rows,
    warp_columns,
    warp_id,
    route_device,
    route_slot,
    weight,
):
    devices = lax.axis_size("exp") * lax.axis_size("tile")
    image = exposure[0]
    tile_rows, width = image.shape
    per_tile = tile_rows * width // (BLOCK * BLOCK)
    slot_count = SLOT_ROWS * SLOT_COLS
    myself = lax.axis_index("exp") * lax.axis_size("tile") + lax.axis_index("tile")

    bases = row_taps.shape[0]
    rows = band_matrices(row_taps, BLOCK + 2 * RIM, BLOCK, RIM - HALF, 0)
    rows = rows.reshape(bases * BLOCK, BLOCK + 2 * RIM)
    columns = band_matrices(column_taps, CHUNK + 2 * BLOCK, CHUNK, BLOCK - HALF, 1)
    my_ident = lax.dynamic_slice_in_dim(warp_id.reshape(devices, per_tile), myself, 1, 0)
    my_weight = lax.dynamic_slice_in_dim(weight.reshape(devices, 1), myself, 1, 0)

    above, below = rims(image)
    mine = forward(
        my_ident, my_weight, basis_coef, above, image, below, rows, columns, warp_rows, warp_columns
    )
    arrived = exchange(mine, devices)

    owner = route_device.reshape(-1)
    place = route_slot.reshape(-1)
    block_weight = jnp.repeat(weight.reshape(-1), per_tile)
    by_owner = jnp.where(
        owner[None, :] == jnp.arange(devices, dtype=jnp.int32)[:, None], block_weight[None, :], 0.0
    )
    by_place = (place[:, None] == jnp.arange(slot_count, dtype=jnp.int32)[None, :]).astype(
        jnp.float32
    )
    total = jnp.dot(by_owner, by_place, precision=lax.Precision.HIGHEST)
    total = jnp.broadcast_to(total.reshape(-1, 1), (devices * slot_count, BLOCK))
    slots = (route_device * slot_count + route_slot).reshape(devices, per_tile)

    template_rows, coadd_rows = slot_values(slots, arrived, total)
    returned = exchange(template_rows, devices)
    owned = exchange(coadd_rows, devices)

    template = unwarp(my_ident, returned, warp_rows, warp_columns, tile_rows, width)
    above, below = rims(template)
    difference = subtract(basis_coef, above, template, below, image, rows, columns)
    return patch(owned), difference[None]


def solution(mesh):
    placed = (P("exp", "tile", None), P(), P(), P("exp", None), P(), P(), P(), P(), P(), P())
    return jax.shard_map(
        shards,
        mesh=mesh,
        in_specs=placed,
        out_specs=(P("exp", "tile"), P("exp", "tile", None)),
        check_vma=False,
    )
```

```python
import functools

import jax
import jax.numpy as jnp
from jax import lax
from jax.experimental import pallas as pl
from jax.experimental.pallas import tpu as pltpu
from jax.sharding import PartitionSpec as P

BLOCK = 128
HALF = 10
RIM = 16
CHUNK = 256
WIDE = 512
SPAN = CHUNK + 2 * BLOCK
WINDOW = BLOCK + 2 * RIM
SLOT_ROWS = 8
SLOT_COLS = 8
LANES = 4
PAD = 8
VMEM_BYTES = 60 * 1024 * 1024
VMEM = pl.BlockSpec(memory_space=pltpu.VMEM)
SMEM = pl.BlockSpec(memory_space=pltpu.SMEM)
ANY = pl.BlockSpec(memory_space=pl.ANY)
PARAMS = pltpu.CompilerParams(vmem_limit_bytes=VMEM_BYTES)


def bands_kernel(row_taps_ref, column_taps_ref, rows_ref, columns_ref):
    bases, taps = row_taps_ref.shape
    lead = RIM - HALF

    def banded(taps_ref, offsets):
        bands = [jnp.zeros(offsets.shape, jnp.float32) for _ in range(bases)]
        for tap in range(taps):
            hit = offsets == tap
            bands = [jnp.where(hit, taps_ref[base, tap], bands[base]) for base in range(bases)]
        return [band.astype(jnp.bfloat16) for band in bands]

    shape = (BLOCK, WINDOW)
    across = lax.broadcasted_iota(jnp.int32, shape, 1) - lax.broadcasted_iota(jnp.int32, shape, 0)
    for base, band in enumerate(banded(row_taps_ref, across - lead)):
        rows_ref[base * BLOCK : (base + 1) * BLOCK, :] = band
    shape = (WINDOW, BLOCK)
    down = lax.broadcasted_iota(jnp.int32, shape, 0) - lax.broadcasted_iota(jnp.int32, shape, 1)
    columns_ref[...] = jnp.zeros_like(columns_ref)
    for base, band in enumerate(banded(column_taps_ref, down - lead)):
        for part in range(CHUNK // BLOCK):
            top = base * SPAN + (part + 1) * BLOCK - RIM
            columns_ref[top : top + WINDOW, part * BLOCK : (part + 1) * BLOCK] = band


def band_matrices(row_taps, column_taps):
    bases = row_taps.shape[0]
    return pl.pallas_call(
        bands_kernel,
        out_shape=(
            jax.ShapeDtypeStruct((bases * BLOCK, WINDOW), jnp.bfloat16),
            jax.ShapeDtypeStruct((bases * SPAN, CHUNK), jnp.bfloat16),
        ),
        in_specs=[SMEM, SMEM],
        out_specs=(VMEM, VMEM),
        name="bands",
    )(row_taps.astype(jnp.float32), column_taps.astype(jnp.float32))


def swap_rims(top, bottom):
    count = lax.axis_size("tile")
    forward = [(i, i + 1) for i in range(count - 1)]
    backward = [(target, source) for source, target in forward]
    return lax.ppermute(bottom, "tile", forward), lax.ppermute(top, "tile", backward)


def clear_sides(pass_ref):
    bases, height, width = pass_ref.shape
    side = jnp.zeros((bases, height, BLOCK), pass_ref.dtype)
    pass_ref[:, :, :BLOCK] = side
    pass_ref[:, :, width - BLOCK :] = side


def row_step(index, strips, coef_ref, rows_ref, pass_ref):
    bases = pass_ref.shape[0]
    columns = pl.ds(pl.multiple_of(index * WIDE, WIDE), WIDE)
    for start, count, pieces in strips:
        window = [ref[first : first + size, columns] for ref, first, size in pieces]
        window = window[0] if len(window) == 1 else jnp.concatenate(window, axis=0)
        depth = window.shape[0]
        if count == BLOCK and depth == WINDOW:
            band = rows_ref[...]
        else:
            band = jnp.concatenate(
                [rows_ref[base * BLOCK : base * BLOCK + count, :depth] for base in range(bases)],
                axis=0,
            )
        summed = jnp.dot(band, window, preferred_element_type=jnp.float32)
        to = pl.ds(pl.multiple_of(index * WIDE + BLOCK, BLOCK), WIDE)
        for base in range(bases):
            pass_ref[base, start : start + count, to] = (
                coef_ref[0, base] * summed[base * count : (base + 1) * count]
            ).astype(jnp.bfloat16)


def column_step(index, start, count, columns_ref, pass_ref):
    bases = pass_ref.shape[0]
    parts = []
    for part in range(WIDE // CHUNK):
        window = pl.ds(pl.multiple_of(index * WIDE + part * CHUNK, CHUNK), SPAN)
        parts.append(
            jnp.concatenate(
                [pass_ref[base, start : start + count, window] for base in range(bases)], axis=1
            )
        )
    summed = jnp.dot(
        jnp.concatenate(parts, axis=0), columns_ref[...], preferred_element_type=jnp.float32
    )
    return [summed[part * count : (part + 1) * count] for part in range(WIDE // CHUNK)]


def forward_kernel(
    ident_ref,
    weight_ref,
    coef_ref,
    above_ref,
    image_ref,
    below_ref,
    rows_ref,
    columns_ref,
    bank_rows_ref,
    bank_columns_ref,
    out_ref,
    pass_ref,
    turned_ref,
    warp_rows_ref,
    warp_columns_ref,
    sems,
):
    tile_rows, width = image_ref.shape
    across = width // BLOCK
    per_tile = tile_rows // BLOCK * across
    pitch = per_tile + PAD
    wides = width // WIDE
    loads = [
        pltpu.make_async_copy(bank_rows_ref, warp_rows_ref, sems.at[0]),
        pltpu.make_async_copy(bank_columns_ref, warp_columns_ref, sems.at[1]),
    ]
    for load in loads:
        load.start()

    strips = [
        (0, BLOCK, [(above_ref, 0, RIM), (image_ref, 0, BLOCK + RIM)]),
        (BLOCK, BLOCK, [(image_ref, BLOCK - RIM, BLOCK + RIM), (below_ref, 0, RIM)]),
    ]
    clear_sides(pass_ref)
    row_step(0, strips, coef_ref, rows_ref, pass_ref)
    row_step(1, strips, coef_ref, rows_ref, pass_ref)
    for load in loads:
        load.wait()

    def warp_step(index):
        for half, summed in enumerate(column_step(index, 0, tile_rows, columns_ref, pass_ref)):
            matched = summed.astype(jnp.bfloat16)
            for part in range(tile_rows // BLOCK):
                for inner in range(CHUNK // BLOCK):
                    column = index * (WIDE // BLOCK) + half * (CHUNK // BLOCK) + inner
                    block = part * across + column
                    ident = ident_ref[0, block]
                    piece = matched[
                        part * BLOCK : (part + 1) * BLOCK, inner * BLOCK : (inner + 1) * BLOCK
                    ]
                    first = jnp.dot(
                        warp_rows_ref[ident], piece, preferred_element_type=jnp.float32
                    ).astype(jnp.bfloat16)
                    second = lax.dot_general(
                        first,
                        warp_columns_ref[ident],
                        (((1,), (1,)), ((), ())),
                        preferred_element_type=jnp.float32,
                    )
                    turned_ref[pl.ds(block, BLOCK, stride=pitch), :] = weight_ref[0, 0] * second

    @pl.loop(0, wides - 2)
    def _(index):
        warp_step(index)
        row_step(index + 2, strips, coef_ref, rows_ref, pass_ref)

    @pl.loop(wides - 2, wides)
    def _(index):
        warp_step(index)

    @pl.loop(0, BLOCK, unroll=2)
    def _(row):
        to = pl.ds(pl.multiple_of(row * per_tile, per_tile), per_tile)
        at = pl.ds(pl.multiple_of(row * pitch, PAD), per_tile)
        out_ref[to, :] = turned_ref[at, :].astype(jnp.bfloat16)


def forward(ident, weight, coef, above, image, below, rows, columns, warp_rows, warp_columns):
    tile_rows, width = image.shape
    bases = rows.shape[0] // BLOCK
    items = tile_rows * width // BLOCK
    return pl.pallas_call(
        forward_kernel,
        out_shape=jax.ShapeDtypeStruct((items, BLOCK), jnp.bfloat16),
        in_specs=[SMEM, SMEM, SMEM, VMEM, VMEM, VMEM, VMEM, VMEM, ANY, ANY],
        out_specs=VMEM,
        scratch_shapes=[
            pltpu.VMEM((bases, tile_rows, width + 2 * BLOCK), jnp.bfloat16),
            pltpu.VMEM((items + BLOCK * PAD, BLOCK), jnp.float32),
            pltpu.VMEM(warp_rows.shape, jnp.bfloat16),
            pltpu.VMEM(warp_columns.shape, jnp.bfloat16),
            pltpu.SemaphoreType.DMA((2,)),
        ],
        compiler_params=PARAMS,
        name="match_warp",
    )(ident, weight, coef, above, image, below, rows, columns, warp_rows, warp_columns)


def slots_kernel(slot_ref, arrived_ref, template_ref, coadd_ref, wide_ref, *sums):
    sources, per_tile = slot_ref.shape

    def at(source):
        return pl.ds(pl.multiple_of(source * per_tile, per_tile), per_tile)

    @pl.loop(0, sources)
    def _(source):
        wide_ref[at(source), :] = arrived_ref[at(source), :].astype(jnp.float32)
        for sum_ref in sums:
            sum_ref[at(source), :] = jnp.zeros((per_tile, BLOCK), jnp.float32)

    @pl.loop(0, sources)
    def _(source):
        for first in range(0, per_tile, len(sums)):
            slots = [slot_ref[source, first + lane] for lane in range(len(sums))]
            values = [
                sum_ref[pl.ds(slot, 1), :] + wide_ref[pl.ds(source * per_tile + first + lane, 1), :]
                for lane, (slot, sum_ref) in enumerate(zip(slots, sums))
            ]
            for slot, sum_ref, value in zip(slots, sums, values):
                sum_ref[pl.ds(slot, 1), :] = value

    @pl.loop(0, sources)
    def _(source):
        value = sums[0][at(source), :]
        for sum_ref in sums[1:]:
            value = value + sum_ref[at(source), :]
        sums[0][at(source), :] = value
        coadd_ref[at(source), :] = value.astype(jnp.bfloat16)

    @pl.loop(0, sources)
    def _(source):
        for item in range(per_tile):
            slot = slot_ref[source, item]
            wide_ref[pl.ds(source * per_tile + item, 1), :] = sums[0][pl.ds(slot, 1), :]

    @pl.loop(0, sources)
    def _(source):
        template_ref[at(source), :] = wide_ref[at(source), :].astype(jnp.bfloat16)


def slot_sums(slots, arrived):
    shape = jax.ShapeDtypeStruct(arrived.shape, jnp.bfloat16)
    return pl.pallas_call(
        slots_kernel,
        out_shape=(shape, shape),
        in_specs=[SMEM, VMEM],
        out_specs=(VMEM, VMEM),
        scratch_shapes=[pltpu.VMEM(arrived.shape, jnp.float32)] * (1 + LANES),
        compiler_params=PARAMS,
        name="slot_sums",
    )(slots, arrived)


def unwarp_kernel(
    ident_ref,
    scale_ref,
    returned_ref,
    bank_rows_ref,
    bank_columns_ref,
    out_ref,
    top_ref,
    bottom_ref,
    wide_ref,
    warp_rows_ref,
    warp_columns_ref,
    sems,
):
    tile_rows, width = out_ref.shape
    across = width // BLOCK
    parts = tile_rows // BLOCK
    per_tile = ident_ref.shape[1]
    pitch = per_tile + PAD
    loads = [
        pltpu.make_async_copy(bank_rows_ref, warp_rows_ref, sems.at[0]),
        pltpu.make_async_copy(bank_columns_ref, warp_columns_ref, sems.at[1]),
    ]
    for load in loads:
        load.start()

    @pl.loop(0, BLOCK, unroll=2)
    def _(row):
        to = pl.ds(pl.multiple_of(row * pitch, PAD), per_tile)
        at = pl.ds(pl.multiple_of(row * per_tile, per_tile), per_tile)
        wide_ref[to, :] = returned_ref[at, :].astype(jnp.float32)

    for load in loads:
        load.wait()

    @pl.loop(0, across // 4)
    def _(quad):
        for part in range(parts):
            for inner in range(4):
                column = quad * 4 + inner
                block = part * across + column
                ident = ident_ref[0, block]
                numerator = wide_ref[pl.ds(block, BLOCK, stride=pitch), :].astype(jnp.bfloat16)
                first = lax.dot_general(
                    warp_rows_ref[ident],
                    numerator,
                    (((0,), (0,)), ((), ())),
                    preferred_element_type=jnp.float32,
                )
                image = jnp.dot(
                    (scale_ref[0, block] * first).astype(jnp.bfloat16),
                    warp_columns_ref[ident],
                    preferred_element_type=jnp.float32,
                ).astype(jnp.bfloat16)
                to = pl.ds(pl.multiple_of(column * BLOCK, BLOCK), BLOCK)
                out_ref[part * BLOCK : (part + 1) * BLOCK, to] = image
                if part == 0:
                    top_ref[:, to] = image[:RIM]
                if part == parts - 1:
                    bottom_ref[:, to] = image[BLOCK - RIM :]


def unwarp(ident, scale, returned, warp_rows, warp_columns, tile_rows, width):
    rim = jax.ShapeDtypeStruct((RIM, width), jnp.bfloat16)
    return pl.pallas_call(
        unwarp_kernel,
        out_shape=(jax.ShapeDtypeStruct((tile_rows, width), jnp.bfloat16), rim, rim),
        in_specs=[SMEM, SMEM, VMEM, ANY, ANY],
        out_specs=(VMEM, VMEM, VMEM),
        scratch_shapes=[
            pltpu.VMEM((returned.shape[0] + BLOCK * PAD, BLOCK), jnp.float32),
            pltpu.VMEM(warp_rows.shape, jnp.bfloat16),
            pltpu.VMEM(warp_columns.shape, jnp.bfloat16),
            pltpu.SemaphoreType.DMA((2,)),
        ],
        compiler_params=PARAMS,
        name="unwarp",
    )(ident, scale, returned, warp_rows, warp_columns)


def inner_kernel(
    coef_ref, image_ref, exposure_ref, rows_ref, columns_ref, out_ref, pass_ref, stage_ref, sems
):
    tile_rows, width = image_ref.shape
    wides = width // WIDE
    inner = tile_rows - 2 * RIM
    rest = inner - BLOCK
    strips = [
        (0, BLOCK, [(image_ref, 0, WINDOW)]),
        (BLOCK, rest, [(image_ref, BLOCK, tile_rows - BLOCK)]),
    ]
    clear_sides(pass_ref)
    row_step(0, strips, coef_ref, rows_ref, pass_ref)
    row_step(1, strips, coef_ref, rows_ref, pass_ref)

    def store(index):
        at = pl.ds(pl.multiple_of(index * WIDE, WIDE), WIDE)
        return pltpu.make_async_copy(
            stage_ref.at[:, at], out_ref.at[pl.ds(RIM, inner), at], sems.at[index]
        )

    def subtract_step(index):
        for half, summed in enumerate(column_step(index, 0, inner, columns_ref, pass_ref)):
            at = pl.ds(pl.multiple_of(index * WIDE + half * CHUNK, CHUNK), CHUNK)
            stage_ref[:, at] = (
                exposure_ref[RIM : RIM + inner, at].astype(jnp.float32) - summed
            )
        store(index).start()

    @pl.loop(0, wides - 2)
    def _(index):
        subtract_step(index)
        row_step(index + 2, strips, coef_ref, rows_ref, pass_ref)

    @pl.loop(wides - 2, wides)
    def _(index):
        subtract_step(index)

    @pl.loop(0, wides)
    def _(index):
        store(index).wait()


def subtract_inner(coef, image, exposure, rows, columns):
    tile_rows, width = image.shape
    bases = rows.shape[0] // BLOCK
    inner = tile_rows - 2 * RIM
    return pl.pallas_call(
        inner_kernel,
        out_shape=jax.ShapeDtypeStruct((tile_rows, width), jnp.float32),
        in_specs=[SMEM, VMEM, VMEM, VMEM, VMEM],
        out_specs=ANY,
        scratch_shapes=[
            pltpu.VMEM((bases, inner, width + 2 * BLOCK), jnp.bfloat16),
            pltpu.VMEM((inner, width), jnp.float32),
            pltpu.SemaphoreType.DMA((width // WIDE,)),
        ],
        compiler_params=PARAMS,
        name="subtract_inner",
    )(coef, image, exposure, rows, columns)


def outer_kernel(
    coef_ref,
    above_ref,
    top_ref,
    bottom_ref,
    below_ref,
    exposure_top_ref,
    exposure_bottom_ref,
    rows_ref,
    columns_ref,
    partial_ref,
    out_ref,
    pass_ref,
    stage_ref,
    sems,
):
    del partial_ref
    width = top_ref.shape[1]
    tile_rows = out_ref.shape[0]
    wides = width // WIDE
    strips = [
        (0, RIM, [(above_ref, 0, RIM), (top_ref, 0, 2 * RIM)]),
        (RIM, RIM, [(bottom_ref, 0, 2 * RIM), (below_ref, 0, RIM)]),
    ]
    clear_sides(pass_ref)
    for index in range(wides):
        row_step(index, strips, coef_ref, rows_ref, pass_ref)
    for index in range(wides):
        for half, summed in enumerate(column_step(index, 0, 2 * RIM, columns_ref, pass_ref)):
            at = pl.ds(index * WIDE + half * CHUNK, CHUNK)
            stage_ref[:RIM, at] = exposure_top_ref[:, at].astype(jnp.float32) - summed[:RIM]
            stage_ref[RIM:, at] = exposure_bottom_ref[:, at].astype(jnp.float32) - summed[RIM:]
    stores = [
        pltpu.make_async_copy(stage_ref.at[:RIM], out_ref.at[:RIM], sems.at[0]),
        pltpu.make_async_copy(
            stage_ref.at[RIM:], out_ref.at[pl.ds(tile_rows - RIM, RIM)], sems.at[1]
        ),
    ]
    for store in stores:
        store.start()
    for store in stores:
        store.wait()


def subtract_outer(coef, above, image, below, exposure, rows, columns, partial):
    tile_rows, width = image.shape
    bases = rows.shape[0] // BLOCK
    rim = pl.BlockSpec((RIM, width), lambda _: (0, 0))
    last_rim = pl.BlockSpec((RIM, width), lambda _: (tile_rows // RIM - 1, 0))
    pair = pl.BlockSpec((2 * RIM, width), lambda _: (0, 0))
    last_pair = pl.BlockSpec((2 * RIM, width), lambda _: (tile_rows // (2 * RIM) - 1, 0))
    return pl.pallas_call(
        outer_kernel,
        out_shape=jax.ShapeDtypeStruct((tile_rows, width), jnp.float32),
        grid=(1,),
        in_specs=[SMEM, VMEM, pair, last_pair, VMEM, rim, last_rim, VMEM, VMEM, ANY],
        out_specs=ANY,
        scratch_shapes=[
            pltpu.VMEM((bases, 2 * RIM, width + 2 * BLOCK), jnp.bfloat16),
            pltpu.VMEM((2 * RIM, width), jnp.float32),
            pltpu.SemaphoreType.DMA((2,)),
        ],
        input_output_aliases={9: 0},
        compiler_params=PARAMS,
        name="subtract_outer",
    )(coef, above, image, image, below, exposure, exposure, rows, columns, partial)


def patch_kernel(scale_ref, rows_ref, out_ref, wide_ref, stage_ref, sems):
    slots = SLOT_ROWS * SLOT_COLS
    pitch = slots + PAD

    @pl.loop(0, BLOCK, unroll=2)
    def _(row):
        to = pl.ds(pl.multiple_of(row * pitch, PAD), slots)
        at = pl.ds(pl.multiple_of(row * slots, slots), slots)
        wide_ref[to, :] = rows_ref[at, :].astype(jnp.float32)

    def store(down):
        at = pl.ds(pl.multiple_of(down * BLOCK, BLOCK), BLOCK)
        return pltpu.make_async_copy(stage_ref.at[at], out_ref.at[at], sems.at[down])

    @pl.loop(0, SLOT_ROWS)
    def _(down):
        to = pl.ds(pl.multiple_of(down * BLOCK, BLOCK), BLOCK)
        for across in range(SLOT_COLS):
            slot = down * SLOT_COLS + across
            stage_ref[to, across * BLOCK : (across + 1) * BLOCK] = (
                scale_ref[0, slot] * wide_ref[pl.ds(slot, BLOCK, stride=pitch), :]
            )
        store(down).start()

    @pl.loop(0, SLOT_ROWS)
    def _(down):
        store(down).wait()


def patch(scale, rows):
    shape = (SLOT_ROWS * BLOCK, SLOT_COLS * BLOCK)
    return pl.pallas_call(
        patch_kernel,
        out_shape=jax.ShapeDtypeStruct(shape, jnp.float32),
        in_specs=[SMEM, VMEM],
        out_specs=ANY,
        scratch_shapes=[
            pltpu.VMEM((rows.shape[0] + BLOCK * PAD, BLOCK), jnp.float32),
            pltpu.VMEM(shape, jnp.float32),
            pltpu.SemaphoreType.DMA((SLOT_ROWS,)),
        ],
        compiler_params=PARAMS,
        name="patch",
    )(scale, rows)


def exchange(rows, devices):
    shaped = rows.reshape(devices, -1, BLOCK)
    moved = lax.all_to_all(shaped, ("exp", "tile"), split_axis=0, concat_axis=0, tiled=True)
    return moved.reshape(rows.shape)


def shards(
    exposure,
    row_taps,
    column_taps,
    basis_coef,
    warp_rows,
    warp_columns,
    warp_id,
    route_device,
    route_slot,
    weight,
):
    devices = lax.axis_size("exp") * lax.axis_size("tile")
    image = exposure[0]
    tile_rows, width = image.shape
    per_tile = tile_rows * width // (BLOCK * BLOCK)
    slot_count = SLOT_ROWS * SLOT_COLS
    myself = lax.axis_index("exp") * lax.axis_size("tile") + lax.axis_index("tile")

    def mine(table):
        return lax.dynamic_slice_in_dim(table.reshape(devices, -1), myself, 1, 0)

    above, below = swap_rims(image[:RIM], image[tile_rows - RIM :])
    rows, columns = band_matrices(row_taps, column_taps)
    my_ident = mine(warp_id)
    my_weight = mine(weight)
    weighted = forward(
        my_ident, my_weight, basis_coef, above, image, below, rows, columns, warp_rows, warp_columns
    )
    arrived = exchange(weighted, devices)

    owner = route_device.reshape(-1)
    place = route_slot.reshape(-1)
    block_weight = jnp.repeat(weight.reshape(-1), per_tile)
    by_owner = jnp.where(
        owner[None, :] == jnp.arange(devices, dtype=jnp.int32)[:, None], block_weight[None, :], 0.0
    )
    by_place = (place[:, None] == jnp.arange(slot_count, dtype=jnp.int32)[None, :]).astype(
        jnp.float32
    )
    total = jnp.dot(by_owner, by_place, precision=lax.Precision.HIGHEST)
    scale = 1.0 / jnp.maximum(total, 1.0)
    slots = (route_device * slot_count + route_slot).reshape(devices, per_tile)
    owned_scale = mine(scale)
    block_scale = scale.reshape(-1)[mine(slots)]

    template_rows, coadd_rows = slot_sums(slots, arrived)
    returned = exchange(template_rows, devices)
    owned = exchange(coadd_rows, devices)

    template, top, bottom = unwarp(
        my_ident, block_scale, returned, warp_rows, warp_columns, tile_rows, width
    )
    above, below = swap_rims(top, bottom)
    difference = subtract_inner(basis_coef, template, image, rows, columns)
    difference = subtract_outer(
        basis_coef, above, template, below, image, rows, columns, difference
    )
    return patch(owned_scale, owned), difference[None]


def solution(mesh):
    placed = (P("exp", "tile", None), P(), P(), P("exp", None), P(), P(), P(), P(), P(), P())
    return jax.shard_map(
        shards,
        mesh=mesh,
        in_specs=placed,
        out_specs=(P("exp", "tile"), P("exp", "tile", None)),
        check_vma=False,
    )
```

```python
import functools

import jax
import jax.numpy as jnp
from jax import lax
from jax.experimental import pallas as pl
from jax.experimental.pallas import tpu as pltpu
from jax.sharding import PartitionSpec as P

BLOCK = 128
HALF = 10
RIM = 16
CHUNK = 256
WIDE = 512
SPAN = CHUNK + 2 * BLOCK
WINDOW = BLOCK + 2 * RIM
HALVES = 2
LEFT = 3
SLOT_ROWS = 8
SLOT_COLS = 8
LANES = 4
PAD = 8
VMEM_BYTES = 60 * 1024 * 1024
VMEM = pl.BlockSpec(memory_space=pltpu.VMEM)
SMEM = pl.BlockSpec(memory_space=pltpu.SMEM)
ANY = pl.BlockSpec(memory_space=pl.ANY)
PARAMS = pltpu.CompilerParams(vmem_limit_bytes=VMEM_BYTES)


def bands_kernel(row_taps_ref, column_taps_ref, rows_ref, columns_ref):
    bases, taps = row_taps_ref.shape
    lead = RIM - HALF

    def banded(taps_ref, offsets):
        bands = [jnp.zeros(offsets.shape, jnp.float32) for _ in range(bases)]
        for tap in range(taps):
            hit = offsets == tap
            bands = [jnp.where(hit, taps_ref[base, tap], bands[base]) for base in range(bases)]
        return [band.astype(jnp.bfloat16) for band in bands]

    shape = (BLOCK, WINDOW)
    across = lax.broadcasted_iota(jnp.int32, shape, 1) - lax.broadcasted_iota(jnp.int32, shape, 0)
    for base, band in enumerate(banded(row_taps_ref, across - lead)):
        rows_ref[base * BLOCK : (base + 1) * BLOCK, :] = band
    shape = (WINDOW, BLOCK)
    down = lax.broadcasted_iota(jnp.int32, shape, 0) - lax.broadcasted_iota(jnp.int32, shape, 1)
    columns_ref[...] = jnp.zeros_like(columns_ref)
    for base, band in enumerate(banded(column_taps_ref, down - lead)):
        for part in range(CHUNK // BLOCK):
            top = base * SPAN + (part + 1) * BLOCK - RIM
            columns_ref[top : top + WINDOW, part * BLOCK : (part + 1) * BLOCK] = band


def band_matrices(row_taps, column_taps):
    bases = row_taps.shape[0]
    return pl.pallas_call(
        bands_kernel,
        out_shape=(
            jax.ShapeDtypeStruct((bases * BLOCK, WINDOW), jnp.bfloat16),
            jax.ShapeDtypeStruct((bases * SPAN, CHUNK), jnp.bfloat16),
        ),
        in_specs=[SMEM, SMEM],
        out_specs=(VMEM, VMEM),
        name="bands",
    )(row_taps.astype(jnp.float32), column_taps.astype(jnp.float32))


def swap_rims(top, bottom):
    count = lax.axis_size("tile")
    forward = [(i, i + 1) for i in range(count - 1)]
    backward = [(target, source) for source, target in forward]
    return lax.ppermute(bottom, "tile", forward), lax.ppermute(top, "tile", backward)


def clear(pass_ref, start):
    bases, height, _ = pass_ref.shape
    pass_ref[:, :, start : start + BLOCK] = jnp.zeros((bases, height, BLOCK), pass_ref.dtype)


def row_step(lanes, start, to, strips, coef_ref, rows_ref, pass_ref):
    bases = pass_ref.shape[0]
    for first_row, count, pieces in strips:
        window = [
            ref[first : first + size, pl.ds(pl.multiple_of(start + shift, BLOCK), lanes)]
            for ref, first, size, shift in pieces
        ]
        window = window[0] if len(window) == 1 else jnp.concatenate(window, axis=0)
        depth = window.shape[0]
        if count == BLOCK and depth == WINDOW:
            band = rows_ref[...]
        else:
            band = jnp.concatenate(
                [rows_ref[base * BLOCK : base * BLOCK + count, :depth] for base in range(bases)],
                axis=0,
            )
        summed = jnp.dot(band, window, preferred_element_type=jnp.float32)
        for base in range(bases):
            pass_ref[
                base, first_row : first_row + count, pl.ds(pl.multiple_of(to, BLOCK), lanes)
            ] = (coef_ref[0, base] * summed[base * count : (base + 1) * count]).astype(jnp.bfloat16)


def column_step(index, count, columns_ref, pass_ref):
    bases = pass_ref.shape[0]
    parts = []
    for part in range(WIDE // CHUNK):
        window = pl.ds(pl.multiple_of(index * WIDE + part * CHUNK, CHUNK), SPAN)
        parts.append(
            jnp.concatenate([pass_ref[base, :count, window] for base in range(bases)], axis=1)
        )
    summed = jnp.dot(
        jnp.concatenate(parts, axis=0), columns_ref[...], preferred_element_type=jnp.float32
    )
    return [summed[part * count : (part + 1) * count] for part in range(WIDE // CHUNK)]


def forward_kernel(
    ident_ref,
    weight_ref,
    coef_ref,
    above_ref,
    image_hbm,
    below_ref,
    rows_ref,
    columns_ref,
    bank_rows_ref,
    bank_columns_ref,
    out_ref,
    image_ref,
    pass_ref,
    matched_ref,
    turned_ref,
    warp_rows_ref,
    warp_columns_ref,
    sems,
    *,
    half,
):
    tile_rows, width = image_hbm.shape
    part_width = width // HALVES
    parts = tile_rows // BLOCK
    across = part_width // BLOCK
    items = parts * across
    pitch = items + PAD
    wides = part_width // WIDE
    low = max(half * part_width - BLOCK, 0)
    high = min((half + 1) * part_width + BLOCK, width)
    offset = half * part_width - BLOCK
    fetch = pltpu.make_async_copy(
        image_hbm.at[:, low:high], image_ref.at[:, low - offset : high - offset], sems.at[0]
    )
    loads = [
        pltpu.make_async_copy(bank_rows_ref, warp_rows_ref, sems.at[1]),
        pltpu.make_async_copy(bank_columns_ref, warp_columns_ref, sems.at[2]),
    ]
    fetch.start()
    for load in loads:
        load.start()
    fetch.wait()

    strips = [
        (0, BLOCK, [(above_ref, 0, RIM, offset), (image_ref, 0, BLOCK + RIM, 0)]),
        (
            BLOCK,
            BLOCK,
            [(image_ref, BLOCK - RIM, BLOCK + RIM, 0), (below_ref, 0, RIM, offset)],
        ),
    ]
    step = functools.partial(
        row_step, strips=strips, coef_ref=coef_ref, rows_ref=rows_ref, pass_ref=pass_ref
    )
    if low == offset:
        step(BLOCK, 0, 0)
    else:
        clear(pass_ref, 0)
    last = BLOCK + part_width
    if high == (half + 1) * part_width + BLOCK:
        step(BLOCK, last, last)
    else:
        clear(pass_ref, last)

    def wide_step(index):
        step(WIDE, BLOCK + index * WIDE, BLOCK + index * WIDE)

    def match_step(index):
        for inner, summed in enumerate(column_step(index, tile_rows, columns_ref, pass_ref)):
            matched_ref[:, pl.ds(pl.multiple_of(index * WIDE + inner * CHUNK, CHUNK), CHUNK)] = (
                summed.astype(jnp.bfloat16)
            )

    wide_step(0)
    wide_step(1)

    @pl.loop(0, wides - 2)
    def _(index):
        match_step(index)
        wide_step(index + 2)

    @pl.loop(wides - 2, wides)
    def _(index):
        match_step(index)

    for load in loads:
        load.wait()

    @pl.loop(0, across // 4)
    def _(quad):
        todo = []
        for part in range(parts):
            for inner in range(4):
                column = quad * 4 + inner
                ident = ident_ref[0, part * (across * HALVES) + half * across + column]
                piece = matched_ref[
                    part * BLOCK : (part + 1) * BLOCK,
                    pl.ds(pl.multiple_of(column * BLOCK, BLOCK), BLOCK),
                ]
                todo.append((part * across + column, ident, piece))
        todo = [
            (
                item,
                ident,
                jnp.dot(warp_rows_ref[ident], piece, preferred_element_type=jnp.float32).astype(
                    jnp.bfloat16
                ),
            )
            for item, ident, piece in todo
        ]
        todo = [
            (
                item,
                lax.dot_general(
                    first,
                    warp_columns_ref[ident],
                    (((1,), (1,)), ((), ())),
                    preferred_element_type=jnp.float32,
                ),
            )
            for item, ident, first in todo
        ]
        for item, second in todo:
            turned_ref[pl.ds(item, BLOCK, stride=pitch), :] = weight_ref[0, 0] * second

    @pl.loop(0, BLOCK, unroll=4)
    def _(row):
        to = pl.ds(pl.multiple_of(row * items, items), items)
        at = pl.ds(pl.multiple_of(row * pitch, PAD), items)
        out_ref[to, :] = turned_ref[at, :].astype(jnp.bfloat16)


def forward(half, ident, weight, coef, above, image, below, rows, columns, warp_rows, warp_columns):
    tile_rows, width = image.shape
    bases = rows.shape[0] // BLOCK
    part_width = width // HALVES
    lines = tile_rows * part_width // BLOCK
    return pl.pallas_call(
        functools.partial(forward_kernel, half=half),
        out_shape=jax.ShapeDtypeStruct((lines, BLOCK), jnp.bfloat16),
        in_specs=[SMEM, SMEM, SMEM, VMEM, ANY, VMEM, VMEM, VMEM, ANY, ANY],
        out_specs=VMEM,
        scratch_shapes=[
            pltpu.VMEM((tile_rows, part_width + 2 * BLOCK), jnp.bfloat16),
            pltpu.VMEM((bases, tile_rows, part_width + 2 * BLOCK), jnp.bfloat16),
            pltpu.VMEM((tile_rows, part_width), jnp.bfloat16),
            pltpu.VMEM((lines + BLOCK * PAD, BLOCK), jnp.float32),
            pltpu.VMEM(warp_rows.shape, jnp.bfloat16),
            pltpu.VMEM(warp_columns.shape, jnp.bfloat16),
            pltpu.SemaphoreType.DMA((3,)),
        ],
        compiler_params=PARAMS,
        name=f"match_warp_{half}",
    )(ident, weight, coef, above, image, below, rows, columns, warp_rows, warp_columns)


def table_columns(half, per_tile, across):
    items = per_tile // HALVES
    here = across // HALVES
    return [item // here * across + half * here + item % here for item in range(items)]


def add_rows(slot_ref, table, arrived_ref, wide_ref, sums):
    sources = slot_ref.shape[0]
    items = len(table)
    slots_each = wide_ref.shape[0] // sources

    def at(source, count):
        return pl.ds(pl.multiple_of(source * count, count), count)

    @pl.loop(0, sources)
    def _(source):
        wide_ref[at(source, slots_each), :] = arrived_ref[at(source, slots_each), :].astype(
            jnp.float32
        )
        for sum_ref in sums:
            count = sum_ref.shape[0] // sources
            sum_ref[at(source, count), :] = jnp.zeros((count, BLOCK), jnp.float32)

    @pl.loop(0, sources)
    def _(source):
        for first in range(0, items, len(sums)):
            slots = [slot_ref[source, table[first + lane]] for lane in range(len(sums))]
            values = [
                sum_ref[pl.ds(slot, 1), :] + wide_ref[pl.ds(source * items + first + lane, 1), :]
                for lane, (slot, sum_ref) in enumerate(zip(slots, sums))
            ]
            for slot, sum_ref, value in zip(slots, sums, values):
                sum_ref[pl.ds(slot, 1), :] = value


def take_rows(slot_ref, table, value_ref, wide_ref, out_ref):
    sources = slot_ref.shape[0]
    items = len(table)

    @pl.loop(0, sources)
    def _(source):
        for item in range(items):
            slot = slot_ref[source, table[item]]
            wide_ref[pl.ds(source * items + item, 1), :] = value_ref[pl.ds(slot, 1), :]

    @pl.loop(0, sources, unroll=2)
    def _(source):
        at = pl.ds(pl.multiple_of(source * items, items), items)
        out_ref[at, :] = wide_ref[at, :].astype(jnp.bfloat16)


def early_kernel(slot_ref, arrived_ref, sum_ref, wide_ref, *sums, table):
    add_rows(slot_ref, table, arrived_ref, wide_ref, sums)

    @pl.loop(0, sum_ref.shape[0] // BLOCK)
    def _(group):
        at = pl.ds(pl.multiple_of(group * BLOCK, BLOCK), BLOCK)
        value = sums[0][at, :]
        for other in sums[1:]:
            value = value + other[at, :]
        sum_ref[at, :] = value


def early_sums(slots, arrived, across, slot_total):
    table = table_columns(0, slots.shape[1], across)
    return pl.pallas_call(
        functools.partial(early_kernel, table=table),
        out_shape=jax.ShapeDtypeStruct((slot_total, BLOCK), jnp.float32),
        in_specs=[SMEM, VMEM],
        out_specs=VMEM,
        scratch_shapes=[pltpu.VMEM(arrived.shape, jnp.float32)]
        + [pltpu.VMEM((slot_total, BLOCK), jnp.float32)] * LANES,
        compiler_params=PARAMS,
        name="early_sums",
    )(slots, arrived)


def late_kernel(
    slot_ref, arrived_ref, early_ref, template_ref, coadd_ref, wide_ref, *sums, tables
):
    add_rows(slot_ref, tables[1], arrived_ref, wide_ref, sums)

    @pl.loop(0, early_ref.shape[0] // BLOCK)
    def _(group):
        at = pl.ds(pl.multiple_of(group * BLOCK, BLOCK), BLOCK)
        value = early_ref[at, :]
        for other in sums:
            value = value + other[at, :]
        sums[0][at, :] = value
        coadd_ref[at, :] = value.astype(jnp.bfloat16)

    take_rows(slot_ref, tables[0], sums[0], wide_ref, template_ref)


def late_sums(slots, arrived, early, across):
    tables = [table_columns(half, slots.shape[1], across) for half in range(HALVES)]
    return pl.pallas_call(
        functools.partial(late_kernel, tables=tables),
        out_shape=(
            jax.ShapeDtypeStruct(arrived.shape, jnp.bfloat16),
            jax.ShapeDtypeStruct(early.shape, jnp.bfloat16),
        ),
        in_specs=[SMEM, VMEM, VMEM],
        out_specs=(VMEM, VMEM),
        scratch_shapes=[pltpu.VMEM(arrived.shape, jnp.float32)]
        + [pltpu.VMEM(early.shape, jnp.float32)] * LANES,
        compiler_params=PARAMS,
        name="late_sums",
    )(slots, arrived, early)


def more_kernel(slot_ref, coadd_ref, template_ref, value_ref, wide_ref, *, table):
    @pl.loop(0, value_ref.shape[0] // BLOCK)
    def _(group):
        at = pl.ds(pl.multiple_of(group * BLOCK, BLOCK), BLOCK)
        value_ref[at, :] = coadd_ref[at, :].astype(jnp.float32)

    take_rows(slot_ref, table, value_ref, wide_ref, template_ref)


def more_rows(slots, coadd, across):
    table = table_columns(1, slots.shape[1], across)
    shape = (slots.shape[0] * len(table), BLOCK)
    return pl.pallas_call(
        functools.partial(more_kernel, table=table),
        out_shape=jax.ShapeDtypeStruct(shape, jnp.bfloat16),
        in_specs=[SMEM, VMEM],
        out_specs=VMEM,
        scratch_shapes=[pltpu.VMEM(coadd.shape, jnp.float32), pltpu.VMEM(shape, jnp.float32)],
        compiler_params=PARAMS,
        name="more_rows",
    )(slots, coadd)


def unwarp_kernel(
    ident_ref,
    scale_ref,
    returned_ref,
    bank_rows_ref,
    bank_columns_ref,
    out_ref,
    top_ref,
    bottom_ref,
    wide_ref,
    warp_rows_ref,
    warp_columns_ref,
    sems,
    *,
    half,
):
    tile_rows, part_width = out_ref.shape
    across = part_width // BLOCK
    parts = tile_rows // BLOCK
    items = parts * across
    pitch = items + PAD
    loads = [
        pltpu.make_async_copy(bank_rows_ref, warp_rows_ref, sems.at[0]),
        pltpu.make_async_copy(bank_columns_ref, warp_columns_ref, sems.at[1]),
    ]
    for load in loads:
        load.start()

    @pl.loop(0, BLOCK, unroll=4)
    def _(row):
        to = pl.ds(pl.multiple_of(row * pitch, PAD), items)
        at = pl.ds(pl.multiple_of(row * items, items), items)
        wide_ref[to, :] = returned_ref[at, :].astype(jnp.float32)

    for load in loads:
        load.wait()

    @pl.loop(0, across // 4)
    def _(quad):
        todo = []
        for part in range(parts):
            for inner in range(4):
                column = quad * 4 + inner
                item = part * across + column
                block = part * (across * HALVES) + half * across + column
                ident = ident_ref[0, block]
                numerator = wide_ref[pl.ds(item, BLOCK, stride=pitch), :].astype(jnp.bfloat16)
                todo.append((part, column, block, ident, numerator))
        todo = [
            (
                part,
                column,
                ident,
                scale_ref[0, block]
                * lax.dot_general(
                    warp_rows_ref[ident],
                    numerator,
                    (((0,), (0,)), ((), ())),
                    preferred_element_type=jnp.float32,
                ),
            )
            for part, column, block, ident, numerator in todo
        ]
        for part, column, ident, first in todo:
            image = jnp.dot(
                first.astype(jnp.bfloat16),
                warp_columns_ref[ident],
                preferred_element_type=jnp.float32,
            ).astype(jnp.bfloat16)
            to = pl.ds(pl.multiple_of(column * BLOCK, BLOCK), BLOCK)
            out_ref[part * BLOCK : (part + 1) * BLOCK, to] = image
            if part == 0:
                top_ref[:, to] = image[:RIM]
            if part == parts - 1:
                bottom_ref[:, to] = image[BLOCK - RIM :]


def unwarp(half, ident, scale, returned, warp_rows, warp_columns, tile_rows):
    lines = returned.shape[0]
    part_width = lines * BLOCK // tile_rows
    rim = jax.ShapeDtypeStruct((RIM, part_width), jnp.bfloat16)
    return pl.pallas_call(
        functools.partial(unwarp_kernel, half=half),
        out_shape=(jax.ShapeDtypeStruct((tile_rows, part_width), jnp.bfloat16), rim, rim),
        in_specs=[SMEM, SMEM, VMEM, ANY, ANY],
        out_specs=(VMEM, VMEM, VMEM),
        scratch_shapes=[
            pltpu.VMEM((lines + BLOCK * PAD, BLOCK), jnp.float32),
            pltpu.VMEM(warp_rows.shape, jnp.bfloat16),
            pltpu.VMEM(warp_columns.shape, jnp.bfloat16),
            pltpu.SemaphoreType.DMA((2,)),
        ],
        compiler_params=PARAMS,
        name=f"unwarp_{half}",
    )(ident, scale, returned, warp_rows, warp_columns)


def inner_strips(image_ref):
    tile_rows = image_ref.shape[0]
    rest = tile_rows - 2 * RIM - BLOCK
    return [
        (0, BLOCK, [(image_ref, 0, WINDOW, 0)]),
        (BLOCK, rest, [(image_ref, BLOCK, tile_rows - BLOCK, 0)]),
    ]


def inner_parts(first, coef_ref, exposure_hbm, rows_ref, columns_ref, out_ref, refs):
    exposure_ref, pass_ref, stage_ref, sems = refs
    inner, width = stage_ref.shape
    fetch = pltpu.make_async_copy(
        exposure_hbm.at[pl.ds(RIM, inner), pl.ds(first, width)], exposure_ref, sems.at[0]
    )

    def store(index):
        at = pl.multiple_of(index * WIDE, WIDE)
        return pltpu.make_async_copy(
            stage_ref.at[:, pl.ds(at, WIDE)],
            out_ref.at[pl.ds(RIM, inner), pl.ds(first + at, WIDE)],
            sems.at[1 + index],
        )

    def step(image_ref):
        return functools.partial(
            row_step,
            strips=inner_strips(image_ref),
            coef_ref=coef_ref,
            rows_ref=rows_ref,
            pass_ref=pass_ref,
        )

    def subtract_step(index):
        for half, summed in enumerate(column_step(index, inner, columns_ref, pass_ref)):
            at = pl.ds(pl.multiple_of(index * WIDE + half * CHUNK, CHUNK), CHUNK)
            stage_ref[:, at] = exposure_ref[:, at].astype(jnp.float32) - summed
        store(index).start()

    return fetch, step, subtract_step, store


def inner_left_kernel(
    coef_ref, left_ref, exposure_hbm, rows_ref, columns_ref, out_ref, *refs
):
    fetch, step, subtract_step, store = inner_parts(
        0, coef_ref, exposure_hbm, rows_ref, columns_ref, out_ref, refs
    )
    pass_ref = refs[1]
    fetch.start()
    clear(pass_ref, 0)
    step = step(left_ref)

    @pl.loop(0, LEFT)
    def _(index):
        step(WIDE, index * WIDE, BLOCK + index * WIDE)

    step(BLOCK, LEFT * WIDE, BLOCK + LEFT * WIDE)
    fetch.wait()

    @pl.loop(0, LEFT)
    def _(index):
        subtract_step(index)

    @pl.loop(0, LEFT)
    def _(index):
        store(index).wait()


def inner_right_kernel(
    coef_ref, left_ref, right_ref, exposure_hbm, rows_ref, columns_ref, partial_ref, out_ref, *refs
):
    del partial_ref
    first = LEFT * WIDE
    fetch, step, subtract_step, store = inner_parts(
        first, coef_ref, exposure_hbm, rows_ref, columns_ref, out_ref, refs
    )
    pass_ref = refs[1]
    half_width = left_ref.shape[1]
    ahead = half_width - first
    wides = right_ref.shape[1] // WIDE
    total = wides + ahead // WIDE
    fetch.start()
    clear(pass_ref, pass_ref.shape[2] - BLOCK)
    step(left_ref)(BLOCK + ahead, first - BLOCK, 0)
    step = step(right_ref)
    base = BLOCK + ahead
    step(WIDE, 0, base)
    fetch.wait()

    @pl.loop(0, wides - 1)
    def _(index):
        subtract_step(index)
        step(WIDE, (index + 1) * WIDE, base + (index + 1) * WIDE)

    @pl.loop(wides - 1, total)
    def _(index):
        subtract_step(index)

    @pl.loop(0, total)
    def _(index):
        store(index).wait()


def inner_call(kernel, name, width, images, coef, exposure, rows, columns, partial):
    tile_rows = exposure.shape[0]
    bases = rows.shape[0] // BLOCK
    inner = tile_rows - 2 * RIM
    more = [] if partial is None else [partial]
    operands = [coef, *images, exposure, rows, columns, *more]
    return pl.pallas_call(
        kernel,
        out_shape=jax.ShapeDtypeStruct(exposure.shape, jnp.float32),
        in_specs=[SMEM] + [VMEM] * len(images) + [ANY, VMEM, VMEM] + [ANY] * len(more),
        out_specs=ANY,
        scratch_shapes=[
            pltpu.VMEM((inner, width), jnp.bfloat16),
            pltpu.VMEM((bases, inner, width + 2 * BLOCK), jnp.bfloat16),
            pltpu.VMEM((inner, width), jnp.float32),
            pltpu.SemaphoreType.DMA((1 + width // WIDE,)),
        ],
        input_output_aliases={len(operands) - 1: 0} if more else {},
        compiler_params=PARAMS,
        name=name,
    )(*operands)


def outer_kernel(
    coef_ref,
    above_left_ref,
    above_right_ref,
    top_left_ref,
    top_right_ref,
    bottom_left_ref,
    bottom_right_ref,
    below_left_ref,
    below_right_ref,
    exposure_top_ref,
    exposure_bottom_ref,
    rows_ref,
    columns_ref,
    partial_ref,
    out_ref,
    pass_ref,
    stage_ref,
    sems,
):
    del partial_ref
    tile_rows, width = out_ref.shape
    clear(pass_ref, 0)
    clear(pass_ref, BLOCK + width)
    done = 0
    for above_ref, top_ref, bottom_ref, below_ref in (
        (above_left_ref, top_left_ref, bottom_left_ref, below_left_ref),
        (above_right_ref, top_right_ref, bottom_right_ref, below_right_ref),
    ):
        strips = [
            (0, RIM, [(above_ref, 0, RIM, 0), (top_ref, 0, 2 * RIM, 0)]),
            (RIM, RIM, [(bottom_ref, 0, 2 * RIM, 0), (below_ref, 0, RIM, 0)]),
        ]
        for index in range(top_ref.shape[1] // WIDE):
            row_step(
                WIDE, index * WIDE, BLOCK + done * WIDE, strips, coef_ref, rows_ref, pass_ref
            )
            done += 1
    for index in range(width // WIDE):
        for half, summed in enumerate(column_step(index, 2 * RIM, columns_ref, pass_ref)):
            at = pl.ds(index * WIDE + half * CHUNK, CHUNK)
            stage_ref[:RIM, at] = exposure_top_ref[:, at].astype(jnp.float32) - summed[:RIM]
            stage_ref[RIM:, at] = exposure_bottom_ref[:, at].astype(jnp.float32) - summed[RIM:]
    stores = [
        pltpu.make_async_copy(stage_ref.at[:RIM], out_ref.at[:RIM], sems.at[0]),
        pltpu.make_async_copy(
            stage_ref.at[RIM:], out_ref.at[pl.ds(tile_rows - RIM, RIM)], sems.at[1]
        ),
    ]
    for store in stores:
        store.start()
    for store in stores:
        store.wait()


def subtract_outer(coef, above, images, below, exposure, rows, columns, partial):
    tile_rows, width = exposure.shape
    bases = rows.shape[0] // BLOCK
    part_width = images[0].shape[1]
    rim = pl.BlockSpec((RIM, width), lambda _: (0, 0))
    last_rim = pl.BlockSpec((RIM, width), lambda _: (tile_rows // RIM - 1, 0))
    pair = pl.BlockSpec((2 * RIM, part_width), lambda _: (0, 0))
    last_pair = pl.BlockSpec((2 * RIM, part_width), lambda _: (tile_rows // (2 * RIM) - 1, 0))
    specs = [SMEM, VMEM, VMEM, pair, pair, last_pair, last_pair, VMEM, VMEM, rim, last_rim]
    return pl.pallas_call(
        outer_kernel,
        out_shape=jax.ShapeDtypeStruct((tile_rows, width), jnp.float32),
        grid=(1,),
        in_specs=specs + [VMEM, VMEM, ANY],
        out_specs=ANY,
        scratch_shapes=[
            pltpu.VMEM((bases, 2 * RIM, width + 2 * BLOCK), jnp.bfloat16),
            pltpu.VMEM((2 * RIM, width), jnp.float32),
            pltpu.SemaphoreType.DMA((2,)),
        ],
        input_output_aliases={13: 0},
        compiler_params=PARAMS,
        name="subtract_outer",
    )(coef, *above, *images, *images, *below, exposure, exposure, rows, columns, partial)


def patch_kernel(scale_ref, rows_ref, out_ref, wide_ref, stage_ref, sems):
    slots = SLOT_ROWS * SLOT_COLS
    pitch = slots + PAD

    @pl.loop(0, BLOCK, unroll=2)
    def _(row):
        to = pl.ds(pl.multiple_of(row * pitch, PAD), slots)
        at = pl.ds(pl.multiple_of(row * slots, slots), slots)
        wide_ref[to, :] = rows_ref[at, :].astype(jnp.float32)

    def store(down):
        at = pl.ds(pl.multiple_of(down * BLOCK, BLOCK), BLOCK)
        return pltpu.make_async_copy(stage_ref.at[at], out_ref.at[at], sems.at[down])

    @pl.loop(0, SLOT_ROWS)
    def _(down):
        to = pl.ds(pl.multiple_of(down * BLOCK, BLOCK), BLOCK)
        for across in range(SLOT_COLS):
            slot = down * SLOT_COLS + across
            stage_ref[to, across * BLOCK : (across + 1) * BLOCK] = (
                scale_ref[0, slot] * wide_ref[pl.ds(slot, BLOCK, stride=pitch), :]
            )
        store(down).start()

    @pl.loop(0, SLOT_ROWS)
    def _(down):
        store(down).wait()


def patch(scale, rows):
    shape = (SLOT_ROWS * BLOCK, SLOT_COLS * BLOCK)
    return pl.pallas_call(
        patch_kernel,
        out_shape=jax.ShapeDtypeStruct(shape, jnp.float32),
        in_specs=[SMEM, VMEM],
        out_specs=ANY,
        scratch_shapes=[
            pltpu.VMEM((rows.shape[0] + BLOCK * PAD, BLOCK), jnp.float32),
            pltpu.VMEM(shape, jnp.float32),
            pltpu.SemaphoreType.DMA((SLOT_ROWS,)),
        ],
        compiler_params=PARAMS,
        name="patch",
    )(scale, rows)


def exchange(rows, devices):
    shaped = rows.reshape(devices, -1, BLOCK)
    moved = lax.all_to_all(shaped, ("exp", "tile"), split_axis=0, concat_axis=0, tiled=True)
    return moved.reshape(rows.shape)


def shards(
    exposure,
    row_taps,
    column_taps,
    basis_coef,
    warp_rows,
    warp_columns,
    warp_id,
    route_device,
    route_slot,
    weight,
):
    devices = lax.axis_size("exp") * lax.axis_size("tile")
    image = exposure[0]
    tile_rows, width = image.shape
    per_tile = tile_rows * width // (BLOCK * BLOCK)
    slot_count = SLOT_ROWS * SLOT_COLS
    myself = lax.axis_index("exp") * lax.axis_size("tile") + lax.axis_index("tile")

    def mine(table):
        return lax.dynamic_slice_in_dim(table.reshape(devices, -1), myself, 1, 0)

    across = width // BLOCK
    slots = (route_device * slot_count + route_slot).reshape(devices, per_tile)
    above, below = swap_rims(image[:RIM], image[tile_rows - RIM :])
    rows, columns = band_matrices(row_taps, column_taps)
    my_ident = mine(warp_id)
    my_weight = mine(weight)
    arrived = []
    for half in range(HALVES):
        weighted = forward(
            half, my_ident, my_weight, basis_coef, above, image, below, rows, columns,
            warp_rows, warp_columns,
        )
        arrived.append(exchange(weighted, devices))

    owner = route_device.reshape(-1)
    place = route_slot.reshape(-1)
    block_weight = jnp.repeat(weight.reshape(-1), per_tile)
    by_owner = jnp.where(
        owner[None, :] == jnp.arange(devices, dtype=jnp.int32)[:, None], block_weight[None, :], 0.0
    )
    by_place = (place[:, None] == jnp.arange(slot_count, dtype=jnp.int32)[None, :]).astype(
        jnp.float32
    )
    total = jnp.dot(by_owner, by_place, precision=lax.Precision.HIGHEST)
    scale = 1.0 / jnp.maximum(total, 1.0)
    owned_scale = mine(scale)
    block_scale = scale.reshape(-1)[mine(slots)]

    early = early_sums(slots, arrived[0], across, devices * slot_count)
    first_rows, coadd_rows = late_sums(slots, arrived[1], early, across)
    second_rows = more_rows(slots, coadd_rows, across)
    returned = [exchange(first_rows, devices), exchange(second_rows, devices)]
    owned = exchange(coadd_rows, devices)

    images, above, below = [], [], []
    for half in range(HALVES):
        template, top, bottom = unwarp(
            half, my_ident, block_scale, returned[half], warp_rows, warp_columns, tile_rows
        )
        upper, lower = swap_rims(top, bottom)
        images.append(template)
        above.append(upper)
        below.append(lower)
    shared = (basis_coef, image, rows, columns)
    difference = inner_call(
        inner_left_kernel, "inner_left", LEFT * WIDE, images[:1], *shared, None
    )
    difference = inner_call(
        inner_right_kernel, "inner_right", width - LEFT * WIDE, images, *shared, difference
    )
    difference = subtract_outer(
        basis_coef, above, images, below, image, rows, columns, difference
    )
    return patch(owned_scale, owned), difference[None]


def solution(mesh):
    placed = (P("exp", "tile", None), P(), P(), P("exp", None), P(), P(), P(), P(), P(), P())
    return jax.shard_map(
        shards,
        mesh=mesh,
        in_specs=placed,
        out_specs=(P("exp", "tile"), P("exp", "tile", None)),
        check_vma=False,
    )
```

```python
import functools

import jax
import jax.numpy as jnp
from jax import lax
from jax.experimental import pallas as pl
from jax.experimental.pallas import tpu as pltpu
from jax.sharding import PartitionSpec as P

BLOCK = 128
HALF = 10
RIM = 16
CHUNK = 256
WIDE = 1024
SPAN = CHUNK + BLOCK
WINDOW = BLOCK + 2 * RIM
SLOT_ROWS = 8
SLOT_COLS = 8
LANES = 8
PAD = 8
VMEM = pl.BlockSpec(memory_space=pltpu.VMEM)
SMEM = pl.BlockSpec(memory_space=pltpu.SMEM)
ANY = pl.BlockSpec(memory_space=pl.ANY)


def grant(mebibytes):
    return pltpu.CompilerParams(vmem_limit_bytes=mebibytes * 1024 * 1024)


def bands_kernel(row_taps_ref, column_taps_ref, rows_ref, columns_ref):
    bases, taps = row_taps_ref.shape
    lead = RIM - HALF

    def banded(taps_ref, offsets):
        values = taps_ref[...].astype(jnp.float32)
        bands = [jnp.zeros(offsets.shape, jnp.float32) for _ in range(bases)]
        for tap in range(taps):
            hit = offsets == tap
            for base in range(bases):
                value = jnp.broadcast_to(values[base : base + 1, tap : tap + 1], offsets.shape)
                bands[base] = jnp.where(hit, value, bands[base])
        return [band.astype(jnp.bfloat16) for band in bands]

    shape = (BLOCK, WINDOW)
    across = lax.broadcasted_iota(jnp.int32, shape, 1) - lax.broadcasted_iota(jnp.int32, shape, 0)
    for base, band in enumerate(banded(row_taps_ref, across - lead)):
        rows_ref[base * BLOCK : (base + 1) * BLOCK, :] = band
    shape = (WINDOW, BLOCK)
    down = lax.broadcasted_iota(jnp.int32, shape, 0) - lax.broadcasted_iota(jnp.int32, shape, 1)
    columns_ref[...] = jnp.zeros_like(columns_ref)
    for base, band in enumerate(banded(column_taps_ref, down - lead)):
        top = base * CHUNK
        columns_ref[top : top + WINDOW - RIM, :BLOCK] = band[RIM:]
        columns_ref[top + BLOCK - RIM : top + CHUNK, BLOCK:] = band[: WINDOW - RIM]
        top = bases * CHUNK + base * BLOCK
        columns_ref[top : top + RIM, BLOCK:] = band[WINDOW - RIM :]
        columns_ref[top + BLOCK - RIM : top + BLOCK, :BLOCK] = band[:RIM]


def band_matrices(row_taps, column_taps):
    bases = row_taps.shape[0]
    return pl.pallas_call(
        bands_kernel,
        out_shape=(
            jax.ShapeDtypeStruct((bases * BLOCK, WINDOW), jnp.bfloat16),
            jax.ShapeDtypeStruct((bases * SPAN, CHUNK), jnp.bfloat16),
        ),
        in_specs=[VMEM, VMEM],
        out_specs=(VMEM, VMEM),
        compiler_params=grant(58),
        name="bands",
    )(row_taps, column_taps)


def swap_rims(top, bottom):
    count = lax.axis_size("tile")
    forward = [(i, i + 1) for i in range(count - 1)]
    backward = [(target, source) for source, target in forward]
    return lax.ppermute(bottom, "tile", forward), lax.ppermute(top, "tile", backward)


def clear(pass_ref, start):
    bases, height, _ = pass_ref.shape
    pass_ref[:, :, start : start + BLOCK] = jnp.zeros((bases, height, BLOCK), pass_ref.dtype)


def row_step(lanes, start, to, strips, coef_ref, rows_ref, pass_ref):
    bases = pass_ref.shape[0]
    for first_row, count, pieces in strips:
        window = [
            ref[first : first + size, pl.ds(pl.multiple_of(start + shift, BLOCK), lanes)]
            for ref, first, size, shift in pieces
        ]
        window = window[0] if len(window) == 1 else jnp.concatenate(window, axis=0)
        depth = window.shape[0]
        if count == BLOCK and depth == WINDOW:
            band = rows_ref[...]
        else:
            band = jnp.concatenate(
                [rows_ref[base * BLOCK : base * BLOCK + count, :depth] for base in range(bases)],
                axis=0,
            )
        summed = jnp.dot(band, window, preferred_element_type=jnp.float32)
        for base in range(bases):
            pass_ref[
                base, first_row : first_row + count, pl.ds(pl.multiple_of(to, BLOCK), lanes)
            ] = (coef_ref[0, base] * summed[base * count : (base + 1) * count]).astype(jnp.bfloat16)


def column_step(index, count, columns_ref, pass_ref):
    bases = pass_ref.shape[0]
    right = lax.broadcasted_iota(jnp.int32, (count, BLOCK), 1) < BLOCK // 2
    summed = []
    for part in range(WIDE // CHUNK):
        at = index * WIDE + part * CHUNK

        def columns(shift, size):
            return pl.ds(pl.multiple_of(at + shift, BLOCK), size)

        middle = [pass_ref[base, :count, columns(BLOCK, CHUNK)] for base in range(bases)]
        sides = [
            jnp.where(
                right,
                pass_ref[base, :count, columns(BLOCK + CHUNK, BLOCK)],
                pass_ref[base, :count, columns(0, BLOCK)],
            )
            for base in range(bases)
        ]
        summed.append(
            jnp.dot(
                jnp.concatenate(middle + sides, axis=1),
                columns_ref[...],
                preferred_element_type=jnp.float32,
            )
        )
    return summed


def my_device():
    return lax.axis_index("exp") * lax.axis_size("tile") + lax.axis_index("tile")


def wide_copy(source, target, sems, first_row, rows):
    def copy(index):
        at = pl.ds(pl.multiple_of(index * WIDE, WIDE), WIDE)
        return pltpu.make_async_copy(
            source.at[pl.ds(first_row, rows), at], target.at[:, at], sems.at[index]
        )

    return copy


def passes(fetch, step, consume, pass_ref, width):
    wides = width // WIDE

    def wide_step(index):
        fetch(index).wait()
        step(WIDE, index * WIDE, BLOCK + index * WIDE)

    clear(pass_ref, 0)
    clear(pass_ref, BLOCK + width)
    wide_step(0)
    wide_step(1)

    @pl.loop(0, wides - 2)
    def _(index):
        consume(index)
        wide_step(index + 2)

    @pl.loop(wides - 2, wides)
    def _(index):
        consume(index)


def forward_kernel(
    ident_ref,
    weight_ref,
    coef_ref,
    above_ref,
    image_hbm,
    below_ref,
    rows_ref,
    columns_ref,
    bank_rows_ref,
    bank_columns_ref,
    out_ref,
    image_ref,
    pass_ref,
    matched_ref,
    turned_ref,
    warp_rows_ref,
    warp_columns_ref,
    fetch_sems,
    load_sems,
):
    tile_rows, width = image_ref.shape
    parts = tile_rows // BLOCK
    across = width // BLOCK
    items = parts * across
    pitch = items + PAD
    myself = my_device()
    weight = weight_ref[lax.axis_index("exp"), lax.axis_index("tile")]
    fetch = wide_copy(image_hbm, image_ref, fetch_sems, 0, tile_rows)
    loads = [
        pltpu.make_async_copy(bank_rows_ref, warp_rows_ref, load_sems.at[0]),
        pltpu.make_async_copy(bank_columns_ref, warp_columns_ref, load_sems.at[1]),
    ]
    for index in range(width // WIDE):
        fetch(index).start()
    for load in loads:
        load.start()

    strips = [
        (0, BLOCK, [(above_ref, 0, RIM, 0), (image_ref, 0, BLOCK + RIM, 0)]),
        (BLOCK, BLOCK, [(image_ref, BLOCK - RIM, BLOCK + RIM, 0), (below_ref, 0, RIM, 0)]),
    ]
    step = functools.partial(
        row_step, strips=strips, coef_ref=coef_ref, rows_ref=rows_ref, pass_ref=pass_ref
    )

    def match_step(index):
        for inner, summed in enumerate(column_step(index, tile_rows, columns_ref, pass_ref)):
            matched_ref[:, pl.ds(pl.multiple_of(index * WIDE + inner * CHUNK, CHUNK), CHUNK)] = (
                summed.astype(jnp.bfloat16)
            )

    passes(fetch, step, match_step, pass_ref, width)
    for load in loads:
        load.wait()

    @pl.loop(0, across // 4)
    def _(quad):
        todo = []
        for part in range(parts):
            for inner in range(4):
                column = quad * 4 + inner
                ident = ident_ref[myself, part * across + column]
                piece = matched_ref[
                    part * BLOCK : (part + 1) * BLOCK,
                    pl.ds(pl.multiple_of(column * BLOCK, BLOCK), BLOCK),
                ]
                todo.append((part * across + column, ident, piece))
        todo = [
            (
                item,
                ident,
                jnp.dot(warp_rows_ref[ident], piece, preferred_element_type=jnp.float32).astype(
                    jnp.bfloat16
                ),
            )
            for item, ident, piece in todo
        ]
        todo = [
            (
                item,
                lax.dot_general(
                    first,
                    warp_columns_ref[ident],
                    (((1,), (1,)), ((), ())),
                    preferred_element_type=jnp.float32,
                ),
            )
            for item, ident, first in todo
        ]
        for item, second in todo:
            turned_ref[pl.ds(item, BLOCK, stride=pitch), :] = weight * second

    @pl.loop(0, BLOCK, unroll=4)
    def _(row):
        to = pl.ds(pl.multiple_of(row * items, items), items)
        at = pl.ds(pl.multiple_of(row * pitch, PAD), items)
        out_ref[to, :] = turned_ref[at, :].astype(jnp.bfloat16)


def forward(ident, weight, coef, above, image, below, rows, columns, warp_rows, warp_columns):
    tile_rows, width = image.shape
    bases = rows.shape[0] // BLOCK
    lines = tile_rows * width // BLOCK
    return pl.pallas_call(
        forward_kernel,
        out_shape=jax.ShapeDtypeStruct((lines, BLOCK), jnp.bfloat16),
        in_specs=[SMEM, SMEM, SMEM, VMEM, ANY, VMEM, VMEM, VMEM, ANY, ANY],
        out_specs=VMEM,
        scratch_shapes=[
            pltpu.VMEM((tile_rows, width), jnp.bfloat16),
            pltpu.VMEM((bases, tile_rows, width + 2 * BLOCK), jnp.bfloat16),
            pltpu.VMEM((tile_rows, width), jnp.bfloat16),
            pltpu.VMEM((lines + BLOCK * PAD, BLOCK), jnp.float32),
            pltpu.VMEM(warp_rows.shape, jnp.bfloat16),
            pltpu.VMEM(warp_columns.shape, jnp.bfloat16),
            pltpu.SemaphoreType.DMA((width // WIDE,)),
            pltpu.SemaphoreType.DMA((2,)),
        ],
        compiler_params=grant(58),
        name="match_warp",
    )(ident, weight, coef, above, image, below, rows, columns, warp_rows, warp_columns)


def slots_kernel(slot_hbm, arrived_ref, scale_ref, template_ref, coadd_ref, wide_ref, *refs):
    del scale_ref
    items, _, sources = slot_hbm.shape
    sums, tables, sems = refs[:LANES], refs[LANES : LANES + items], refs[LANES + items]
    loads = [pltpu.make_async_copy(slot_hbm.at[k], tables[k], sems.at[k]) for k in range(items)]
    for load in loads:
        load.start()

    def at(source):
        return pl.ds(pl.multiple_of(source * items, items), items)

    @pl.loop(0, sources)
    def _(source):
        wide_ref[at(source), :] = arrived_ref[at(source), :].astype(jnp.float32)
        for sum_ref in sums:
            sum_ref[at(source), :] = jnp.zeros((items, BLOCK), jnp.float32)

    for load in loads:
        load.wait()

    @pl.loop(0, sources)
    def _(source):
        for first in range(0, items, LANES):
            slots = [tables[first + lane][0, source] for lane in range(LANES)]
            values = [
                sum_ref[pl.ds(slot, 1), :] + wide_ref[pl.ds(source * items + first + lane, 1), :]
                for lane, (slot, sum_ref) in enumerate(zip(slots, sums))
            ]
            for slot, sum_ref, value in zip(slots, sums, values):
                sum_ref[pl.ds(slot, 1), :] = value

    @pl.loop(0, sources)
    def _(source):
        value = sums[0][at(source), :]
        for sum_ref in sums[1:]:
            value = value + sum_ref[at(source), :]
        sums[0][at(source), :] = value
        coadd_ref[at(source), :] = value.astype(jnp.bfloat16)

    @pl.loop(0, sources)
    def _(source):
        for item in range(items):
            slot = tables[item][0, source]
            wide_ref[pl.ds(source * items + item, 1), :] = sums[0][pl.ds(slot, 1), :]

    @pl.loop(0, sources)
    def _(source):
        template_ref[at(source), :] = wide_ref[at(source), :].astype(jnp.bfloat16)


def slot_sums(slots, arrived, scale):
    shape = jax.ShapeDtypeStruct(arrived.shape, jnp.bfloat16)
    sources, items = slots.shape
    return pl.pallas_call(
        slots_kernel,
        out_shape=(shape, shape),
        in_specs=[ANY, VMEM, ANY],
        out_specs=(VMEM, VMEM),
        scratch_shapes=[pltpu.VMEM(arrived.shape, jnp.float32)] * (1 + LANES)
        + [pltpu.SMEM((1, sources), jnp.int32)] * items
        + [pltpu.SemaphoreType.DMA((items,))],
        compiler_params=grant(44),
        name="slot_sums",
    )(slots.T.reshape(items, 1, sources), arrived, scale)


def unwarp_kernel(
    ident_ref,
    scale_ref,
    returned_ref,
    bank_rows_ref,
    bank_columns_ref,
    out_ref,
    top_ref,
    bottom_ref,
    wide_ref,
    warp_rows_ref,
    warp_columns_ref,
    sems,
):
    tile_rows, part_width = out_ref.shape
    across = part_width // BLOCK
    parts = tile_rows // BLOCK
    items = parts * across
    pitch = items + PAD
    myself = my_device()
    loads = [
        pltpu.make_async_copy(bank_rows_ref, warp_rows_ref, sems.at[0]),
        pltpu.make_async_copy(bank_columns_ref, warp_columns_ref, sems.at[1]),
    ]
    for load in loads:
        load.start()

    @pl.loop(0, BLOCK, unroll=4)
    def _(row):
        to = pl.ds(pl.multiple_of(row * pitch, PAD), items)
        at = pl.ds(pl.multiple_of(row * items, items), items)
        wide_ref[to, :] = returned_ref[at, :].astype(jnp.float32)

    for load in loads:
        load.wait()

    @pl.loop(0, across // 4)
    def _(quad):
        todo = []
        for part in range(parts):
            for inner in range(4):
                column = quad * 4 + inner
                item = part * across + column
                ident = ident_ref[myself, item]
                numerator = wide_ref[pl.ds(item, BLOCK, stride=pitch), :].astype(jnp.bfloat16)
                todo.append((part, column, item, ident, numerator))
        todo = [
            (
                part,
                column,
                ident,
                scale_ref[0, item]
                * lax.dot_general(
                    warp_rows_ref[ident],
                    numerator,
                    (((0,), (0,)), ((), ())),
                    preferred_element_type=jnp.float32,
                ),
            )
            for part, column, item, ident, numerator in todo
        ]
        for part, column, ident, first in todo:
            image = jnp.dot(
                first.astype(jnp.bfloat16),
                warp_columns_ref[ident],
                preferred_element_type=jnp.float32,
            ).astype(jnp.bfloat16)
            to = pl.ds(pl.multiple_of(column * BLOCK, BLOCK), BLOCK)
            out_ref[part * BLOCK : (part + 1) * BLOCK, to] = image
            if part == 0:
                top_ref[:, to] = image[:RIM]
            if part == parts - 1:
                bottom_ref[:, to] = image[BLOCK - RIM :]


def unwarp(ident, scale, returned, warp_rows, warp_columns, tile_rows):
    lines = returned.shape[0]
    part_width = lines * BLOCK // tile_rows
    rim = jax.ShapeDtypeStruct((RIM, part_width), jnp.bfloat16)
    return pl.pallas_call(
        unwarp_kernel,
        out_shape=(jax.ShapeDtypeStruct((tile_rows, part_width), jnp.bfloat16), rim, rim),
        in_specs=[SMEM, SMEM, VMEM, ANY, ANY],
        out_specs=(VMEM, VMEM, VMEM),
        scratch_shapes=[
            pltpu.VMEM((lines + BLOCK * PAD, BLOCK), jnp.float32),
            pltpu.VMEM(warp_rows.shape, jnp.bfloat16),
            pltpu.VMEM(warp_columns.shape, jnp.bfloat16),
            pltpu.SemaphoreType.DMA((2,)),
        ],
        compiler_params=grant(58),
        name="unwarp",
    )(ident, scale, returned, warp_rows, warp_columns)


def inner_kernel(
    coef_ref,
    image_hbm,
    exposure_hbm,
    rows_ref,
    columns_ref,
    out_ref,
    image_ref,
    exposure_ref,
    pass_ref,
    stage_ref,
    fetch_sems,
    load_sem,
    sems,
):
    tile_rows, width = image_ref.shape
    inner = tile_rows - 2 * RIM
    fetch = wide_copy(image_hbm, image_ref, fetch_sems, 0, tile_rows)
    load = pltpu.make_async_copy(exposure_hbm.at[pl.ds(RIM, inner)], exposure_ref, load_sem)
    for index in range(width // WIDE):
        fetch(index).start()
    load.start()
    strips = [
        (0, BLOCK, [(image_ref, 0, WINDOW, 0)]),
        (BLOCK, inner - BLOCK, [(image_ref, BLOCK, tile_rows - BLOCK, 0)]),
    ]
    step = functools.partial(
        row_step, strips=strips, coef_ref=coef_ref, rows_ref=rows_ref, pass_ref=pass_ref
    )

    def store(index):
        at = pl.ds(pl.multiple_of(index * WIDE, WIDE), WIDE)
        return pltpu.make_async_copy(
            stage_ref.at[:, at], out_ref.at[pl.ds(RIM, inner), at], sems.at[index]
        )

    def subtract_step(index):
        for part, summed in enumerate(column_step(index, inner, columns_ref, pass_ref)):
            at = pl.ds(pl.multiple_of(index * WIDE + part * CHUNK, CHUNK), CHUNK)
            stage_ref[:, at] = exposure_ref[:, at].astype(jnp.float32) - summed
        store(index).start()

    load.wait()
    passes(fetch, step, subtract_step, pass_ref, width)

    @pl.loop(0, width // WIDE)
    def _(index):
        store(index).wait()


def subtract_inner(coef, image, exposure, rows, columns):
    tile_rows, width = image.shape
    bases = rows.shape[0] // BLOCK
    inner = tile_rows - 2 * RIM
    return pl.pallas_call(
        inner_kernel,
        out_shape=jax.ShapeDtypeStruct((tile_rows, width), jnp.float32),
        in_specs=[SMEM, ANY, ANY, VMEM, VMEM],
        out_specs=ANY,
        scratch_shapes=[
            pltpu.VMEM((tile_rows, width), jnp.bfloat16),
            pltpu.VMEM((inner, width), jnp.bfloat16),
            pltpu.VMEM((bases, inner, width + 2 * BLOCK), jnp.bfloat16),
            pltpu.VMEM((inner, width), jnp.float32),
            pltpu.SemaphoreType.DMA((width // WIDE,)),
            pltpu.SemaphoreType.DMA,
            pltpu.SemaphoreType.DMA((width // WIDE,)),
        ],
        compiler_params=grant(58),
        name="subtract_inner",
    )(coef, image, exposure, rows, columns)


def outer_kernel(
    coef_ref,
    above_ref,
    top_ref,
    bottom_ref,
    below_ref,
    exposure_top_ref,
    exposure_bottom_ref,
    rows_ref,
    columns_ref,
    partial_ref,
    out_ref,
    pass_ref,
    stage_ref,
    sems,
):
    del partial_ref
    width = top_ref.shape[1]
    tile_rows = out_ref.shape[0]
    wides = width // WIDE
    strips = [
        (0, RIM, [(above_ref, 0, RIM, 0), (top_ref, 0, 2 * RIM, 0)]),
        (RIM, RIM, [(bottom_ref, 0, 2 * RIM, 0), (below_ref, 0, RIM, 0)]),
    ]
    clear(pass_ref, 0)
    clear(pass_ref, BLOCK + width)
    for index in range(wides):
        row_step(
            WIDE, index * WIDE, BLOCK + index * WIDE, strips, coef_ref, rows_ref, pass_ref
        )
    for index in range(wides):
        for half, summed in enumerate(column_step(index, 2 * RIM, columns_ref, pass_ref)):
            at = pl.ds(index * WIDE + half * CHUNK, CHUNK)
            stage_ref[:RIM, at] = exposure_top_ref[:, at].astype(jnp.float32) - summed[:RIM]
            stage_ref[RIM:, at] = exposure_bottom_ref[:, at].astype(jnp.float32) - summed[RIM:]
    stores = [
        pltpu.make_async_copy(stage_ref.at[:RIM], out_ref.at[:RIM], sems.at[0]),
        pltpu.make_async_copy(
            stage_ref.at[RIM:], out_ref.at[pl.ds(tile_rows - RIM, RIM)], sems.at[1]
        ),
    ]
    for store in stores:
        store.start()
    for store in stores:
        store.wait()


def subtract_outer(coef, above, image, below, exposure, rows, columns, partial):
    tile_rows, width = image.shape
    bases = rows.shape[0] // BLOCK
    rim = pl.BlockSpec((RIM, width), lambda _: (0, 0))
    last_rim = pl.BlockSpec((RIM, width), lambda _: (tile_rows // RIM - 1, 0))
    pair = pl.BlockSpec((2 * RIM, width), lambda _: (0, 0))
    last_pair = pl.BlockSpec((2 * RIM, width), lambda _: (tile_rows // (2 * RIM) - 1, 0))
    return pl.pallas_call(
        outer_kernel,
        out_shape=jax.ShapeDtypeStruct((tile_rows, width), jnp.float32),
        grid=(1,),
        in_specs=[SMEM, VMEM, pair, last_pair, VMEM, rim, last_rim, VMEM, VMEM, ANY],
        out_specs=ANY,
        scratch_shapes=[
            pltpu.VMEM((bases, 2 * RIM, width + 2 * BLOCK), jnp.bfloat16),
            pltpu.VMEM((2 * RIM, width), jnp.float32),
            pltpu.SemaphoreType.DMA((2,)),
        ],
        input_output_aliases={9: 0},
        compiler_params=grant(58),
        name="subtract_outer",
    )(coef, above, image, image, below, exposure, exposure, rows, columns, partial)


def patch_kernel(scale_ref, rows_ref, after_ref, out_ref, wide_ref, stage_ref, sems):
    del after_ref
    slots = SLOT_ROWS * SLOT_COLS
    pitch = slots + PAD
    myself = my_device()

    @pl.loop(0, BLOCK, unroll=2)
    def _(row):
        to = pl.ds(pl.multiple_of(row * pitch, PAD), slots)
        at = pl.ds(pl.multiple_of(row * slots, slots), slots)
        wide_ref[to, :] = rows_ref[at, :].astype(jnp.float32)

    def store(down):
        at = pl.ds(pl.multiple_of(down * BLOCK, BLOCK), BLOCK)
        return pltpu.make_async_copy(stage_ref.at[at], out_ref.at[at], sems.at[down])

    @pl.loop(0, SLOT_ROWS)
    def _(down):
        to = pl.ds(pl.multiple_of(down * BLOCK, BLOCK), BLOCK)
        for across in range(SLOT_COLS):
            slot = down * SLOT_COLS + across
            stage_ref[to, across * BLOCK : (across + 1) * BLOCK] = (
                scale_ref[myself, slot] * wide_ref[pl.ds(slot, BLOCK, stride=pitch), :]
            )
        store(down).start()

    @pl.loop(0, SLOT_ROWS)
    def _(down):
        store(down).wait()


def patch(scale, rows, after):
    shape = (SLOT_ROWS * BLOCK, SLOT_COLS * BLOCK)
    return pl.pallas_call(
        patch_kernel,
        out_shape=jax.ShapeDtypeStruct(shape, jnp.float32),
        in_specs=[SMEM, VMEM, ANY],
        out_specs=ANY,
        scratch_shapes=[
            pltpu.VMEM((rows.shape[0] + BLOCK * PAD, BLOCK), jnp.float32),
            pltpu.VMEM(shape, jnp.float32),
            pltpu.SemaphoreType.DMA((SLOT_ROWS,)),
        ],
        compiler_params=grant(14),
        name="patch",
    )(scale, rows, after)


def exchange(rows, devices):
    shaped = rows.reshape(devices, -1, BLOCK)
    moved = lax.all_to_all(shaped, ("exp", "tile"), split_axis=0, concat_axis=0, tiled=True)
    return moved.reshape(rows.shape)


def shards(
    exposure,
    row_taps,
    column_taps,
    basis_coef,
    warp_rows,
    warp_columns,
    warp_id,
    route_device,
    route_slot,
    weight,
):
    devices = lax.axis_size("exp") * lax.axis_size("tile")
    image = exposure[0]
    tile_rows, width = image.shape
    per_tile = tile_rows * width // (BLOCK * BLOCK)
    slot_count = SLOT_ROWS * SLOT_COLS
    ident = warp_id.reshape(devices, per_tile)

    above, below = swap_rims(image[:RIM], image[tile_rows - RIM :])
    rows, columns = band_matrices(row_taps, column_taps)
    weighted = forward(
        ident, weight, basis_coef, above, image, below, rows, columns, warp_rows, warp_columns
    )
    arrived = exchange(weighted, devices)

    owner = route_device.reshape(-1)
    place = route_slot.reshape(-1)
    block_weight = jnp.repeat(weight.reshape(-1), per_tile)
    by_owner = jnp.where(
        owner[None, :] == jnp.arange(devices, dtype=jnp.int32)[:, None], block_weight[None, :], 0.0
    )
    by_place = (place[:, None] == jnp.arange(slot_count, dtype=jnp.int32)[None, :]).astype(
        jnp.float32
    )
    total = jnp.dot(by_owner, by_place, precision=lax.Precision.HIGHEST)
    scale = 1.0 / jnp.maximum(total, 1.0)
    slots = (route_device * slot_count + route_slot).reshape(devices, per_tile)
    my_slots = lax.dynamic_slice_in_dim(slots, my_device(), 1, 0)
    block_scale = scale.reshape(-1)[my_slots]

    template_rows, coadd_rows = slot_sums(slots, arrived, block_scale)
    returned = exchange(template_rows, devices)
    owned = exchange(coadd_rows, devices)

    template, top, bottom = unwarp(
        ident, block_scale, returned, warp_rows, warp_columns, tile_rows
    )
    above, below = swap_rims(top, bottom)
    difference = subtract_inner(basis_coef, template, image, rows, columns)
    difference = subtract_outer(
        basis_coef, above, template, below, image, rows, columns, difference
    )
    return patch(scale, owned, difference), difference[None]


def solution(mesh):
    placed = (P("exp", "tile", None), P(), P(), P("exp", None), P(), P(), P(), P(), P(), P())
    return jax.shard_map(
        shards,
        mesh=mesh,
        in_specs=placed,
        out_specs=(P("exp", "tile"), P("exp", "tile", None)),
        check_vma=False,
    )
```

```python
import functools

import jax
import jax.numpy as jnp
from jax import lax
from jax.experimental import pallas as pl
from jax.experimental.pallas import tpu as pltpu
from jax.sharding import PartitionSpec as P

BLOCK = 128
HALF = 10
RIM = 16
CHUNK = 256
WIDE = 1024
SPAN = CHUNK + BLOCK
WINDOW = BLOCK + 2 * RIM
SLOT_ROWS = 8
SLOT_COLS = 8
LANES = 8
PAD = 8
VMEM = pl.BlockSpec(memory_space=pltpu.VMEM)
SMEM = pl.BlockSpec(memory_space=pltpu.SMEM)
ANY = pl.BlockSpec(memory_space=pl.ANY)
HBM = pl.BlockSpec(memory_space=pltpu.HBM)
GROUPS = 4


def grant(mebibytes):
    return pltpu.CompilerParams(vmem_limit_bytes=mebibytes * 1024 * 1024)


def make_bands(row_taps_ref, column_taps_ref, rows_ref, columns_ref):
    bases, taps = row_taps_ref.shape
    lead = RIM - HALF

    def banded(taps_ref, offsets):
        values = taps_ref[...].astype(jnp.float32)
        bands = [jnp.zeros(offsets.shape, jnp.float32) for _ in range(bases)]
        for tap in range(taps):
            hit = offsets == tap
            for base in range(bases):
                value = jnp.broadcast_to(values[base : base + 1, tap : tap + 1], offsets.shape)
                bands[base] = jnp.where(hit, value, bands[base])
        return [band.astype(jnp.bfloat16) for band in bands]

    shape = (BLOCK, WINDOW)
    across = lax.broadcasted_iota(jnp.int32, shape, 1) - lax.broadcasted_iota(jnp.int32, shape, 0)
    for base, band in enumerate(banded(row_taps_ref, across - lead)):
        rows_ref[base * BLOCK : (base + 1) * BLOCK, :] = band
    shape = (WINDOW, BLOCK)
    down = lax.broadcasted_iota(jnp.int32, shape, 0) - lax.broadcasted_iota(jnp.int32, shape, 1)
    columns_ref[...] = jnp.zeros_like(columns_ref)
    for base, band in enumerate(banded(column_taps_ref, down - lead)):
        top = base * CHUNK
        columns_ref[top : top + WINDOW - RIM, :BLOCK] = band[RIM:]
        columns_ref[top + BLOCK - RIM : top + CHUNK, BLOCK:] = band[: WINDOW - RIM]
        top = bases * CHUNK + base * BLOCK
        columns_ref[top : top + RIM, BLOCK:] = band[WINDOW - RIM :]
        columns_ref[top + BLOCK - RIM : top + BLOCK, :BLOCK] = band[:RIM]


def swap_rims(top, bottom):
    count = lax.axis_size("tile")
    forward = [(i, i + 1) for i in range(count - 1)]
    backward = [(target, source) for source, target in forward]
    return lax.ppermute(bottom, "tile", forward), lax.ppermute(top, "tile", backward)


def clear(pass_ref, start):
    bases, height, _ = pass_ref.shape
    pass_ref[:, :, start : start + BLOCK] = jnp.zeros((bases, height, BLOCK), pass_ref.dtype)


def row_step(lanes, start, to, strips, coef_ref, rows_ref, pass_ref):
    bases = pass_ref.shape[0]
    for first_row, count, pieces in strips:
        window = [
            ref[first : first + size, pl.ds(pl.multiple_of(start + shift, BLOCK), lanes)]
            for ref, first, size, shift in pieces
        ]
        window = window[0] if len(window) == 1 else jnp.concatenate(window, axis=0)
        depth = window.shape[0]
        if count == BLOCK and depth == WINDOW:
            band = rows_ref[...]
        else:
            band = jnp.concatenate(
                [rows_ref[base * BLOCK : base * BLOCK + count, :depth] for base in range(bases)],
                axis=0,
            )
        summed = jnp.dot(band, window, preferred_element_type=jnp.float32)
        for base in range(bases):
            pass_ref[
                base, first_row : first_row + count, pl.ds(pl.multiple_of(to, BLOCK), lanes)
            ] = (coef_ref[0, base] * summed[base * count : (base + 1) * count]).astype(jnp.bfloat16)


def column_step(index, count, columns_ref, pass_ref):
    bases = pass_ref.shape[0]
    right = lax.broadcasted_iota(jnp.int32, (count, BLOCK), 1) < BLOCK // 2
    summed = []
    for part in range(WIDE // CHUNK):
        at = index * WIDE + part * CHUNK

        def columns(shift, size):
            return pl.ds(pl.multiple_of(at + shift, BLOCK), size)

        middle = [pass_ref[base, :count, columns(BLOCK, CHUNK)] for base in range(bases)]
        sides = [
            jnp.where(
                right,
                pass_ref[base, :count, columns(BLOCK + CHUNK, BLOCK)],
                pass_ref[base, :count, columns(0, BLOCK)],
            )
            for base in range(bases)
        ]
        summed.append(
            jnp.dot(
                jnp.concatenate(middle + sides, axis=1),
                columns_ref[...],
                preferred_element_type=jnp.float32,
            )
        )
    return summed


def my_device():
    return lax.axis_index("exp") * lax.axis_size("tile") + lax.axis_index("tile")


def wide_copy(source, target, sems, first_row, rows):
    def copy(index):
        at = pl.ds(pl.multiple_of(index * WIDE, WIDE), WIDE)
        return pltpu.make_async_copy(
            source.at[pl.ds(first_row, rows), at], target.at[:, at], sems.at[index]
        )

    return copy


def passes(fetch, step, consume, pass_ref, width, load=None):
    wides = width // WIDE

    def wide_step(index):
        fetch(index).wait()
        step(WIDE, index * WIDE, BLOCK + index * WIDE)

    clear(pass_ref, 0)
    clear(pass_ref, BLOCK + width)
    wide_step(0)
    wide_step(1)
    if load is not None:
        load.wait()

    @pl.loop(0, wides - 2)
    def _(index):
        consume(index)
        wide_step(index + 2)

    @pl.loop(wides - 2, wides)
    def _(index):
        consume(index)


def forward_kernel(
    ident_ref,
    weight_ref,
    coef_ref,
    above_ref,
    image_hbm,
    below_ref,
    row_taps_ref,
    column_taps_ref,
    bank_rows_ref,
    bank_columns_ref,
    out_hbm,
    rows_ref,
    columns_ref,
    image_ref,
    pass_ref,
    matched_ref,
    turned_ref,
    out_ref,
    warp_rows_ref,
    warp_columns_ref,
    fetch_sems,
    load_sems,
    store_sems,
):
    tile_rows, width = image_ref.shape
    parts = tile_rows // BLOCK
    across = width // BLOCK
    items = parts * across
    pitch = items + PAD
    myself = my_device()
    weight = weight_ref[lax.axis_index("exp"), lax.axis_index("tile")]
    fetch = wide_copy(image_hbm, image_ref, fetch_sems, 0, tile_rows)
    loads = [
        pltpu.make_async_copy(bank_rows_ref, warp_rows_ref, load_sems.at[0]),
        pltpu.make_async_copy(bank_columns_ref, warp_columns_ref, load_sems.at[1]),
    ]
    for index in range(width // WIDE):
        fetch(index).start()
    for load in loads:
        load.start()
    make_bands(row_taps_ref, column_taps_ref, rows_ref, columns_ref)

    strips = [
        (0, BLOCK, [(above_ref, 0, RIM, 0), (image_ref, 0, BLOCK + RIM, 0)]),
        (BLOCK, BLOCK, [(image_ref, BLOCK - RIM, BLOCK + RIM, 0), (below_ref, 0, RIM, 0)]),
    ]
    step = functools.partial(
        row_step, strips=strips, coef_ref=coef_ref, rows_ref=rows_ref, pass_ref=pass_ref
    )

    def match_step(index):
        for inner, summed in enumerate(column_step(index, tile_rows, columns_ref, pass_ref)):
            matched_ref[:, pl.ds(pl.multiple_of(index * WIDE + inner * CHUNK, CHUNK), CHUNK)] = (
                summed.astype(jnp.bfloat16)
            )

    passes(fetch, step, match_step, pass_ref, width)
    for load in loads:
        load.wait()

    @pl.loop(0, across // 4)
    def _(quad):
        todo = []
        for part in range(parts):
            for inner in range(4):
                column = quad * 4 + inner
                ident = ident_ref[myself, part * across + column]
                piece = matched_ref[
                    part * BLOCK : (part + 1) * BLOCK,
                    pl.ds(pl.multiple_of(column * BLOCK, BLOCK), BLOCK),
                ]
                todo.append((part * across + column, ident, piece))
        todo = [
            (
                item,
                ident,
                jnp.dot(warp_rows_ref[ident], piece, preferred_element_type=jnp.float32).astype(
                    jnp.bfloat16
                ),
            )
            for item, ident, piece in todo
        ]
        todo = [
            (
                item,
                lax.dot_general(
                    first,
                    warp_columns_ref[ident],
                    (((1,), (1,)), ((), ())),
                    preferred_element_type=jnp.float32,
                ),
            )
            for item, ident, first in todo
        ]
        for item, second in todo:
            turned_ref[pl.ds(item, BLOCK, stride=pitch), :] = weight * second

    lines = out_ref.shape[0] // GROUPS

    def store(group):
        at = pl.ds(pl.multiple_of(group * lines, lines), lines)
        return pltpu.make_async_copy(out_ref.at[at], out_hbm.at[at], store_sems.at[group])

    for group in range(GROUPS):

        @pl.loop(group * BLOCK // GROUPS, (group + 1) * BLOCK // GROUPS, unroll=2)
        def _(row):
            to = pl.ds(pl.multiple_of(row * items, items), items)
            at = pl.ds(pl.multiple_of(row * pitch, PAD), items)
            out_ref[to, :] = turned_ref[at, :].astype(jnp.bfloat16)

        store(group).start()
    for group in range(GROUPS):
        store(group).wait()


def forward(
    ident, weight, coef, above, image, below, row_taps, column_taps, warp_rows, warp_columns
):
    tile_rows, width = image.shape
    bases = row_taps.shape[0]
    lines = tile_rows * width // BLOCK
    return pl.pallas_call(
        forward_kernel,
        out_shape=(
            jax.ShapeDtypeStruct((lines, BLOCK), jnp.bfloat16),
            jax.ShapeDtypeStruct((bases * BLOCK, WINDOW), jnp.bfloat16),
            jax.ShapeDtypeStruct((bases * SPAN, CHUNK), jnp.bfloat16),
        ),
        in_specs=[SMEM, SMEM, SMEM, VMEM, HBM, VMEM, VMEM, VMEM, HBM, HBM],
        out_specs=(HBM, VMEM, VMEM),
        scratch_shapes=[
            pltpu.VMEM((tile_rows, width), jnp.bfloat16),
            pltpu.VMEM((bases, tile_rows, width + 2 * BLOCK), jnp.bfloat16),
            pltpu.VMEM((tile_rows, width), jnp.bfloat16),
            pltpu.VMEM((lines + BLOCK * PAD, BLOCK), jnp.float32),
            pltpu.VMEM((lines, BLOCK), jnp.bfloat16),
            pltpu.VMEM(warp_rows.shape, jnp.bfloat16),
            pltpu.VMEM(warp_columns.shape, jnp.bfloat16),
            pltpu.SemaphoreType.DMA((width // WIDE,)),
            pltpu.SemaphoreType.DMA((2,)),
            pltpu.SemaphoreType.DMA((GROUPS,)),
        ],
        compiler_params=grant(58),
        name="match_warp",
    )(ident, weight, coef, above, image, below, row_taps, column_taps, warp_rows, warp_columns)


def slots_kernel(slot_hbm, arrived_ref, scale_ref, template_ref, coadd_ref, wide_ref, *refs):
    del scale_ref
    items, _, sources = slot_hbm.shape
    sums, tables, sems = refs[:LANES], refs[LANES : LANES + items], refs[LANES + items]
    loads = [pltpu.make_async_copy(slot_hbm.at[k], tables[k], sems.at[k]) for k in range(items)]
    for load in loads:
        load.start()

    def at(source):
        return pl.ds(pl.multiple_of(source * items, items), items)

    @pl.loop(0, sources)
    def _(source):
        wide_ref[at(source), :] = arrived_ref[at(source), :].astype(jnp.float32)
        for sum_ref in sums:
            sum_ref[at(source), :] = jnp.zeros((items, BLOCK), jnp.float32)

    for load in loads:
        load.wait()

    @pl.loop(0, sources)
    def _(source):
        for first in range(0, items, LANES):
            slots = [tables[first + lane][0, source] for lane in range(LANES)]
            values = [
                sum_ref[pl.ds(slot, 1), :] + wide_ref[pl.ds(source * items + first + lane, 1), :]
                for lane, (slot, sum_ref) in enumerate(zip(slots, sums))
            ]
            for slot, sum_ref, value in zip(slots, sums, values):
                sum_ref[pl.ds(slot, 1), :] = value

    @pl.loop(0, sources)
    def _(source):
        value = sums[0][at(source), :]
        for sum_ref in sums[1:]:
            value = value + sum_ref[at(source), :]
        sums[0][at(source), :] = value
        coadd_ref[at(source), :] = value.astype(jnp.bfloat16)

    @pl.loop(0, sources)
    def _(source):
        for item in range(items):
            slot = tables[item][0, source]
            wide_ref[pl.ds(source * items + item, 1), :] = sums[0][pl.ds(slot, 1), :]

    @pl.loop(0, sources)
    def _(source):
        template_ref[at(source), :] = wide_ref[at(source), :].astype(jnp.bfloat16)


def slot_sums(slots, arrived, scale):
    shape = jax.ShapeDtypeStruct(arrived.shape, jnp.bfloat16)
    sources, items = slots.shape
    return pl.pallas_call(
        slots_kernel,
        out_shape=(shape, shape),
        in_specs=[ANY, VMEM, SMEM],
        out_specs=(VMEM, VMEM),
        scratch_shapes=[pltpu.VMEM(arrived.shape, jnp.float32)] * (1 + LANES)
        + [pltpu.SMEM((1, sources), jnp.int32)] * items
        + [pltpu.SemaphoreType.DMA((items,))],
        compiler_params=grant(44),
        name="slot_sums",
    )(slots.T.reshape(items, 1, sources), arrived, scale)


def unwarp_kernel(
    ident_ref,
    scale_ref,
    returned_hbm,
    bank_rows_ref,
    bank_columns_ref,
    out_hbm,
    top_ref,
    bottom_ref,
    returned_ref,
    out_ref,
    wide_ref,
    warp_rows_ref,
    warp_columns_ref,
    fetch_sems,
    load_sems,
    store_sems,
):
    tile_rows, width = out_ref.shape
    across = width // BLOCK
    parts = tile_rows // BLOCK
    items = parts * across
    pitch = items + PAD
    myself = my_device()
    lines = returned_ref.shape[0] // GROUPS

    def fetch(group):
        at = pl.ds(group * lines, lines)
        return pltpu.make_async_copy(
            returned_hbm.at[at], returned_ref.at[at], fetch_sems.at[group]
        )

    loads = [
        pltpu.make_async_copy(bank_rows_ref, warp_rows_ref, load_sems.at[0]),
        pltpu.make_async_copy(bank_columns_ref, warp_columns_ref, load_sems.at[1]),
    ]
    for group in range(GROUPS):
        fetch(group).start()
    for load in loads:
        load.start()
    for group in range(GROUPS):
        fetch(group).wait()

        @pl.loop(group * BLOCK // GROUPS, (group + 1) * BLOCK // GROUPS, unroll=2)
        def _(row):
            to = pl.ds(pl.multiple_of(row * pitch, PAD), items)
            at = pl.ds(pl.multiple_of(row * items, items), items)
            wide_ref[to, :] = returned_ref[at, :].astype(jnp.float32)

    for load in loads:
        load.wait()

    def store(quad):
        at = pl.ds(pl.multiple_of(quad * 4 * BLOCK, 4 * BLOCK), 4 * BLOCK)
        return pltpu.make_async_copy(out_ref.at[:, at], out_hbm.at[:, at], store_sems.at[quad])

    @pl.loop(0, across // 4)
    def _(quad):
        todo = []
        for part in range(parts):
            for inner in range(4):
                column = quad * 4 + inner
                item = part * across + column
                ident = ident_ref[myself, item]
                numerator = wide_ref[pl.ds(item, BLOCK, stride=pitch), :].astype(jnp.bfloat16)
                todo.append((part, column, item, ident, numerator))
        todo = [
            (
                part,
                column,
                ident,
                scale_ref[0, item]
                * lax.dot_general(
                    warp_rows_ref[ident],
                    numerator,
                    (((0,), (0,)), ((), ())),
                    preferred_element_type=jnp.float32,
                ),
            )
            for part, column, item, ident, numerator in todo
        ]
        for part, column, ident, first in todo:
            image = jnp.dot(
                first.astype(jnp.bfloat16),
                warp_columns_ref[ident],
                preferred_element_type=jnp.float32,
            ).astype(jnp.bfloat16)
            to = pl.ds(pl.multiple_of(column * BLOCK, BLOCK), BLOCK)
            out_ref[part * BLOCK : (part + 1) * BLOCK, to] = image
            if part == 0:
                top_ref[:, to] = image[:RIM]
            if part == parts - 1:
                bottom_ref[:, to] = image[BLOCK - RIM :]
        store(quad).start()

    @pl.loop(0, across // 4)
    def _(quad):
        store(quad).wait()


def unwarp(ident, scale, returned, warp_rows, warp_columns, tile_rows):
    lines = returned.shape[0]
    width = lines * BLOCK // tile_rows
    rim = jax.ShapeDtypeStruct((RIM, width), jnp.bfloat16)
    return pl.pallas_call(
        unwarp_kernel,
        out_shape=(jax.ShapeDtypeStruct((tile_rows, width), jnp.bfloat16), rim, rim),
        in_specs=[SMEM, SMEM, HBM, HBM, HBM],
        out_specs=(HBM, VMEM, VMEM),
        scratch_shapes=[
            pltpu.VMEM((lines, BLOCK), jnp.bfloat16),
            pltpu.VMEM((tile_rows, width), jnp.bfloat16),
            pltpu.VMEM((lines + BLOCK * PAD, BLOCK), jnp.float32),
            pltpu.VMEM(warp_rows.shape, jnp.bfloat16),
            pltpu.VMEM(warp_columns.shape, jnp.bfloat16),
            pltpu.SemaphoreType.DMA((GROUPS,)),
            pltpu.SemaphoreType.DMA((2,)),
            pltpu.SemaphoreType.DMA((width // (4 * BLOCK),)),
        ],
        compiler_params=grant(58),
        name="unwarp",
    )(ident, scale, returned, warp_rows, warp_columns)


def inner_kernel(
    coef_ref,
    image_hbm,
    exposure_hbm,
    rows_ref,
    columns_ref,
    out_ref,
    image_ref,
    exposure_ref,
    pass_ref,
    stage_ref,
    fetch_sems,
    load_sem,
    sems,
):
    tile_rows, width = image_ref.shape
    inner = tile_rows - 2 * RIM
    fetch = wide_copy(image_hbm, image_ref, fetch_sems, 0, tile_rows)
    load = pltpu.make_async_copy(exposure_hbm.at[pl.ds(RIM, inner)], exposure_ref, load_sem)
    for index in range(width // WIDE):
        fetch(index).start()
    load.start()
    strips = [
        (0, BLOCK, [(image_ref, 0, WINDOW, 0)]),
        (BLOCK, inner - BLOCK, [(image_ref, BLOCK, tile_rows - BLOCK, 0)]),
    ]
    step = functools.partial(
        row_step, strips=strips, coef_ref=coef_ref, rows_ref=rows_ref, pass_ref=pass_ref
    )

    def store(index):
        at = pl.ds(pl.multiple_of(index * WIDE, WIDE), WIDE)
        return pltpu.make_async_copy(
            stage_ref.at[:, at], out_ref.at[pl.ds(RIM, inner), at], sems.at[index]
        )

    def subtract_step(index):
        for part, summed in enumerate(column_step(index, inner, columns_ref, pass_ref)):
            at = pl.ds(pl.multiple_of(index * WIDE + part * CHUNK, CHUNK), CHUNK)
            stage_ref[:, at] = exposure_ref[:, at].astype(jnp.float32) - summed
        store(index).start()

    passes(fetch, step, subtract_step, pass_ref, width, load)

    @pl.loop(0, width // WIDE)
    def _(index):
        store(index).wait()


def subtract_inner(coef, image, exposure, rows, columns):
    tile_rows, width = image.shape
    bases = rows.shape[0] // BLOCK
    inner = tile_rows - 2 * RIM
    return pl.pallas_call(
        inner_kernel,
        out_shape=jax.ShapeDtypeStruct((tile_rows, width), jnp.float32),
        in_specs=[SMEM, HBM, HBM, VMEM, VMEM],
        out_specs=HBM,
        scratch_shapes=[
            pltpu.VMEM((tile_rows, width), jnp.bfloat16),
            pltpu.VMEM((inner, width), jnp.bfloat16),
            pltpu.VMEM((bases, inner, width + 2 * BLOCK), jnp.bfloat16),
            pltpu.VMEM((inner, width), jnp.float32),
            pltpu.SemaphoreType.DMA((width // WIDE,)),
            pltpu.SemaphoreType.DMA,
            pltpu.SemaphoreType.DMA((width // WIDE,)),
        ],
        compiler_params=grant(58),
        name="subtract_inner",
    )(coef, image, exposure, rows, columns)


def finish_kernel(
    coef_ref,
    scale_ref,
    owned_ref,
    above_ref,
    image_hbm,
    below_ref,
    exposure_hbm,
    rows_ref,
    columns_ref,
    partial_hbm,
    patch_hbm,
    out_hbm,
    ends_ref,
    exposure_ref,
    pass_ref,
    stage_ref,
    wide_ref,
    patch_ref,
    fetch_sems,
    rim_sems,
    patch_sems,
):
    del partial_hbm
    tile_rows, width = out_hbm.shape
    slots = SLOT_ROWS * SLOT_COLS
    pitch = slots + PAD
    myself = my_device()
    pair = 2 * RIM

    def ends(source, target, size, first):
        return [
            pltpu.make_async_copy(
                source.at[pl.ds(0, size)], target.at[pl.ds(0, size)], fetch_sems.at[first]
            ),
            pltpu.make_async_copy(
                source.at[pl.ds(tile_rows - size, size)],
                target.at[pl.ds(size, size)],
                fetch_sems.at[first + 1],
            ),
        ]

    fetches = ends(image_hbm, ends_ref, pair, 0) + ends(exposure_hbm, exposure_ref, RIM, 2)
    for fetch in fetches:
        fetch.start()

    @pl.loop(0, BLOCK, unroll=2)
    def _(row):
        to = pl.ds(pl.multiple_of(row * pitch, PAD), slots)
        at = pl.ds(pl.multiple_of(row * slots, slots), slots)
        wide_ref[to, :] = owned_ref[at, :].astype(jnp.float32)

    def store(down):
        at = pl.ds(pl.multiple_of(down * BLOCK, BLOCK), BLOCK)
        return pltpu.make_async_copy(patch_ref.at[at], patch_hbm.at[at], patch_sems.at[down])

    @pl.loop(0, SLOT_ROWS)
    def _(down):
        to = pl.ds(pl.multiple_of(down * BLOCK, BLOCK), BLOCK)
        for across in range(SLOT_COLS):
            slot = down * SLOT_COLS + across
            patch_ref[to, across * BLOCK : (across + 1) * BLOCK] = (
                scale_ref[myself, slot] * wide_ref[pl.ds(slot, BLOCK, stride=pitch), :]
            )
        store(down).start()

    for fetch in fetches:
        fetch.wait()
    strips = [
        (0, RIM, [(above_ref, 0, RIM, 0), (ends_ref, 0, pair, 0)]),
        (RIM, RIM, [(ends_ref, pair, pair, 0), (below_ref, 0, RIM, 0)]),
    ]
    clear(pass_ref, 0)
    clear(pass_ref, BLOCK + width)
    for index in range(width // WIDE):
        row_step(
            WIDE, index * WIDE, BLOCK + index * WIDE, strips, coef_ref, rows_ref, pass_ref
        )
    for index in range(width // WIDE):
        for part, summed in enumerate(column_step(index, pair, columns_ref, pass_ref)):
            at = pl.ds(index * WIDE + part * CHUNK, CHUNK)
            stage_ref[:, at] = exposure_ref[:, at].astype(jnp.float32) - summed
    rims = [
        pltpu.make_async_copy(stage_ref.at[:RIM], out_hbm.at[:RIM], rim_sems.at[0]),
        pltpu.make_async_copy(
            stage_ref.at[RIM:], out_hbm.at[pl.ds(tile_rows - RIM, RIM)], rim_sems.at[1]
        ),
    ]
    for rim in rims:
        rim.start()
    for rim in rims:
        rim.wait()

    @pl.loop(0, SLOT_ROWS)
    def _(down):
        store(down).wait()


def finish(coef, scale, owned, above, image, below, exposure, rows, columns, partial):
    tile_rows, width = image.shape
    bases = rows.shape[0] // BLOCK
    shape = (SLOT_ROWS * BLOCK, SLOT_COLS * BLOCK)
    return pl.pallas_call(
        finish_kernel,
        out_shape=(
            jax.ShapeDtypeStruct(shape, jnp.float32),
            jax.ShapeDtypeStruct((tile_rows, width), jnp.float32),
        ),
        in_specs=[SMEM, SMEM, VMEM, VMEM, HBM, VMEM, HBM, VMEM, VMEM, HBM],
        out_specs=(HBM, HBM),
        scratch_shapes=[
            pltpu.VMEM((4 * RIM, width), jnp.bfloat16),
            pltpu.VMEM((2 * RIM, width), jnp.bfloat16),
            pltpu.VMEM((bases, 2 * RIM, width + 2 * BLOCK), jnp.bfloat16),
            pltpu.VMEM((2 * RIM, width), jnp.float32),
            pltpu.VMEM((owned.shape[0] + BLOCK * PAD, BLOCK), jnp.float32),
            pltpu.VMEM(shape, jnp.float32),
            pltpu.SemaphoreType.DMA((4,)),
            pltpu.SemaphoreType.DMA((2,)),
            pltpu.SemaphoreType.DMA((SLOT_ROWS,)),
        ],
        input_output_aliases={9: 1},
        compiler_params=grant(16),
        name="finish",
    )(coef, scale, owned, above, image, below, exposure, rows, columns, partial)


def exchange(rows, devices):
    shaped = rows.reshape(devices, -1, BLOCK)
    moved = lax.all_to_all(shaped, ("exp", "tile"), split_axis=0, concat_axis=0, tiled=True)
    return moved.reshape(rows.shape)


def shards(
    exposure,
    row_taps,
    column_taps,
    basis_coef,
    warp_rows,
    warp_columns,
    warp_id,
    route_device,
    route_slot,
    weight,
):
    devices = lax.axis_size("exp") * lax.axis_size("tile")
    image = exposure[0]
    tile_rows, width = image.shape
    per_tile = tile_rows * width // (BLOCK * BLOCK)
    slot_count = SLOT_ROWS * SLOT_COLS
    ident = warp_id.reshape(devices, per_tile)

    above, below = swap_rims(image[:RIM], image[tile_rows - RIM :])
    weighted, rows, columns = forward(
        ident,
        weight,
        basis_coef,
        above,
        image,
        below,
        row_taps,
        column_taps,
        warp_rows,
        warp_columns,
    )
    arrived = exchange(weighted, devices)

    owner = route_device.reshape(-1)
    place = route_slot.reshape(-1)
    block_weight = jnp.repeat(weight.reshape(-1), per_tile)
    by_owner = jnp.where(
        owner[None, :] == jnp.arange(devices, dtype=jnp.int32)[:, None], block_weight[None, :], 0.0
    )
    by_place = (place[:, None] == jnp.arange(slot_count, dtype=jnp.int32)[None, :]).astype(
        jnp.float32
    )
    total = jnp.dot(by_owner, by_place, precision=lax.Precision.HIGHEST)
    scale = 1.0 / jnp.maximum(total, 1.0)
    slots = (route_device * slot_count + route_slot).reshape(devices, per_tile)
    my_slots = lax.dynamic_slice_in_dim(slots, my_device(), 1, 0)
    block_scale = scale.reshape(-1)[my_slots]

    template_rows, coadd_rows = slot_sums(slots, arrived, block_scale)
    returned = exchange(template_rows, devices)
    owned = exchange(coadd_rows, devices)

    template, top, bottom = unwarp(
        ident, block_scale, returned, warp_rows, warp_columns, tile_rows
    )
    above, below = swap_rims(top, bottom)
    difference = subtract_inner(basis_coef, template, image, rows, columns)
    coadd, difference = finish(
        basis_coef, scale, owned, above, template, below, image, rows, columns, difference
    )
    return coadd, difference[None]


def solution(mesh):
    placed = (P("exp", "tile", None), P(), P(), P("exp", None), P(), P(), P(), P(), P(), P())
    return jax.shard_map(
        shards,
        mesh=mesh,
        in_specs=placed,
        out_specs=(P("exp", "tile"), P("exp", "tile", None)),
        check_vma=False,
    )
```

```python
import functools

import jax
import jax.numpy as jnp
from jax import lax
from jax.experimental import pallas as pl
from jax.experimental.pallas import tpu as pltpu
from jax.sharding import PartitionSpec as P

BLOCK = 128
HALF = 10
RIM = 16
CHUNK = 256
WIDE = 1024
SPAN = CHUNK + BLOCK
WINDOW = BLOCK + 2 * RIM
SLOT_ROWS = 8
SLOT_COLS = 8
LANES = 4
PAD = 8
VMEM = pl.BlockSpec(memory_space=pltpu.VMEM)
SMEM = pl.BlockSpec(memory_space=pltpu.SMEM)
ANY = pl.BlockSpec(memory_space=pl.ANY)
HBM = pl.BlockSpec(memory_space=pltpu.HBM)
GROUPS = 4


def grant(mebibytes):
    return pltpu.CompilerParams(vmem_limit_bytes=mebibytes * 1024 * 1024)


def bands_kernel(row_taps_ref, column_taps_ref, rows_ref, columns_ref):
    bases, taps = row_taps_ref.shape
    lead = RIM - HALF

    def banded(taps_ref, offsets):
        values = taps_ref[...].astype(jnp.float32)
        bands = [jnp.zeros(offsets.shape, jnp.float32) for _ in range(bases)]
        for tap in range(taps):
            hit = offsets == tap
            for base in range(bases):
                value = jnp.broadcast_to(values[base : base + 1, tap : tap + 1], offsets.shape)
                bands[base] = jnp.where(hit, value, bands[base])
        return [band.astype(jnp.bfloat16) for band in bands]

    shape = (BLOCK, WINDOW)
    across = lax.broadcasted_iota(jnp.int32, shape, 1) - lax.broadcasted_iota(jnp.int32, shape, 0)
    for base, band in enumerate(banded(row_taps_ref, across - lead)):
        rows_ref[base * BLOCK : (base + 1) * BLOCK, :] = band
    shape = (WINDOW, BLOCK)
    down = lax.broadcasted_iota(jnp.int32, shape, 0) - lax.broadcasted_iota(jnp.int32, shape, 1)
    columns_ref[...] = jnp.zeros_like(columns_ref)
    for base, band in enumerate(banded(column_taps_ref, down - lead)):
        top = base * CHUNK
        columns_ref[top : top + WINDOW - RIM, :BLOCK] = band[RIM:]
        columns_ref[top + BLOCK - RIM : top + CHUNK, BLOCK:] = band[: WINDOW - RIM]
        top = bases * CHUNK + base * BLOCK
        columns_ref[top : top + RIM, BLOCK:] = band[WINDOW - RIM :]
        columns_ref[top + BLOCK - RIM : top + BLOCK, :BLOCK] = band[:RIM]


def band_matrices(row_taps, column_taps):
    bases = row_taps.shape[0]
    return pl.pallas_call(
        bands_kernel,
        out_shape=(
            jax.ShapeDtypeStruct((bases * BLOCK, WINDOW), jnp.bfloat16),
            jax.ShapeDtypeStruct((bases * SPAN, CHUNK), jnp.bfloat16),
        ),
        in_specs=[VMEM, VMEM],
        out_specs=(VMEM, VMEM),
        compiler_params=grant(58),
        name="bands",
    )(row_taps, column_taps)


def swap_rims(top, bottom):
    count = lax.axis_size("tile")
    forward = [(i, i + 1) for i in range(count - 1)]
    backward = [(target, source) for source, target in forward]
    return lax.ppermute(bottom, "tile", forward), lax.ppermute(top, "tile", backward)


def clear(pass_ref, start):
    bases, height, _ = pass_ref.shape
    pass_ref[:, :, start : start + BLOCK] = jnp.zeros((bases, height, BLOCK), pass_ref.dtype)


def row_step(lanes, start, to, strips, coef_ref, rows_ref, pass_ref):
    bases = pass_ref.shape[0]
    for first_row, count, pieces in strips:
        window = [
            ref[first : first + size, pl.ds(pl.multiple_of(start + shift, BLOCK), lanes)]
            for ref, first, size, shift in pieces
        ]
        window = window[0] if len(window) == 1 else jnp.concatenate(window, axis=0)
        depth = window.shape[0]
        if count == BLOCK and depth == WINDOW:
            band = rows_ref[...]
        else:
            band = jnp.concatenate(
                [rows_ref[base * BLOCK : base * BLOCK + count, :depth] for base in range(bases)],
                axis=0,
            )
        summed = jnp.dot(band, window, preferred_element_type=jnp.float32)
        for base in range(bases):
            pass_ref[
                base, first_row : first_row + count, pl.ds(pl.multiple_of(to, BLOCK), lanes)
            ] = (coef_ref[0, base] * summed[base * count : (base + 1) * count]).astype(jnp.bfloat16)


def column_step(index, count, columns_ref, pass_ref):
    bases = pass_ref.shape[0]
    right = lax.broadcasted_iota(jnp.int32, (count, BLOCK), 1) < BLOCK // 2
    summed = []
    for part in range(WIDE // CHUNK):
        at = index * WIDE + part * CHUNK

        def columns(shift, size):
            return pl.ds(pl.multiple_of(at + shift, BLOCK), size)

        middle = [pass_ref[base, :count, columns(BLOCK, CHUNK)] for base in range(bases)]
        sides = [
            jnp.where(
                right,
                pass_ref[base, :count, columns(BLOCK + CHUNK, BLOCK)],
                pass_ref[base, :count, columns(0, BLOCK)],
            )
            for base in range(bases)
        ]
        summed.append(
            jnp.dot(
                jnp.concatenate(middle + sides, axis=1),
                columns_ref[...],
                preferred_element_type=jnp.float32,
            )
        )
    return summed


def my_device():
    return lax.axis_index("exp") * lax.axis_size("tile") + lax.axis_index("tile")


def wide_copy(source, target, sems, first_row, rows):
    def copy(index):
        at = pl.ds(pl.multiple_of(index * WIDE, WIDE), WIDE)
        return pltpu.make_async_copy(
            source.at[pl.ds(first_row, rows), at], target.at[:, at], sems.at[index]
        )

    return copy


def passes(fetch, step, consume, pass_ref, width, load=None):
    wides = width // WIDE

    def wide_step(index):
        fetch(index).wait()
        step(WIDE, index * WIDE, BLOCK + index * WIDE)

    clear(pass_ref, 0)
    clear(pass_ref, BLOCK + width)
    wide_step(0)
    wide_step(1)
    if load is not None:
        load.wait()

    @pl.loop(0, wides - 2)
    def _(index):
        consume(index)
        wide_step(index + 2)

    @pl.loop(wides - 2, wides)
    def _(index):
        consume(index)


def forward_kernel(
    ident_ref,
    weight_ref,
    coef_ref,
    above_ref,
    image_hbm,
    below_ref,
    rows_ref,
    columns_ref,
    bank_rows_ref,
    bank_columns_ref,
    out_hbm,
    image_ref,
    pass_ref,
    matched_ref,
    turned_ref,
    out_ref,
    warp_rows_ref,
    warp_columns_ref,
    fetch_sems,
    load_sems,
    store_sems,
):
    tile_rows, width = image_ref.shape
    parts = tile_rows // BLOCK
    across = width // BLOCK
    items = parts * across
    pitch = items + PAD
    myself = my_device()
    weight = weight_ref[lax.axis_index("exp"), lax.axis_index("tile")]
    fetch = wide_copy(image_hbm, image_ref, fetch_sems, 0, tile_rows)
    loads = [
        pltpu.make_async_copy(bank_rows_ref, warp_rows_ref, load_sems.at[0]),
        pltpu.make_async_copy(bank_columns_ref, warp_columns_ref, load_sems.at[1]),
    ]
    for index in range(width // WIDE):
        fetch(index).start()
    for load in loads:
        load.start()

    strips = [
        (0, BLOCK, [(above_ref, 0, RIM, 0), (image_ref, 0, BLOCK + RIM, 0)]),
        (BLOCK, BLOCK, [(image_ref, BLOCK - RIM, BLOCK + RIM, 0), (below_ref, 0, RIM, 0)]),
    ]
    step = functools.partial(
        row_step, strips=strips, coef_ref=coef_ref, rows_ref=rows_ref, pass_ref=pass_ref
    )

    def match_step(index):
        for inner, summed in enumerate(column_step(index, tile_rows, columns_ref, pass_ref)):
            matched_ref[:, pl.ds(pl.multiple_of(index * WIDE + inner * CHUNK, CHUNK), CHUNK)] = (
                summed.astype(jnp.bfloat16)
            )

    passes(fetch, step, match_step, pass_ref, width)
    for load in loads:
        load.wait()

    @pl.loop(0, across // 4)
    def _(quad):
        todo = []
        for part in range(parts):
            for inner in range(4):
                column = quad * 4 + inner
                ident = ident_ref[myself, part * across + column]
                piece = matched_ref[
                    part * BLOCK : (part + 1) * BLOCK,
                    pl.ds(pl.multiple_of(column * BLOCK, BLOCK), BLOCK),
                ]
                todo.append((part * across + column, ident, piece))
        todo = [
            (
                item,
                ident,
                jnp.dot(warp_rows_ref[ident], piece, preferred_element_type=jnp.float32).astype(
                    jnp.bfloat16
                ),
            )
            for item, ident, piece in todo
        ]
        todo = [
            (
                item,
                lax.dot_general(
                    first,
                    warp_columns_ref[ident],
                    (((1,), (1,)), ((), ())),
                    preferred_element_type=jnp.float32,
                ),
            )
            for item, ident, first in todo
        ]
        for item, second in todo:
            turned_ref[pl.ds(item, BLOCK, stride=pitch), :] = weight * second

    lines = out_ref.shape[0] // GROUPS

    def store(group):
        at = pl.ds(pl.multiple_of(group * lines, lines), lines)
        return pltpu.make_async_copy(out_ref.at[at], out_hbm.at[at], store_sems.at[group])

    for group in range(GROUPS):

        @pl.loop(group * BLOCK // GROUPS, (group + 1) * BLOCK // GROUPS, unroll=2)
        def _(row):
            to = pl.ds(pl.multiple_of(row * items, items), items)
            at = pl.ds(pl.multiple_of(row * pitch, PAD), items)
            out_ref[to, :] = turned_ref[at, :].astype(jnp.bfloat16)

        store(group).start()
    for group in range(GROUPS):
        store(group).wait()


def forward(
    ident, weight, coef, above, image, below, rows, columns, warp_rows, warp_columns
):
    tile_rows, width = image.shape
    bases = rows.shape[0] // BLOCK
    lines = tile_rows * width // BLOCK
    return pl.pallas_call(
        forward_kernel,
        out_shape=jax.ShapeDtypeStruct((lines, BLOCK), jnp.bfloat16),
        in_specs=[SMEM, SMEM, SMEM, VMEM, HBM, VMEM, VMEM, VMEM, HBM, HBM],
        out_specs=HBM,
        scratch_shapes=[
            pltpu.VMEM((tile_rows, width), jnp.bfloat16),
            pltpu.VMEM((bases, tile_rows, width + 2 * BLOCK), jnp.bfloat16),
            pltpu.VMEM((tile_rows, width), jnp.bfloat16),
            pltpu.VMEM((lines + BLOCK * PAD, BLOCK), jnp.float32),
            pltpu.VMEM((lines, BLOCK), jnp.bfloat16),
            pltpu.VMEM(warp_rows.shape, jnp.bfloat16),
            pltpu.VMEM(warp_columns.shape, jnp.bfloat16),
            pltpu.SemaphoreType.DMA((width // WIDE,)),
            pltpu.SemaphoreType.DMA((2,)),
            pltpu.SemaphoreType.DMA((GROUPS,)),
        ],
        compiler_params=grant(58),
        name="match_warp",
    )(ident, weight, coef, above, image, below, rows, columns, warp_rows, warp_columns)


def slots_kernel(
    slot_hbm, repeat_ref, arrived_ref, scale_ref, template_ref, coadd_ref, wide_ref, *refs
):
    del scale_ref
    items, _, sources = slot_hbm.shape
    sums, tables, sems = refs[:LANES], refs[LANES : LANES + items], refs[LANES + items]
    loads = [pltpu.make_async_copy(slot_hbm.at[k], tables[k], sems.at[k]) for k in range(items)]
    for load in loads:
        load.start()

    def at(source):
        return pl.ds(pl.multiple_of(source * items, items), items)

    @pl.loop(0, sources)
    def _(source):
        wide_ref[at(source), :] = arrived_ref[at(source), :].astype(jnp.float32)
        for sum_ref in sums:
            sum_ref[at(source), :] = jnp.zeros((items, BLOCK), jnp.float32)

    for load in loads:
        load.wait()

    def add(source, blocks, sum_ref):
        slots = [tables[block][0, source] for block in blocks]
        values = [
            sum_ref[pl.ds(slot, 1), :] + wide_ref[pl.ds(source * items + block, 1), :]
            for slot, block in zip(slots, blocks)
        ]
        for slot, value in zip(slots, values):
            sum_ref[pl.ds(slot, 1), :] = value

    groups = [list(range(first, first + LANES)) for first in range(0, items, LANES)]

    @pl.loop(0, sources)
    def _(source):
        repeats = repeat_ref[0, source]

        @pl.when(repeats == 0)
        def _():
            for index, blocks in enumerate(groups):
                add(source, blocks, sums[index % LANES])

        @pl.when(repeats != 0)
        def _():
            for index, blocks in enumerate(groups):
                repeated = (repeats // 2**index) % 2

                @pl.when(repeated == 0)
                def _():
                    add(source, blocks, sums[index % LANES])

                @pl.when(repeated != 0)
                def _():
                    for lane, block in enumerate(blocks):
                        add(source, [block], sums[lane])

    @pl.loop(0, sources)
    def _(source):
        value = sums[0][at(source), :]
        for sum_ref in sums[1:]:
            value = value + sum_ref[at(source), :]
        sums[0][at(source), :] = value
        coadd_ref[at(source), :] = value.astype(jnp.bfloat16)

    @pl.loop(0, sources)
    def _(source):
        for item in range(items):
            slot = tables[item][0, source]
            wide_ref[pl.ds(source * items + item, 1), :] = sums[0][pl.ds(slot, 1), :]

    @pl.loop(0, sources, unroll=2)
    def _(source):
        template_ref[at(source), :] = wide_ref[at(source), :].astype(jnp.bfloat16)


def group_repeats(slots):
    grouped = slots.T.reshape(-1, LANES, slots.shape[0])
    repeated = jnp.zeros(grouped[:, 0].shape, jnp.bool_)
    for later in range(1, LANES):
        for earlier in range(later):
            repeated = repeated | (grouped[:, later] == grouped[:, earlier])
    bits = 2 ** jnp.arange(grouped.shape[0], dtype=jnp.int32)
    return jnp.sum(jnp.where(repeated, bits[:, None], 0), axis=0, keepdims=True)


def slot_sums(slots, arrived, scale):
    shape = jax.ShapeDtypeStruct(arrived.shape, jnp.bfloat16)
    sources, items = slots.shape
    return pl.pallas_call(
        slots_kernel,
        out_shape=(shape, shape),
        in_specs=[ANY, SMEM, VMEM, SMEM],
        out_specs=(VMEM, VMEM),
        scratch_shapes=[pltpu.VMEM(arrived.shape, jnp.float32)] * (1 + LANES)
        + [pltpu.SMEM((1, sources), jnp.int32)] * items
        + [pltpu.SemaphoreType.DMA((items,))],
        compiler_params=grant(44),
        name="slot_sums",
    )(slots.T.reshape(items, 1, sources), group_repeats(slots), arrived, scale)


def unwarp_kernel(
    ident_ref,
    scale_ref,
    returned_ref,
    bank_rows_ref,
    bank_columns_ref,
    out_ref,
    top_ref,
    under_top_ref,
    over_bottom_ref,
    bottom_ref,
    wide_ref,
    warp_rows_ref,
    warp_columns_ref,
    sems,
):
    tile_rows, part_width = out_ref.shape
    across = part_width // BLOCK
    parts = tile_rows // BLOCK
    items = parts * across
    pitch = items + PAD
    myself = my_device()
    loads = [
        pltpu.make_async_copy(bank_rows_ref, warp_rows_ref, sems.at[0]),
        pltpu.make_async_copy(bank_columns_ref, warp_columns_ref, sems.at[1]),
    ]
    for load in loads:
        load.start()

    @pl.loop(0, BLOCK, unroll=4)
    def _(row):
        to = pl.ds(pl.multiple_of(row * pitch, PAD), items)
        at = pl.ds(pl.multiple_of(row * items, items), items)
        wide_ref[to, :] = returned_ref[at, :].astype(jnp.float32)

    for load in loads:
        load.wait()

    @pl.loop(0, across // 4)
    def _(quad):
        todo = []
        for part in range(parts):
            for inner in range(4):
                column = quad * 4 + inner
                item = part * across + column
                ident = ident_ref[myself, item]
                numerator = wide_ref[pl.ds(item, BLOCK, stride=pitch), :].astype(jnp.bfloat16)
                todo.append((part, column, item, ident, numerator))
        todo = [
            (
                part,
                column,
                ident,
                scale_ref[0, item]
                * lax.dot_general(
                    warp_rows_ref[ident],
                    numerator,
                    (((0,), (0,)), ((), ())),
                    preferred_element_type=jnp.float32,
                ),
            )
            for part, column, item, ident, numerator in todo
        ]
        for part, column, ident, first in todo:
            image = jnp.dot(
                first.astype(jnp.bfloat16),
                warp_columns_ref[ident],
                preferred_element_type=jnp.float32,
            ).astype(jnp.bfloat16)
            to = pl.ds(pl.multiple_of(column * BLOCK, BLOCK), BLOCK)
            out_ref[part * BLOCK : (part + 1) * BLOCK, to] = image
            if part == 0:
                top_ref[:, to] = image[:RIM]
                under_top_ref[:, to] = image[RIM : 2 * RIM]
            if part == parts - 1:
                over_bottom_ref[:, to] = image[BLOCK - 2 * RIM : BLOCK - RIM]
                bottom_ref[:, to] = image[BLOCK - RIM :]


def unwarp(ident, scale, returned, warp_rows, warp_columns, tile_rows):
    lines = returned.shape[0]
    part_width = lines * BLOCK // tile_rows
    rim = jax.ShapeDtypeStruct((RIM, part_width), jnp.bfloat16)
    return pl.pallas_call(
        unwarp_kernel,
        out_shape=(jax.ShapeDtypeStruct((tile_rows, part_width), jnp.bfloat16),) + (rim,) * 4,
        in_specs=[SMEM, SMEM, VMEM, ANY, ANY],
        out_specs=(VMEM,) * 5,
        scratch_shapes=[
            pltpu.VMEM((lines + BLOCK * PAD, BLOCK), jnp.float32),
            pltpu.VMEM(warp_rows.shape, jnp.bfloat16),
            pltpu.VMEM(warp_columns.shape, jnp.bfloat16),
            pltpu.SemaphoreType.DMA((2,)),
        ],
        compiler_params=grant(58),
        name="unwarp",
    )(ident, scale, returned, warp_rows, warp_columns)


def inner_kernel(
    coef_ref,
    image_hbm,
    exposure_hbm,
    rows_ref,
    columns_ref,
    out_ref,
    image_ref,
    exposure_ref,
    pass_ref,
    stage_ref,
    fetch_sems,
    load_sem,
    sems,
):
    tile_rows, width = image_ref.shape
    inner = tile_rows - 2 * RIM
    fetch = wide_copy(image_hbm, image_ref, fetch_sems, 0, tile_rows)
    load = pltpu.make_async_copy(exposure_hbm.at[pl.ds(RIM, inner)], exposure_ref, load_sem)
    for index in range(width // WIDE):
        fetch(index).start()
    load.start()
    strips = [
        (0, BLOCK, [(image_ref, 0, WINDOW, 0)]),
        (BLOCK, inner - BLOCK, [(image_ref, BLOCK, tile_rows - BLOCK, 0)]),
    ]
    step = functools.partial(
        row_step, strips=strips, coef_ref=coef_ref, rows_ref=rows_ref, pass_ref=pass_ref
    )

    def store(index):
        at = pl.ds(pl.multiple_of(index * WIDE, WIDE), WIDE)
        return pltpu.make_async_copy(
            stage_ref.at[:, at], out_ref.at[pl.ds(RIM, inner), at], sems.at[index]
        )

    def subtract_step(index):
        for part, summed in enumerate(column_step(index, inner, columns_ref, pass_ref)):
            at = pl.ds(pl.multiple_of(index * WIDE + part * CHUNK, CHUNK), CHUNK)
            stage_ref[:, at] = exposure_ref[:, at].astype(jnp.float32) - summed
        store(index).start()

    passes(fetch, step, subtract_step, pass_ref, width, load)

    @pl.loop(0, width // WIDE)
    def _(index):
        store(index).wait()


def subtract_inner(coef, image, exposure, rows, columns):
    tile_rows, width = image.shape
    bases = rows.shape[0] // BLOCK
    inner = tile_rows - 2 * RIM
    return pl.pallas_call(
        inner_kernel,
        out_shape=jax.ShapeDtypeStruct((tile_rows, width), jnp.float32),
        in_specs=[SMEM, HBM, HBM, VMEM, VMEM],
        out_specs=HBM,
        scratch_shapes=[
            pltpu.VMEM((tile_rows, width), jnp.bfloat16),
            pltpu.VMEM((inner, width), jnp.bfloat16),
            pltpu.VMEM((bases, inner, width + 2 * BLOCK), jnp.bfloat16),
            pltpu.VMEM((inner, width), jnp.float32),
            pltpu.SemaphoreType.DMA((width // WIDE,)),
            pltpu.SemaphoreType.DMA,
            pltpu.SemaphoreType.DMA((width // WIDE,)),
        ],
        compiler_params=grant(58),
        name="subtract_inner",
    )(coef, image, exposure, rows, columns)


def outer_kernel(
    coef_ref,
    above_ref,
    top_ref,
    under_top_ref,
    over_bottom_ref,
    bottom_ref,
    below_ref,
    exposure_hbm,
    rows_ref,
    columns_ref,
    partial_hbm,
    out_hbm,
    order_ref,
    exposure_ref,
    pass_ref,
    stage_ref,
    fetch_sems,
    store_sems,
):
    del partial_hbm
    tile_rows, width = out_hbm.shape
    order_ref[...] = jnp.zeros_like(order_ref)

    def ends(index):
        first = index * (tile_rows - RIM)
        here, there = pl.ds(index * RIM, RIM), pl.ds(first, RIM)
        return (
            pltpu.make_async_copy(
                exposure_hbm.at[there], exposure_ref.at[here], fetch_sems.at[index]
            ),
            pltpu.make_async_copy(stage_ref.at[here], out_hbm.at[there], store_sems.at[index]),
        )

    for index in range(2):
        ends(index)[0].start()
    strips = [
        (0, RIM, [(ref, 0, RIM, 0) for ref in (above_ref, top_ref, under_top_ref)]),
        (RIM, RIM, [(ref, 0, RIM, 0) for ref in (over_bottom_ref, bottom_ref, below_ref)]),
    ]
    clear(pass_ref, 0)
    clear(pass_ref, BLOCK + width)
    for index in range(width // WIDE):
        row_step(
            WIDE, index * WIDE, BLOCK + index * WIDE, strips, coef_ref, rows_ref, pass_ref
        )
    for index in range(2):
        ends(index)[0].wait()
    for index in range(width // WIDE):
        for part, summed in enumerate(column_step(index, 2 * RIM, columns_ref, pass_ref)):
            at = pl.ds(index * WIDE + part * CHUNK, CHUNK)
            stage_ref[:, at] = exposure_ref[:, at].astype(jnp.float32) - summed
    for index in range(2):
        ends(index)[1].start()
    for index in range(2):
        ends(index)[1].wait()


def subtract_outer(coef, rims, exposure, rows, columns, partial):
    tile_rows, width = exposure.shape
    bases = rows.shape[0] // BLOCK
    operands = (coef, *rims, exposure, rows, columns, partial)
    return pl.pallas_call(
        outer_kernel,
        out_shape=(
            jax.ShapeDtypeStruct((tile_rows, width), jnp.float32),
            jax.ShapeDtypeStruct((SLOT_ROWS, BLOCK), jnp.float32),
        ),
        in_specs=[SMEM] + [VMEM] * len(rims) + [HBM, VMEM, VMEM, HBM],
        out_specs=(HBM, VMEM),
        scratch_shapes=[
            pltpu.VMEM((2 * RIM, width), jnp.bfloat16),
            pltpu.VMEM((bases, 2 * RIM, width + 2 * BLOCK), jnp.bfloat16),
            pltpu.VMEM((2 * RIM, width), jnp.float32),
            pltpu.SemaphoreType.DMA((2,)),
            pltpu.SemaphoreType.DMA((2,)),
        ],
        input_output_aliases={len(operands) - 1: 0},
        compiler_params=grant(16),
        name="subtract_outer",
    )(*operands)


def patch_kernel(
    scale_ref, owned_hbm, order_ref, out_hbm, owned_ref, wide_ref, stage_ref, fetch_sems, store_sems
):
    del order_ref
    slots = SLOT_ROWS * SLOT_COLS
    pitch = slots + PAD
    myself = my_device()
    lines = owned_ref.shape[0] // GROUPS

    def fetch(group):
        at = pl.ds(group * lines, lines)
        return pltpu.make_async_copy(owned_hbm.at[at], owned_ref.at[at], fetch_sems.at[group])

    for group in range(GROUPS):
        fetch(group).start()
    for group in range(GROUPS):
        fetch(group).wait()

        @pl.loop(group * BLOCK // GROUPS, (group + 1) * BLOCK // GROUPS, unroll=4)
        def _(row):
            to = pl.ds(pl.multiple_of(row * pitch, PAD), slots)
            at = pl.ds(pl.multiple_of(row * slots, slots), slots)
            wide_ref[to, :] = owned_ref[at, :].astype(jnp.float32)

    def store(down):
        at = pl.ds(pl.multiple_of(down * BLOCK, BLOCK), BLOCK)
        return pltpu.make_async_copy(stage_ref.at[at], out_hbm.at[at], store_sems.at[down])

    @pl.loop(0, SLOT_ROWS)
    def _(down):
        to = pl.ds(pl.multiple_of(down * BLOCK, BLOCK), BLOCK)
        for across in range(SLOT_COLS):
            slot = down * SLOT_COLS + across
            stage_ref[to, across * BLOCK : (across + 1) * BLOCK] = (
                scale_ref[myself, slot] * wide_ref[pl.ds(slot, BLOCK, stride=pitch), :]
            )
        store(down).start()

    @pl.loop(0, SLOT_ROWS)
    def _(down):
        store(down).wait()


def patch(scale, owned, order):
    shape = (SLOT_ROWS * BLOCK, SLOT_COLS * BLOCK)
    return pl.pallas_call(
        patch_kernel,
        out_shape=jax.ShapeDtypeStruct(shape, jnp.float32),
        in_specs=[SMEM, HBM, VMEM],
        out_specs=HBM,
        scratch_shapes=[
            pltpu.VMEM(owned.shape, jnp.bfloat16),
            pltpu.VMEM((owned.shape[0] + BLOCK * PAD, BLOCK), jnp.float32),
            pltpu.VMEM(shape, jnp.float32),
            pltpu.SemaphoreType.DMA((GROUPS,)),
            pltpu.SemaphoreType.DMA((SLOT_ROWS,)),
        ],
        compiler_params=grant(14),
        name="patch",
    )(scale, owned, order)


def exchange(rows, devices):
    shaped = rows.reshape(devices, -1, BLOCK)
    moved = lax.all_to_all(shaped, ("exp", "tile"), split_axis=0, concat_axis=0, tiled=True)
    return moved.reshape(rows.shape)


def shards(
    exposure,
    row_taps,
    column_taps,
    basis_coef,
    warp_rows,
    warp_columns,
    warp_id,
    route_device,
    route_slot,
    weight,
):
    devices = lax.axis_size("exp") * lax.axis_size("tile")
    image = exposure[0]
    tile_rows, width = image.shape
    per_tile = tile_rows * width // (BLOCK * BLOCK)
    slot_count = SLOT_ROWS * SLOT_COLS
    ident = warp_id.reshape(devices, per_tile)

    above, below = swap_rims(image[:RIM], image[tile_rows - RIM :])
    rows, columns = band_matrices(row_taps, column_taps)
    weighted = forward(
        ident,
        weight,
        basis_coef,
        above,
        image,
        below,
        rows,
        columns,
        warp_rows,
        warp_columns,
    )
    arrived = exchange(weighted, devices)

    owner = route_device.reshape(-1)
    place = route_slot.reshape(-1)
    block_weight = jnp.repeat(weight.reshape(-1), per_tile)
    by_owner = jnp.where(
        owner[None, :] == jnp.arange(devices, dtype=jnp.int32)[:, None], block_weight[None, :], 0.0
    )
    by_place = (place[:, None] == jnp.arange(slot_count, dtype=jnp.int32)[None, :]).astype(
        jnp.float32
    )
    total = jnp.dot(by_owner, by_place, precision=lax.Precision.HIGHEST)
    scale = 1.0 / jnp.maximum(total, 1.0)
    slots = (route_device * slot_count + route_slot).reshape(devices, per_tile)
    my_slots = lax.dynamic_slice_in_dim(slots, my_device(), 1, 0)
    block_scale = scale.reshape(-1)[my_slots]

    template_rows, coadd_rows = slot_sums(slots, arrived, block_scale)
    returned = exchange(template_rows, devices)
    owned = exchange(coadd_rows, devices)

    template, top, under_top, over_bottom, bottom = unwarp(
        ident, block_scale, returned, warp_rows, warp_columns, tile_rows
    )
    above, below = swap_rims(top, bottom)
    difference = subtract_inner(basis_coef, template, image, rows, columns)
    rims = (above, top, under_top, over_bottom, bottom, below)
    difference, order = subtract_outer(basis_coef, rims, image, rows, columns, difference)
    return patch(scale, owned, order), difference[None]


def solution(mesh):
    placed = (P("exp", "tile", None), P(), P(), P("exp", None), P(), P(), P(), P(), P(), P())
    return jax.shard_map(
        shards,
        mesh=mesh,
        in_specs=placed,
        out_specs=(P("exp", "tile"), P("exp", "tile", None)),
        check_vma=False,
    )
```

```python
import functools

import jax
import jax.numpy as jnp
from jax import lax
from jax.experimental import pallas as pl
from jax.experimental.pallas import tpu as pltpu
from jax.sharding import PartitionSpec as P

BLOCK = 128
HALF = 10
RIM = 16
CHUNK = 256
WIDE = 1024
SPAN = CHUNK + BLOCK
WINDOW = BLOCK + 2 * RIM
SLOT_ROWS = 8
SLOT_COLS = 8
LANES = 8
PAD = 8
VMEM = pl.BlockSpec(memory_space=pltpu.VMEM)
SMEM = pl.BlockSpec(memory_space=pltpu.SMEM)
ANY = pl.BlockSpec(memory_space=pl.ANY)
HBM = pl.BlockSpec(memory_space=pltpu.HBM)
GROUPS = 4


def grant(mebibytes):
    return pltpu.CompilerParams(vmem_limit_bytes=mebibytes * 1024 * 1024)


def make_bands(row_taps_ref, column_taps_ref, rows_ref, columns_ref):
    bases, taps = row_taps_ref.shape
    lead = RIM - HALF

    def banded(taps_ref, offsets):
        values = taps_ref[...].astype(jnp.float32)
        bands = [jnp.zeros(offsets.shape, jnp.float32) for _ in range(bases)]
        for tap in range(taps):
            hit = offsets == tap
            for base in range(bases):
                value = jnp.broadcast_to(values[base : base + 1, tap : tap + 1], offsets.shape)
                bands[base] = jnp.where(hit, value, bands[base])
        return [band.astype(jnp.bfloat16) for band in bands]

    shape = (BLOCK, WINDOW)
    across = lax.broadcasted_iota(jnp.int32, shape, 1) - lax.broadcasted_iota(jnp.int32, shape, 0)
    for base, band in enumerate(banded(row_taps_ref, across - lead)):
        rows_ref[base * BLOCK : (base + 1) * BLOCK, :] = band
    shape = (WINDOW, BLOCK)
    down = lax.broadcasted_iota(jnp.int32, shape, 0) - lax.broadcasted_iota(jnp.int32, shape, 1)
    columns_ref[...] = jnp.zeros_like(columns_ref)
    for base, band in enumerate(banded(column_taps_ref, down - lead)):
        top = base * CHUNK
        columns_ref[top : top + WINDOW - RIM, :BLOCK] = band[RIM:]
        columns_ref[top + BLOCK - RIM : top + CHUNK, BLOCK:] = band[: WINDOW - RIM]
        top = bases * CHUNK + base * BLOCK
        columns_ref[top : top + RIM, BLOCK:] = band[WINDOW - RIM :]
        columns_ref[top + BLOCK - RIM : top + BLOCK, :BLOCK] = band[:RIM]


def swap_rims(top, bottom):
    count = lax.axis_size("tile")
    forward = [(i, i + 1) for i in range(count - 1)]
    backward = [(target, source) for source, target in forward]
    return lax.ppermute(bottom, "tile", forward), lax.ppermute(top, "tile", backward)


def clear(pass_ref, start):
    bases, height, _ = pass_ref.shape
    pass_ref[:, :, start : start + BLOCK] = jnp.zeros((bases, height, BLOCK), pass_ref.dtype)


def row_step(lanes, start, to, strips, coef_ref, rows_ref, pass_ref):
    bases = pass_ref.shape[0]
    for first_row, count, pieces in strips:
        window = [
            ref[first : first + size, pl.ds(pl.multiple_of(start + shift, BLOCK), lanes)]
            for ref, first, size, shift in pieces
        ]
        window = window[0] if len(window) == 1 else jnp.concatenate(window, axis=0)
        depth = window.shape[0]
        if count == BLOCK and depth == WINDOW:
            band = rows_ref[...]
        else:
            band = jnp.concatenate(
                [rows_ref[base * BLOCK : base * BLOCK + count, :depth] for base in range(bases)],
                axis=0,
            )
        summed = jnp.dot(band, window, preferred_element_type=jnp.float32)
        for base in range(bases):
            pass_ref[
                base, first_row : first_row + count, pl.ds(pl.multiple_of(to, BLOCK), lanes)
            ] = (coef_ref[0, base] * summed[base * count : (base + 1) * count]).astype(jnp.bfloat16)


def column_window(at, count, pass_ref):
    bases = pass_ref.shape[0]
    right = lax.broadcasted_iota(jnp.int32, (count, BLOCK), 1) < BLOCK // 2

    def columns(shift, size):
        return pl.ds(pl.multiple_of(at + shift, BLOCK), size)

    middle = [pass_ref[base, :count, columns(BLOCK, CHUNK)] for base in range(bases)]
    sides = [
        jnp.where(
            right,
            pass_ref[base, :count, columns(BLOCK + CHUNK, BLOCK)],
            pass_ref[base, :count, columns(0, BLOCK)],
        )
        for base in range(bases)
    ]
    return jnp.concatenate(middle + sides, axis=1)


def column_step(index, count, columns_ref, pass_ref):
    return [
        jnp.dot(
            column_window(index * WIDE + part * CHUNK, count, pass_ref),
            columns_ref[...],
            preferred_element_type=jnp.float32,
        )
        for part in range(WIDE // CHUNK)
    ]


def column_strip(count, columns_ref, pass_ref, consume):
    width = pass_ref.shape[2] - 2 * BLOCK
    chunks = width // CHUNK // 2
    for half in range(2):
        windows = [
            column_window((half * chunks + chunk) * CHUNK, count, pass_ref)
            for chunk in range(chunks)
        ]
        summed = jnp.dot(
            jnp.concatenate(windows, axis=0),
            columns_ref[...],
            preferred_element_type=jnp.float32,
        )
        for chunk in range(chunks):
            consume(
                pl.ds((half * chunks + chunk) * CHUNK, CHUNK),
                summed[chunk * count : (chunk + 1) * count],
            )


def my_device():
    return lax.axis_index("exp") * lax.axis_size("tile") + lax.axis_index("tile")


def wide_copy(source, target, sems, first_row, rows):
    def copy(index):
        at = pl.ds(pl.multiple_of(index * WIDE, WIDE), WIDE)
        return pltpu.make_async_copy(
            source.at[pl.ds(first_row, rows), at], target.at[:, at], sems.at[index]
        )

    return copy


def passes(fetch, step, consume, pass_ref, width, load=None):
    wides = width // WIDE

    def wide_step(index):
        fetch(index).wait()
        step(WIDE, index * WIDE, BLOCK + index * WIDE)

    clear(pass_ref, 0)
    clear(pass_ref, BLOCK + width)
    wide_step(0)
    wide_step(1)
    if load is not None:
        load.wait()

    @pl.loop(0, wides - 2)
    def _(index):
        consume(index)
        wide_step(index + 2)

    @pl.loop(wides - 2, wides)
    def _(index):
        consume(index)


def match_inner_kernel(
    coef_ref,
    row_taps_ref,
    column_taps_ref,
    image_hbm,
    rows_ref,
    columns_ref,
    out_hbm,
    image_ref,
    pass_ref,
    stage_ref,
    fetch_sems,
    store_sems,
):
    tile_rows, width = image_ref.shape
    inner = tile_rows - 2 * RIM
    fetch = wide_copy(image_hbm, image_ref, fetch_sems, 0, tile_rows)
    for index in range(width // WIDE):
        fetch(index).start()
    make_bands(row_taps_ref, column_taps_ref, rows_ref, columns_ref)
    step = functools.partial(
        row_step,
        strips=inner_strips(image_ref),
        coef_ref=coef_ref,
        rows_ref=rows_ref,
        pass_ref=pass_ref,
    )

    def store(index):
        at = pl.ds(pl.multiple_of(index * WIDE, WIDE), WIDE)
        return pltpu.make_async_copy(stage_ref.at[:, at], out_hbm.at[:, at], store_sems.at[index])

    def match_step(index):
        for part, summed in enumerate(column_step(index, inner, columns_ref, pass_ref)):
            at = pl.ds(pl.multiple_of(index * WIDE + part * CHUNK, CHUNK), CHUNK)
            stage_ref[:, at] = summed.astype(jnp.bfloat16)
        store(index).start()

    passes(fetch, step, match_step, pass_ref, width)

    @pl.loop(0, width // WIDE)
    def _(index):
        store(index).wait()


def inner_strips(image_ref):
    tile_rows = image_ref.shape[0]
    return [
        (0, BLOCK, [(image_ref, 0, WINDOW, 0)]),
        (BLOCK, tile_rows - 2 * RIM - BLOCK, [(image_ref, BLOCK, tile_rows - BLOCK, 0)]),
    ]


def match_inner(coef, row_taps, column_taps, image):
    tile_rows, width = image.shape
    bases = row_taps.shape[0]
    inner = tile_rows - 2 * RIM
    return pl.pallas_call(
        match_inner_kernel,
        out_shape=(
            jax.ShapeDtypeStruct((bases * BLOCK, WINDOW), jnp.bfloat16),
            jax.ShapeDtypeStruct((bases * SPAN, CHUNK), jnp.bfloat16),
            jax.ShapeDtypeStruct((inner, width), jnp.bfloat16),
        ),
        in_specs=[SMEM, VMEM, VMEM, HBM],
        out_specs=(VMEM, VMEM, HBM),
        scratch_shapes=[
            pltpu.VMEM((tile_rows, width), jnp.bfloat16),
            pltpu.VMEM((bases, inner, width + 2 * BLOCK), jnp.bfloat16),
            pltpu.VMEM((inner, width), jnp.bfloat16),
            pltpu.SemaphoreType.DMA((width // WIDE,)),
            pltpu.SemaphoreType.DMA((width // WIDE,)),
        ],
        compiler_params=grant(58),
        name="match_inner",
    )(coef, row_taps, column_taps, image)


def forward_kernel(
    ident_ref,
    weight_ref,
    coef_ref,
    above_ref,
    image_hbm,
    below_ref,
    inner_hbm,
    rows_ref,
    columns_ref,
    bank_rows_ref,
    bank_columns_ref,
    out_hbm,
    ends_ref,
    pass_ref,
    matched_ref,
    turned_ref,
    out_ref,
    warp_rows_ref,
    warp_columns_ref,
    fetch_sems,
    load_sems,
    store_sems,
):
    tile_rows, width = matched_ref.shape
    parts = tile_rows // BLOCK
    across = width // BLOCK
    items = parts * across
    pitch = items + PAD
    pair = 2 * RIM
    myself = my_device()
    weight = weight_ref[lax.axis_index("exp"), lax.axis_index("tile")]
    fetches = [
        pltpu.make_async_copy(
            image_hbm.at[pl.ds(end * (tile_rows - pair), pair)],
            ends_ref.at[pl.ds(end * pair, pair)],
            fetch_sems.at[end],
        )
        for end in range(2)
    ]
    loads = [
        pltpu.make_async_copy(
            inner_hbm, matched_ref.at[pl.ds(RIM, tile_rows - pair)], load_sems.at[0]
        ),
        pltpu.make_async_copy(bank_rows_ref, warp_rows_ref, load_sems.at[1]),
        pltpu.make_async_copy(bank_columns_ref, warp_columns_ref, load_sems.at[2]),
    ]
    for copy in fetches + loads:
        copy.start()
    for fetch in fetches:
        fetch.wait()
    strips = [
        (0, RIM, [(above_ref, 0, RIM, 0), (ends_ref, 0, pair, 0)]),
        (RIM, RIM, [(ends_ref, pair, pair, 0), (below_ref, 0, RIM, 0)]),
    ]
    clear(pass_ref, 0)
    clear(pass_ref, BLOCK + width)
    for index in range(width // WIDE):
        row_step(
            WIDE, index * WIDE, BLOCK + index * WIDE, strips, coef_ref, rows_ref, pass_ref
        )

    def match(at, summed):
        matched_ref[:RIM, at] = summed[:RIM].astype(jnp.bfloat16)
        matched_ref[tile_rows - RIM :, at] = summed[RIM:].astype(jnp.bfloat16)

    column_strip(pair, columns_ref, pass_ref, match)
    for load in loads:
        load.wait()

    @pl.loop(0, across // 4)
    def _(quad):
        todo = []
        for part in range(parts):
            for inner in range(4):
                column = quad * 4 + inner
                ident = ident_ref[myself, part * across + column]
                piece = matched_ref[
                    part * BLOCK : (part + 1) * BLOCK,
                    pl.ds(pl.multiple_of(column * BLOCK, BLOCK), BLOCK),
                ]
                todo.append((part * across + column, ident, piece))
        todo = [
            (
                item,
                ident,
                jnp.dot(warp_rows_ref[ident], piece, preferred_element_type=jnp.float32).astype(
                    jnp.bfloat16
                ),
            )
            for item, ident, piece in todo
        ]
        todo = [
            (
                item,
                lax.dot_general(
                    first,
                    warp_columns_ref[ident],
                    (((1,), (1,)), ((), ())),
                    preferred_element_type=jnp.float32,
                ),
            )
            for item, ident, first in todo
        ]
        for item, second in todo:
            turned_ref[pl.ds(item, BLOCK, stride=pitch), :] = weight * second

    lines = out_ref.shape[0] // GROUPS

    def store(group):
        at = pl.ds(pl.multiple_of(group * lines, lines), lines)
        return pltpu.make_async_copy(out_ref.at[at], out_hbm.at[at], store_sems.at[group])

    for group in range(GROUPS):

        @pl.loop(group * BLOCK // GROUPS, (group + 1) * BLOCK // GROUPS, unroll=2)
        def _(row):
            to = pl.ds(pl.multiple_of(row * items, items), items)
            at = pl.ds(pl.multiple_of(row * pitch, PAD), items)
            out_ref[to, :] = turned_ref[at, :].astype(jnp.bfloat16)

        store(group).start()
    for group in range(GROUPS):
        store(group).wait()


def forward(
    ident, weight, coef, above, image, below, inner, rows, columns, warp_rows, warp_columns
):
    tile_rows, width = image.shape
    bases = rows.shape[0] // BLOCK
    lines = tile_rows * width // BLOCK
    return pl.pallas_call(
        forward_kernel,
        out_shape=jax.ShapeDtypeStruct((lines, BLOCK), jnp.bfloat16),
        in_specs=[SMEM, SMEM, SMEM, VMEM, HBM, VMEM, HBM, VMEM, VMEM, HBM, HBM],
        out_specs=HBM,
        scratch_shapes=[
            pltpu.VMEM((4 * RIM, width), jnp.bfloat16),
            pltpu.VMEM((bases, 2 * RIM, width + 2 * BLOCK), jnp.bfloat16),
            pltpu.VMEM((tile_rows, width), jnp.bfloat16),
            pltpu.VMEM((lines + BLOCK * PAD, BLOCK), jnp.float32),
            pltpu.VMEM((lines, BLOCK), jnp.bfloat16),
            pltpu.VMEM(warp_rows.shape, jnp.bfloat16),
            pltpu.VMEM(warp_columns.shape, jnp.bfloat16),
            pltpu.SemaphoreType.DMA((2,)),
            pltpu.SemaphoreType.DMA((3,)),
            pltpu.SemaphoreType.DMA((GROUPS,)),
        ],
        compiler_params=grant(58),
        name="match_warp",
    )(ident, weight, coef, above, image, below, inner, rows, columns, warp_rows, warp_columns)


def slots_kernel(slot_hbm, arrived_ref, scale_ref, template_ref, coadd_ref, wide_ref, *refs):
    del scale_ref
    items, _, sources = slot_hbm.shape
    sums, tables, sems = refs[:LANES], refs[LANES : LANES + items], refs[LANES + items]
    loads = [pltpu.make_async_copy(slot_hbm.at[k], tables[k], sems.at[k]) for k in range(items)]
    for load in loads:
        load.start()

    def at(source):
        return pl.ds(pl.multiple_of(source * items, items), items)

    @pl.loop(0, sources)
    def _(source):
        wide_ref[at(source), :] = arrived_ref[at(source), :].astype(jnp.float32)
        for sum_ref in sums:
            sum_ref[at(source), :] = jnp.zeros((items, BLOCK), jnp.float32)

    for load in loads:
        load.wait()

    @pl.loop(0, sources)
    def _(source):
        for first in range(0, items, LANES):
            slots = [tables[first + lane][0, source] for lane in range(LANES)]
            values = [
                sum_ref[pl.ds(slot, 1), :] + wide_ref[pl.ds(source * items + first + lane, 1), :]
                for lane, (slot, sum_ref) in enumerate(zip(slots, sums))
            ]
            for slot, sum_ref, value in zip(slots, sums, values):
                sum_ref[pl.ds(slot, 1), :] = value

    @pl.loop(0, sources)
    def _(source):
        value = sums[0][at(source), :]
        for sum_ref in sums[1:]:
            value = value + sum_ref[at(source), :]
        sums[0][at(source), :] = value
        coadd_ref[at(source), :] = value.astype(jnp.bfloat16)

    @pl.loop(0, sources)
    def _(source):
        for item in range(items):
            slot = tables[item][0, source]
            wide_ref[pl.ds(source * items + item, 1), :] = sums[0][pl.ds(slot, 1), :]

    @pl.loop(0, sources)
    def _(source):
        template_ref[at(source), :] = wide_ref[at(source), :].astype(jnp.bfloat16)


def slot_sums(slots, arrived, scale):
    shape = jax.ShapeDtypeStruct(arrived.shape, jnp.bfloat16)
    sources, items = slots.shape
    return pl.pallas_call(
        slots_kernel,
        out_shape=(shape, shape),
        in_specs=[ANY, VMEM, SMEM],
        out_specs=(VMEM, VMEM),
        scratch_shapes=[pltpu.VMEM(arrived.shape, jnp.float32)] * (1 + LANES)
        + [pltpu.SMEM((1, sources), jnp.int32)] * items
        + [pltpu.SemaphoreType.DMA((items,))],
        compiler_params=grant(44),
        name="slot_sums",
    )(slots.T.reshape(items, 1, sources), arrived, scale)


def unwarp_kernel(
    ident_ref,
    scale_ref,
    returned_ref,
    bank_rows_ref,
    bank_columns_ref,
    out_ref,
    top_ref,
    under_top_ref,
    over_bottom_ref,
    bottom_ref,
    wide_ref,
    warp_rows_ref,
    warp_columns_ref,
    sems,
):
    tile_rows, part_width = out_ref.shape
    across = part_width // BLOCK
    parts = tile_rows // BLOCK
    items = parts * across
    pitch = items + PAD
    myself = my_device()
    loads = [
        pltpu.make_async_copy(bank_rows_ref, warp_rows_ref, sems.at[0]),
        pltpu.make_async_copy(bank_columns_ref, warp_columns_ref, sems.at[1]),
    ]
    for load in loads:
        load.start()

    @pl.loop(0, BLOCK, unroll=4)
    def _(row):
        to = pl.ds(pl.multiple_of(row * pitch, PAD), items)
        at = pl.ds(pl.multiple_of(row * items, items), items)
        wide_ref[to, :] = returned_ref[at, :].astype(jnp.float32)

    for load in loads:
        load.wait()

    @pl.loop(0, across // 4)
    def _(quad):
        todo = []
        for part in range(parts):
            for inner in range(4):
                column = quad * 4 + inner
                item = part * across + column
                ident = ident_ref[myself, item]
                numerator = wide_ref[pl.ds(item, BLOCK, stride=pitch), :].astype(jnp.bfloat16)
                todo.append((part, column, item, ident, numerator))
        todo = [
            (
                part,
                column,
                ident,
                scale_ref[0, item]
                * lax.dot_general(
                    warp_rows_ref[ident],
                    numerator,
                    (((0,), (0,)), ((), ())),
                    preferred_element_type=jnp.float32,
                ),
            )
            for part, column, item, ident, numerator in todo
        ]
        for part, column, ident, first in todo:
            image = jnp.dot(
                first.astype(jnp.bfloat16),
                warp_columns_ref[ident],
                preferred_element_type=jnp.float32,
            ).astype(jnp.bfloat16)
            to = pl.ds(pl.multiple_of(column * BLOCK, BLOCK), BLOCK)
            out_ref[part * BLOCK : (part + 1) * BLOCK, to] = image
            if part == 0:
                top_ref[:, to] = image[:RIM]
                under_top_ref[:, to] = image[RIM : 2 * RIM]
            if part == parts - 1:
                over_bottom_ref[:, to] = image[BLOCK - 2 * RIM : BLOCK - RIM]
                bottom_ref[:, to] = image[BLOCK - RIM :]


def unwarp(ident, scale, returned, warp_rows, warp_columns, tile_rows):
    lines = returned.shape[0]
    part_width = lines * BLOCK // tile_rows
    rim = jax.ShapeDtypeStruct((RIM, part_width), jnp.bfloat16)
    return pl.pallas_call(
        unwarp_kernel,
        out_shape=(jax.ShapeDtypeStruct((tile_rows, part_width), jnp.bfloat16),) + (rim,) * 4,
        in_specs=[SMEM, SMEM, VMEM, ANY, ANY],
        out_specs=(VMEM,) * 5,
        scratch_shapes=[
            pltpu.VMEM((lines + BLOCK * PAD, BLOCK), jnp.float32),
            pltpu.VMEM(warp_rows.shape, jnp.bfloat16),
            pltpu.VMEM(warp_columns.shape, jnp.bfloat16),
            pltpu.SemaphoreType.DMA((2,)),
        ],
        compiler_params=grant(58),
        name="unwarp",
    )(ident, scale, returned, warp_rows, warp_columns)


def inner_kernel(
    coef_ref,
    image_hbm,
    exposure_hbm,
    rows_ref,
    columns_ref,
    out_ref,
    image_ref,
    exposure_ref,
    pass_ref,
    stage_ref,
    fetch_sems,
    load_sem,
    sems,
):
    tile_rows, width = image_ref.shape
    inner = tile_rows - 2 * RIM
    fetch = wide_copy(image_hbm, image_ref, fetch_sems, 0, tile_rows)
    load = pltpu.make_async_copy(exposure_hbm.at[pl.ds(RIM, inner)], exposure_ref, load_sem)
    for index in range(width // WIDE):
        fetch(index).start()
    load.start()
    step = functools.partial(
        row_step,
        strips=inner_strips(image_ref),
        coef_ref=coef_ref,
        rows_ref=rows_ref,
        pass_ref=pass_ref,
    )

    def store(index):
        at = pl.ds(pl.multiple_of(index * WIDE, WIDE), WIDE)
        return pltpu.make_async_copy(
            stage_ref.at[:, at], out_ref.at[pl.ds(RIM, inner), at], sems.at[index]
        )

    def subtract_step(index):
        for part, summed in enumerate(column_step(index, inner, columns_ref, pass_ref)):
            at = pl.ds(pl.multiple_of(index * WIDE + part * CHUNK, CHUNK), CHUNK)
            stage_ref[:, at] = exposure_ref[:, at].astype(jnp.float32) - summed
        store(index).start()

    passes(fetch, step, subtract_step, pass_ref, width, load)

    @pl.loop(0, width // WIDE)
    def _(index):
        store(index).wait()


def subtract_inner(coef, image, exposure, rows, columns):
    tile_rows, width = image.shape
    bases = rows.shape[0] // BLOCK
    inner = tile_rows - 2 * RIM
    return pl.pallas_call(
        inner_kernel,
        out_shape=jax.ShapeDtypeStruct((tile_rows, width), jnp.float32),
        in_specs=[SMEM, HBM, HBM, VMEM, VMEM],
        out_specs=HBM,
        scratch_shapes=[
            pltpu.VMEM((tile_rows, width), jnp.bfloat16),
            pltpu.VMEM((inner, width), jnp.bfloat16),
            pltpu.VMEM((bases, inner, width + 2 * BLOCK), jnp.bfloat16),
            pltpu.VMEM((inner, width), jnp.float32),
            pltpu.SemaphoreType.DMA((width // WIDE,)),
            pltpu.SemaphoreType.DMA,
            pltpu.SemaphoreType.DMA((width // WIDE,)),
        ],
        compiler_params=grant(58),
        name="subtract_inner",
    )(coef, image, exposure, rows, columns)


def outer_kernel(
    coef_ref,
    above_ref,
    top_ref,
    under_top_ref,
    over_bottom_ref,
    bottom_ref,
    below_ref,
    exposure_hbm,
    rows_ref,
    columns_ref,
    partial_hbm,
    out_hbm,
    order_ref,
    exposure_ref,
    pass_ref,
    stage_ref,
    fetch_sems,
    store_sems,
):
    del partial_hbm
    tile_rows, width = out_hbm.shape
    order_ref[...] = jnp.zeros_like(order_ref)

    def ends(index):
        first = index * (tile_rows - RIM)
        here, there = pl.ds(index * RIM, RIM), pl.ds(first, RIM)
        return (
            pltpu.make_async_copy(
                exposure_hbm.at[there], exposure_ref.at[here], fetch_sems.at[index]
            ),
            pltpu.make_async_copy(stage_ref.at[here], out_hbm.at[there], store_sems.at[index]),
        )

    fetches, stores = zip(*(ends(index) for index in range(2)))
    for fetch in fetches:
        fetch.start()
    strips = [
        (0, RIM, [(ref, 0, RIM, 0) for ref in (above_ref, top_ref, under_top_ref)]),
        (RIM, RIM, [(ref, 0, RIM, 0) for ref in (over_bottom_ref, bottom_ref, below_ref)]),
    ]
    clear(pass_ref, 0)
    clear(pass_ref, BLOCK + width)
    for index in range(width // WIDE):
        row_step(
            WIDE, index * WIDE, BLOCK + index * WIDE, strips, coef_ref, rows_ref, pass_ref
        )
    for fetch in fetches:
        fetch.wait()

    def subtract(at, summed):
        stage_ref[:, at] = exposure_ref[:, at].astype(jnp.float32) - summed

    column_strip(2 * RIM, columns_ref, pass_ref, subtract)
    for store in stores:
        store.start()
    for store in stores:
        store.wait()


def subtract_outer(coef, rims, exposure, rows, columns, partial):
    tile_rows, width = exposure.shape
    bases = rows.shape[0] // BLOCK
    operands = (coef, *rims, exposure, rows, columns, partial)
    return pl.pallas_call(
        outer_kernel,
        out_shape=(
            jax.ShapeDtypeStruct((tile_rows, width), jnp.float32),
            jax.ShapeDtypeStruct((SLOT_ROWS, BLOCK), jnp.float32),
        ),
        in_specs=[SMEM] + [VMEM] * len(rims) + [HBM, VMEM, VMEM, HBM],
        out_specs=(HBM, VMEM),
        scratch_shapes=[
            pltpu.VMEM((2 * RIM, width), jnp.bfloat16),
            pltpu.VMEM((bases, 2 * RIM, width + 2 * BLOCK), jnp.bfloat16),
            pltpu.VMEM((2 * RIM, width), jnp.float32),
            pltpu.SemaphoreType.DMA((2,)),
            pltpu.SemaphoreType.DMA((2,)),
        ],
        input_output_aliases={len(operands) - 1: 0},
        compiler_params=grant(16),
        name="subtract_outer",
    )(*operands)


def patch_kernel(
    scale_ref, owned_hbm, order_ref, out_hbm, owned_ref, wide_ref, stage_ref, fetch_sems, store_sems
):
    del order_ref
    slots = SLOT_ROWS * SLOT_COLS
    pitch = slots + PAD
    myself = my_device()
    lines = owned_ref.shape[0] // GROUPS
    count = BLOCK // GROUPS

    def fetch(group):
        at = pl.ds(group * lines, lines)
        return pltpu.make_async_copy(owned_hbm.at[at], owned_ref.at[at], fetch_sems.at[group])

    def store(group, down):
        at = pl.ds(pl.multiple_of(down * BLOCK + group * count, count), count)
        return pltpu.make_async_copy(
            stage_ref.at[at], out_hbm.at[at], store_sems.at[group, down]
        )

    for group in range(GROUPS):
        fetch(group).start()
    for group in range(GROUPS):
        fetch(group).wait()

        @pl.loop(group * count, (group + 1) * count, unroll=4)
        def _(row):
            to = pl.ds(pl.multiple_of(row * pitch, PAD), slots)
            at = pl.ds(pl.multiple_of(row * slots, slots), slots)
            wide_ref[to, :] = owned_ref[at, :].astype(jnp.float32)

        @pl.loop(0, SLOT_ROWS)
        def _(down):
            to = pl.ds(pl.multiple_of(down * BLOCK + group * count, count), count)
            for across in range(SLOT_COLS):
                slot = down * SLOT_COLS + across
                stage_ref[to, across * BLOCK : (across + 1) * BLOCK] = (
                    scale_ref[myself, slot]
                    * wide_ref[pl.ds(group * count * pitch + slot, count, stride=pitch), :]
                )
            store(group, down).start()

    for group in range(GROUPS):

        @pl.loop(0, SLOT_ROWS)
        def _(down):
            store(group, down).wait()


def patch(scale, owned, order):
    shape = (SLOT_ROWS * BLOCK, SLOT_COLS * BLOCK)
    return pl.pallas_call(
        patch_kernel,
        out_shape=jax.ShapeDtypeStruct(shape, jnp.float32),
        in_specs=[SMEM, HBM, VMEM],
        out_specs=HBM,
        scratch_shapes=[
            pltpu.VMEM(owned.shape, jnp.bfloat16),
            pltpu.VMEM((owned.shape[0] + BLOCK * PAD, BLOCK), jnp.float32),
            pltpu.VMEM(shape, jnp.float32),
            pltpu.SemaphoreType.DMA((GROUPS,)),
            pltpu.SemaphoreType.DMA((GROUPS, SLOT_ROWS)),
        ],
        compiler_params=grant(14),
        name="patch",
    )(scale, owned, order)


def exchange(rows, devices):
    shaped = rows.reshape(devices, -1, BLOCK)
    moved = lax.all_to_all(shaped, ("exp", "tile"), split_axis=0, concat_axis=0, tiled=True)
    return moved.reshape(rows.shape)


def shards(
    exposure,
    row_taps,
    column_taps,
    basis_coef,
    warp_rows,
    warp_columns,
    warp_id,
    route_device,
    route_slot,
    weight,
):
    devices = lax.axis_size("exp") * lax.axis_size("tile")
    image = exposure[0]
    tile_rows, width = image.shape
    per_tile = tile_rows * width // (BLOCK * BLOCK)
    slot_count = SLOT_ROWS * SLOT_COLS
    ident = warp_id.reshape(devices, per_tile)

    above, below = swap_rims(image[:RIM], image[tile_rows - RIM :])
    rows, columns, inner = match_inner(basis_coef, row_taps, column_taps, image)
    weighted = forward(
        ident,
        weight,
        basis_coef,
        above,
        image,
        below,
        inner,
        rows,
        columns,
        warp_rows,
        warp_columns,
    )
    arrived = exchange(weighted, devices)

    owner = route_device.reshape(-1)
    place = route_slot.reshape(-1)
    block_weight = jnp.repeat(weight.reshape(-1), per_tile)
    by_owner = jnp.where(
        owner[None, :] == jnp.arange(devices, dtype=jnp.int32)[:, None], block_weight[None, :], 0.0
    )
    by_place = (place[:, None] == jnp.arange(slot_count, dtype=jnp.int32)[None, :]).astype(
        jnp.float32
    )
    total = jnp.dot(by_owner, by_place, precision=lax.Precision.HIGHEST)
    scale = 1.0 / jnp.maximum(total, 1.0)
    slots = (route_device * slot_count + route_slot).reshape(devices, per_tile)
    my_slots = lax.dynamic_slice_in_dim(slots, my_device(), 1, 0)
    block_scale = scale.reshape(-1)[my_slots]

    template_rows, coadd_rows = slot_sums(slots, arrived, block_scale)
    returned = exchange(template_rows, devices)
    owned = exchange(coadd_rows, devices)

    template, top, under_top, over_bottom, bottom = unwarp(
        ident, block_scale, returned, warp_rows, warp_columns, tile_rows
    )
    above, below = swap_rims(top, bottom)
    difference = subtract_inner(basis_coef, template, image, rows, columns)
    rims = (above, top, under_top, over_bottom, bottom, below)
    difference, order = subtract_outer(basis_coef, rims, image, rows, columns, difference)
    return patch(scale, owned, order), difference[None]


def solution(mesh):
    placed = (P("exp", "tile", None), P(), P(), P("exp", None), P(), P(), P(), P(), P(), P())
    return jax.shard_map(
        shards,
        mesh=mesh,
        in_specs=placed,
        out_specs=(P("exp", "tile"), P("exp", "tile", None)),
        check_vma=False,
    )
```

```python
import functools

import jax
import jax.numpy as jnp
from jax import lax
from jax.experimental import pallas as pl
from jax.experimental.pallas import tpu as pltpu
from jax.sharding import PartitionSpec as P

BLOCK = 128
HALF = 10
RIM = 16
CHUNK = 256
WIDE = 1024
SPAN = CHUNK + BLOCK
WINDOW = BLOCK + 2 * RIM
SLOT_ROWS = 8
SLOT_COLS = 8
LANES = 8
PAD = 8
VMEM = pl.BlockSpec(memory_space=pltpu.VMEM)
SMEM = pl.BlockSpec(memory_space=pltpu.SMEM)
ANY = pl.BlockSpec(memory_space=pl.ANY)
HBM = pl.BlockSpec(memory_space=pltpu.HBM)
GROUPS = 4


def grant(mebibytes):
    return pltpu.CompilerParams(vmem_limit_bytes=int(mebibytes * 1024 * 1024))


def bands_kernel(row_taps_ref, column_taps_ref, rows_ref, columns_ref):
    bases, taps = row_taps_ref.shape
    lead = RIM - HALF

    def banded(taps_ref, offsets):
        values = taps_ref[...].astype(jnp.float32)
        bands = [jnp.zeros(offsets.shape, jnp.float32) for _ in range(bases)]
        for tap in range(taps):
            hit = offsets == tap
            for base in range(bases):
                value = jnp.broadcast_to(values[base : base + 1, tap : tap + 1], offsets.shape)
                bands[base] = jnp.where(hit, value, bands[base])
        return [band.astype(jnp.bfloat16) for band in bands]

    shape = (BLOCK, WINDOW)
    across = lax.broadcasted_iota(jnp.int32, shape, 1) - lax.broadcasted_iota(jnp.int32, shape, 0)
    for base, band in enumerate(banded(row_taps_ref, across - lead)):
        rows_ref[base * BLOCK : (base + 1) * BLOCK, :] = band
    shape = (WINDOW, BLOCK)
    down = lax.broadcasted_iota(jnp.int32, shape, 0) - lax.broadcasted_iota(jnp.int32, shape, 1)
    columns_ref[...] = jnp.zeros_like(columns_ref)
    for base, band in enumerate(banded(column_taps_ref, down - lead)):
        top = base * CHUNK
        columns_ref[top : top + WINDOW - RIM, :BLOCK] = band[RIM:]
        columns_ref[top + BLOCK - RIM : top + CHUNK, BLOCK:] = band[: WINDOW - RIM]
        top = bases * CHUNK + base * BLOCK
        columns_ref[top : top + RIM, BLOCK:] = band[WINDOW - RIM :]
        columns_ref[top + BLOCK - RIM : top + BLOCK, :BLOCK] = band[:RIM]


def band_matrices(row_taps, column_taps):
    bases = row_taps.shape[0]
    return pl.pallas_call(
        bands_kernel,
        out_shape=(
            jax.ShapeDtypeStruct((bases * BLOCK, WINDOW), jnp.bfloat16),
            jax.ShapeDtypeStruct((bases * SPAN, CHUNK), jnp.bfloat16),
        ),
        in_specs=[VMEM, VMEM],
        out_specs=(VMEM, VMEM),
        compiler_params=grant(58),
        name="bands",
    )(row_taps, column_taps)


def swap_rims(top, bottom):
    count = lax.axis_size("tile")
    forward = [(i, i + 1) for i in range(count - 1)]
    backward = [(target, source) for source, target in forward]
    return lax.ppermute(bottom, "tile", forward), lax.ppermute(top, "tile", backward)


def clear(pass_ref, start):
    bases, height, _ = pass_ref.shape
    pass_ref[:, :, start : start + BLOCK] = jnp.zeros((bases, height, BLOCK), pass_ref.dtype)


def row_step(lanes, start, to, strips, coef_ref, rows_ref, pass_ref):
    bases = pass_ref.shape[0]
    for first_row, count, pieces in strips:
        window = [
            ref[first : first + size, pl.ds(pl.multiple_of(start + shift, BLOCK), lanes)]
            for ref, first, size, shift in pieces
        ]
        window = window[0] if len(window) == 1 else jnp.concatenate(window, axis=0)
        depth = window.shape[0]
        if count == BLOCK and depth == WINDOW:
            band = rows_ref[...]
        else:
            band = jnp.concatenate(
                [rows_ref[base * BLOCK : base * BLOCK + count, :depth] for base in range(bases)],
                axis=0,
            )
        summed = jnp.dot(band, window, preferred_element_type=jnp.float32)
        for base in range(bases):
            pass_ref[
                base, first_row : first_row + count, pl.ds(pl.multiple_of(to, BLOCK), lanes)
            ] = (coef_ref[0, base] * summed[base * count : (base + 1) * count]).astype(jnp.bfloat16)


def column_window(at, count, pass_ref):
    bases = pass_ref.shape[0]
    right = lax.broadcasted_iota(jnp.int32, (count, BLOCK), 1) < BLOCK // 2

    def columns(shift, size):
        return pl.ds(pl.multiple_of(at + shift, BLOCK), size)

    middle = [pass_ref[base, :count, columns(BLOCK, CHUNK)] for base in range(bases)]
    sides = [
        jnp.where(
            right,
            pass_ref[base, :count, columns(BLOCK + CHUNK, BLOCK)],
            pass_ref[base, :count, columns(0, BLOCK)],
        )
        for base in range(bases)
    ]
    return jnp.concatenate(middle + sides, axis=1)


def column_step(index, count, columns_ref, pass_ref):
    return [
        jnp.dot(
            column_window(index * WIDE + part * CHUNK, count, pass_ref),
            columns_ref[...],
            preferred_element_type=jnp.float32,
        )
        for part in range(WIDE // CHUNK)
    ]


def column_strip(count, columns_ref, pass_ref, consume):
    width = pass_ref.shape[2] - 2 * BLOCK
    chunks = width // CHUNK // 2
    for half in range(2):
        windows = [
            column_window((half * chunks + chunk) * CHUNK, count, pass_ref)
            for chunk in range(chunks)
        ]
        summed = jnp.dot(
            jnp.concatenate(windows, axis=0),
            columns_ref[...],
            preferred_element_type=jnp.float32,
        )
        for chunk in range(chunks):
            consume(
                pl.ds((half * chunks + chunk) * CHUNK, CHUNK),
                summed[chunk * count : (chunk + 1) * count],
            )


def my_device():
    return lax.axis_index("exp") * lax.axis_size("tile") + lax.axis_index("tile")


def wide_copy(source, target, sems, first_row, rows):
    def copy(index):
        at = pl.ds(pl.multiple_of(index * WIDE, WIDE), WIDE)
        return pltpu.make_async_copy(
            source.at[pl.ds(first_row, rows), at], target.at[:, at], sems.at[index]
        )

    return copy


def passes(fetch, step, consume, pass_ref, width, load=None):
    wides = width // WIDE

    def wide_step(index):
        fetch(index).wait()
        step(WIDE, index * WIDE, BLOCK + index * WIDE)

    clear(pass_ref, 0)
    clear(pass_ref, BLOCK + width)
    wide_step(0)
    wide_step(1)
    if load is not None:
        load.wait()

    @pl.loop(0, wides - 2)
    def _(index):
        consume(index)
        wide_step(index + 2)

    @pl.loop(wides - 2, wides)
    def _(index):
        consume(index)


def forward_kernel(
    ident_ref,
    weight_ref,
    coef_ref,
    above_ref,
    image_hbm,
    below_ref,
    rows_ref,
    columns_ref,
    bank_rows_ref,
    bank_columns_ref,
    out_hbm,
    image_ref,
    pass_ref,
    matched_ref,
    turned_ref,
    out_ref,
    warp_rows_ref,
    warp_columns_ref,
    fetch_sems,
    load_sems,
    store_sems,
):
    tile_rows, width = image_ref.shape
    parts = tile_rows // BLOCK
    across = width // BLOCK
    items = parts * across
    pitch = items + PAD
    myself = my_device()
    weight = weight_ref[lax.axis_index("exp"), lax.axis_index("tile")]
    fetch = wide_copy(image_hbm, image_ref, fetch_sems, 0, tile_rows)
    loads = [
        pltpu.make_async_copy(bank_rows_ref, warp_rows_ref, load_sems.at[0]),
        pltpu.make_async_copy(bank_columns_ref, warp_columns_ref, load_sems.at[1]),
    ]
    for index in range(width // WIDE):
        fetch(index).start()
    for load in loads:
        load.start()

    strips = [
        (0, BLOCK, [(above_ref, 0, RIM, 0), (image_ref, 0, BLOCK + RIM, 0)]),
        (BLOCK, BLOCK, [(image_ref, BLOCK - RIM, BLOCK + RIM, 0), (below_ref, 0, RIM, 0)]),
    ]
    step = functools.partial(
        row_step, strips=strips, coef_ref=coef_ref, rows_ref=rows_ref, pass_ref=pass_ref
    )

    def match_step(index):
        for inner, summed in enumerate(column_step(index, tile_rows, columns_ref, pass_ref)):
            matched_ref[:, pl.ds(pl.multiple_of(index * WIDE + inner * CHUNK, CHUNK), CHUNK)] = (
                summed.astype(jnp.bfloat16)
            )

    passes(fetch, step, match_step, pass_ref, width)
    for load in loads:
        load.wait()

    @pl.loop(0, across // 4)
    def _(quad):
        todo = []
        for part in range(parts):
            for inner in range(4):
                column = quad * 4 + inner
                ident = ident_ref[myself, part * across + column]
                piece = matched_ref[
                    part * BLOCK : (part + 1) * BLOCK,
                    pl.ds(pl.multiple_of(column * BLOCK, BLOCK), BLOCK),
                ]
                todo.append((part * across + column, ident, piece))
        todo = [
            (
                item,
                ident,
                jnp.dot(warp_rows_ref[ident], piece, preferred_element_type=jnp.float32).astype(
                    jnp.bfloat16
                ),
            )
            for item, ident, piece in todo
        ]
        todo = [
            (
                item,
                lax.dot_general(
                    first,
                    warp_columns_ref[ident],
                    (((1,), (1,)), ((), ())),
                    preferred_element_type=jnp.float32,
                ),
            )
            for item, ident, first in todo
        ]
        for item, second in todo:
            turned_ref[pl.ds(item, BLOCK, stride=pitch), :] = weight * second

    lines = out_ref.shape[0] // GROUPS

    def store(group):
        at = pl.ds(pl.multiple_of(group * lines, lines), lines)
        return pltpu.make_async_copy(out_ref.at[at], out_hbm.at[at], store_sems.at[group])

    for group in range(GROUPS):

        @pl.loop(group * BLOCK // GROUPS, (group + 1) * BLOCK // GROUPS, unroll=2)
        def _(row):
            to = pl.ds(pl.multiple_of(row * items, items), items)
            at = pl.ds(pl.multiple_of(row * pitch, PAD), items)
            out_ref[to, :] = turned_ref[at, :].astype(jnp.bfloat16)

        store(group).start()
    for group in range(GROUPS):
        store(group).wait()


def forward(
    ident, weight, coef, above, image, below, rows, columns, warp_rows, warp_columns
):
    tile_rows, width = image.shape
    bases = rows.shape[0] // BLOCK
    lines = tile_rows * width // BLOCK
    return pl.pallas_call(
        forward_kernel,
        out_shape=jax.ShapeDtypeStruct((lines, BLOCK), jnp.bfloat16),
        in_specs=[SMEM, SMEM, SMEM, VMEM, HBM, VMEM, VMEM, VMEM, HBM, HBM],
        out_specs=HBM,
        scratch_shapes=[
            pltpu.VMEM((tile_rows, width), jnp.bfloat16),
            pltpu.VMEM((bases, tile_rows, width + 2 * BLOCK), jnp.bfloat16),
            pltpu.VMEM((tile_rows, width), jnp.bfloat16),
            pltpu.VMEM((lines + BLOCK * PAD, BLOCK), jnp.float32),
            pltpu.VMEM((lines, BLOCK), jnp.bfloat16),
            pltpu.VMEM(warp_rows.shape, jnp.bfloat16),
            pltpu.VMEM(warp_columns.shape, jnp.bfloat16),
            pltpu.SemaphoreType.DMA((width // WIDE,)),
            pltpu.SemaphoreType.DMA((2,)),
            pltpu.SemaphoreType.DMA((GROUPS,)),
        ],
        compiler_params=grant(58),
        name="match_warp",
    )(ident, weight, coef, above, image, below, rows, columns, warp_rows, warp_columns)


def slots_kernel(slot_hbm, arrived_ref, scale_ref, template_ref, coadd_ref, wide_ref, *refs):
    del scale_ref
    items, _, sources = slot_hbm.shape
    sums, tables, sems = refs[:LANES], refs[LANES : LANES + items], refs[LANES + items]
    loads = [pltpu.make_async_copy(slot_hbm.at[k], tables[k], sems.at[k]) for k in range(items)]
    for load in loads:
        load.start()

    def at(source):
        return pl.ds(pl.multiple_of(source * items, items), items)

    @pl.loop(0, sources)
    def _(source):
        wide_ref[at(source), :] = arrived_ref[at(source), :].astype(jnp.float32)
        for sum_ref in sums:
            sum_ref[at(source), :] = jnp.zeros((items, BLOCK), jnp.float32)

    for load in loads:
        load.wait()

    @pl.loop(0, sources)
    def _(source):
        for first in range(0, items, LANES):
            slots = [tables[first + lane][0, source] for lane in range(LANES)]
            values = [
                sum_ref[pl.ds(slot, 1), :] + wide_ref[pl.ds(source * items + first + lane, 1), :]
                for lane, (slot, sum_ref) in enumerate(zip(slots, sums))
            ]
            for slot, sum_ref, value in zip(slots, sums, values):
                sum_ref[pl.ds(slot, 1), :] = value

    @pl.loop(0, sources)
    def _(source):
        value = sums[0][at(source), :]
        for sum_ref in sums[1:]:
            value = value + sum_ref[at(source), :]
        sums[0][at(source), :] = value
        coadd_ref[at(source), :] = value.astype(jnp.bfloat16)

    @pl.loop(0, sources)
    def _(source):
        for item in range(items):
            slot = tables[item][0, source]
            wide_ref[pl.ds(source * items + item, 1), :] = sums[0][pl.ds(slot, 1), :]

    @pl.loop(0, sources)
    def _(source):
        template_ref[at(source), :] = wide_ref[at(source), :].astype(jnp.bfloat16)


def slot_sums(slots, arrived, scale):
    shape = jax.ShapeDtypeStruct(arrived.shape, jnp.bfloat16)
    sources, items = slots.shape
    return pl.pallas_call(
        slots_kernel,
        out_shape=(shape, shape),
        in_specs=[ANY, VMEM, SMEM],
        out_specs=(VMEM, VMEM),
        scratch_shapes=[pltpu.VMEM(arrived.shape, jnp.float32)] * (1 + LANES)
        + [pltpu.SMEM((1, sources), jnp.int32)] * items
        + [pltpu.SemaphoreType.DMA((items,))],
        compiler_params=grant(44),
        name="slot_sums",
    )(slots.T.reshape(items, 1, sources), arrived, scale)


def unwarp_kernel(
    ident_ref,
    scale_ref,
    returned_ref,
    bank_rows_ref,
    bank_columns_ref,
    out_ref,
    top_ref,
    under_top_ref,
    over_bottom_ref,
    bottom_ref,
    wide_ref,
    warp_rows_ref,
    warp_columns_ref,
    sems,
):
    tile_rows, part_width = out_ref.shape
    across = part_width // BLOCK
    parts = tile_rows // BLOCK
    items = parts * across
    pitch = items + PAD
    myself = my_device()
    loads = [
        pltpu.make_async_copy(bank_rows_ref, warp_rows_ref, sems.at[0]),
        pltpu.make_async_copy(bank_columns_ref, warp_columns_ref, sems.at[1]),
    ]
    for load in loads:
        load.start()

    @pl.loop(0, BLOCK, unroll=4)
    def _(row):
        to = pl.ds(pl.multiple_of(row * pitch, PAD), items)
        at = pl.ds(pl.multiple_of(row * items, items), items)
        wide_ref[to, :] = returned_ref[at, :].astype(jnp.float32)

    for load in loads:
        load.wait()

    @pl.loop(0, across // 4)
    def _(quad):
        todo = []
        for part in range(parts):
            for inner in range(4):
                column = quad * 4 + inner
                item = part * across + column
                ident = ident_ref[myself, item]
                numerator = wide_ref[pl.ds(item, BLOCK, stride=pitch), :].astype(jnp.bfloat16)
                todo.append((part, column, item, ident, numerator))
        todo = [
            (
                part,
                column,
                ident,
                scale_ref[0, item]
                * lax.dot_general(
                    warp_rows_ref[ident],
                    numerator,
                    (((0,), (0,)), ((), ())),
                    preferred_element_type=jnp.float32,
                ),
            )
            for part, column, item, ident, numerator in todo
        ]
        for part, column, ident, first in todo:
            image = jnp.dot(
                first.astype(jnp.bfloat16),
                warp_columns_ref[ident],
                preferred_element_type=jnp.float32,
            ).astype(jnp.bfloat16)
            to = pl.ds(pl.multiple_of(column * BLOCK, BLOCK), BLOCK)
            out_ref[part * BLOCK : (part + 1) * BLOCK, to] = image
            if part == 0:
                top_ref[:, to] = image[:RIM]
                under_top_ref[:, to] = image[RIM : 2 * RIM]
            if part == parts - 1:
                over_bottom_ref[:, to] = image[BLOCK - 2 * RIM : BLOCK - RIM]
                bottom_ref[:, to] = image[BLOCK - RIM :]


def unwarp(ident, scale, returned, warp_rows, warp_columns, tile_rows):
    lines = returned.shape[0]
    part_width = lines * BLOCK // tile_rows
    rim = jax.ShapeDtypeStruct((RIM, part_width), jnp.bfloat16)
    return pl.pallas_call(
        unwarp_kernel,
        out_shape=(jax.ShapeDtypeStruct((tile_rows, part_width), jnp.bfloat16),) + (rim,) * 4,
        in_specs=[SMEM, SMEM, VMEM, ANY, ANY],
        out_specs=(VMEM,) * 5,
        scratch_shapes=[
            pltpu.VMEM((lines + BLOCK * PAD, BLOCK), jnp.float32),
            pltpu.VMEM(warp_rows.shape, jnp.bfloat16),
            pltpu.VMEM(warp_columns.shape, jnp.bfloat16),
            pltpu.SemaphoreType.DMA((2,)),
        ],
        compiler_params=grant(58),
        name="unwarp",
    )(ident, scale, returned, warp_rows, warp_columns)


def inner_strips(image_ref):
    tile_rows = image_ref.shape[0]
    return [
        (0, BLOCK, [(image_ref, 0, WINDOW, 0)]),
        (BLOCK, tile_rows - 2 * RIM - BLOCK, [(image_ref, BLOCK, tile_rows - BLOCK, 0)]),
    ]


def inner_kernel(
    coef_ref,
    image_hbm,
    exposure_hbm,
    rows_ref,
    columns_ref,
    out_ref,
    image_ref,
    exposure_ref,
    pass_ref,
    stage_ref,
    fetch_sems,
    load_sem,
    sems,
):
    tile_rows, width = image_ref.shape
    inner = tile_rows - 2 * RIM
    fetch = wide_copy(image_hbm, image_ref, fetch_sems, 0, tile_rows)
    load = pltpu.make_async_copy(exposure_hbm.at[pl.ds(RIM, inner)], exposure_ref, load_sem)
    for index in range(width // WIDE):
        fetch(index).start()
    load.start()
    step = functools.partial(
        row_step,
        strips=inner_strips(image_ref),
        coef_ref=coef_ref,
        rows_ref=rows_ref,
        pass_ref=pass_ref,
    )

    def store(index):
        at = pl.ds(pl.multiple_of(index * WIDE, WIDE), WIDE)
        return pltpu.make_async_copy(
            stage_ref.at[:, at], out_ref.at[pl.ds(RIM, inner), at], sems.at[index]
        )

    def subtract_step(index):
        for part, summed in enumerate(column_step(index, inner, columns_ref, pass_ref)):
            at = pl.ds(pl.multiple_of(index * WIDE + part * CHUNK, CHUNK), CHUNK)
            stage_ref[:, at] = exposure_ref[:, at].astype(jnp.float32) - summed
        store(index).start()

    passes(fetch, step, subtract_step, pass_ref, width, load)

    @pl.loop(0, width // WIDE)
    def _(index):
        store(index).wait()


def subtract_inner(coef, image, exposure, rows, columns):
    tile_rows, width = image.shape
    bases = rows.shape[0] // BLOCK
    inner = tile_rows - 2 * RIM
    return pl.pallas_call(
        inner_kernel,
        out_shape=jax.ShapeDtypeStruct((tile_rows, width), jnp.float32),
        in_specs=[SMEM, HBM, HBM, VMEM, VMEM],
        out_specs=HBM,
        scratch_shapes=[
            pltpu.VMEM((tile_rows, width), jnp.bfloat16),
            pltpu.VMEM((inner, width), jnp.bfloat16),
            pltpu.VMEM((bases, inner, width + 2 * BLOCK), jnp.bfloat16),
            pltpu.VMEM((inner, width), jnp.float32),
            pltpu.SemaphoreType.DMA((width // WIDE,)),
            pltpu.SemaphoreType.DMA,
            pltpu.SemaphoreType.DMA((width // WIDE,)),
        ],
        compiler_params=grant(58),
        name="subtract_inner",
    )(coef, image, exposure, rows, columns)


def outer_kernel(
    coef_ref,
    above_ref,
    top_ref,
    under_top_ref,
    over_bottom_ref,
    bottom_ref,
    below_ref,
    exposure_hbm,
    rows_ref,
    columns_ref,
    partial_hbm,
    out_hbm,
    order_ref,
    exposure_ref,
    pass_ref,
    stage_ref,
    fetch_sems,
    store_sems,
):
    del partial_hbm
    tile_rows, width = out_hbm.shape
    order_ref[...] = jnp.zeros_like(order_ref)

    def ends(index):
        first = index * (tile_rows - RIM)
        here, there = pl.ds(index * RIM, RIM), pl.ds(first, RIM)
        return (
            pltpu.make_async_copy(
                exposure_hbm.at[there], exposure_ref.at[here], fetch_sems.at[index]
            ),
            pltpu.make_async_copy(stage_ref.at[here], out_hbm.at[there], store_sems.at[index]),
        )

    fetches, stores = zip(*(ends(index) for index in range(2)))
    for fetch in fetches:
        fetch.start()
    strips = [
        (0, RIM, [(ref, 0, RIM, 0) for ref in (above_ref, top_ref, under_top_ref)]),
        (RIM, RIM, [(ref, 0, RIM, 0) for ref in (over_bottom_ref, bottom_ref, below_ref)]),
    ]
    clear(pass_ref, 0)
    clear(pass_ref, BLOCK + width)
    for index in range(width // WIDE):
        row_step(
            WIDE, index * WIDE, BLOCK + index * WIDE, strips, coef_ref, rows_ref, pass_ref
        )
    for fetch in fetches:
        fetch.wait()

    def subtract(at, summed):
        stage_ref[:, at] = exposure_ref[:, at].astype(jnp.float32) - summed

    column_strip(2 * RIM, columns_ref, pass_ref, subtract)
    for store in stores:
        store.start()
    for store in stores:
        store.wait()


def subtract_outer(coef, rims, exposure, rows, columns, partial):
    tile_rows, width = exposure.shape
    bases = rows.shape[0] // BLOCK
    operands = (coef, *rims, exposure, rows, columns, partial)
    return pl.pallas_call(
        outer_kernel,
        out_shape=(
            jax.ShapeDtypeStruct((tile_rows, width), jnp.float32),
            jax.ShapeDtypeStruct((SLOT_ROWS, BLOCK), jnp.float32),
        ),
        in_specs=[SMEM] + [VMEM] * len(rims) + [HBM, VMEM, VMEM, HBM],
        out_specs=(HBM, VMEM),
        scratch_shapes=[
            pltpu.VMEM((2 * RIM, width), jnp.bfloat16),
            pltpu.VMEM((bases, 2 * RIM, width + 2 * BLOCK), jnp.bfloat16),
            pltpu.VMEM((2 * RIM, width), jnp.float32),
            pltpu.SemaphoreType.DMA((2,)),
            pltpu.SemaphoreType.DMA((2,)),
        ],
        input_output_aliases={len(operands) - 1: 0},
        compiler_params=grant(16),
        name="subtract_outer",
    )(*operands)


def patch_kernel(scale_ref, owned_ref, order_ref, out_hbm, wide_ref, stage_ref, store_sems):
    del order_ref
    slots = SLOT_ROWS * SLOT_COLS
    pitch = slots + PAD
    myself = my_device()

    @pl.loop(0, BLOCK, unroll=4)
    def _(row):
        to = pl.ds(pl.multiple_of(row * pitch, PAD), slots)
        at = pl.ds(pl.multiple_of(row * slots, slots), slots)
        wide_ref[to, :] = owned_ref[at, :].astype(jnp.float32)

    def store(down):
        at = pl.ds(pl.multiple_of(down * BLOCK, BLOCK), BLOCK)
        return pltpu.make_async_copy(stage_ref.at[at], out_hbm.at[at], store_sems.at[down])

    @pl.loop(0, SLOT_ROWS)
    def _(down):
        to = pl.ds(pl.multiple_of(down * BLOCK, BLOCK), BLOCK)
        for across in range(SLOT_COLS):
            slot = down * SLOT_COLS + across
            stage_ref[to, across * BLOCK : (across + 1) * BLOCK] = (
                scale_ref[myself, slot] * wide_ref[pl.ds(slot, BLOCK, stride=pitch), :]
            )
        store(down).start()

    @pl.loop(0, SLOT_ROWS)
    def _(down):
        store(down).wait()


def patch(scale, owned, order):
    shape = (SLOT_ROWS * BLOCK, SLOT_COLS * BLOCK)
    return pl.pallas_call(
        patch_kernel,
        out_shape=jax.ShapeDtypeStruct(shape, jnp.float32),
        in_specs=[SMEM, VMEM, VMEM],
        out_specs=HBM,
        scratch_shapes=[
            pltpu.VMEM((owned.shape[0] + BLOCK * PAD, BLOCK), jnp.float32),
            pltpu.VMEM(shape, jnp.float32),
            pltpu.SemaphoreType.DMA((SLOT_ROWS,)),
        ],
        compiler_params=grant(12),
        name="patch",
    )(scale, owned, order)


def exchange(rows, devices):
    shaped = rows.reshape(devices, -1, BLOCK)
    moved = lax.all_to_all(shaped, ("exp", "tile"), split_axis=0, concat_axis=0, tiled=True)
    return moved.reshape(rows.shape)


def shards(
    exposure,
    row_taps,
    column_taps,
    basis_coef,
    warp_rows,
    warp_columns,
    warp_id,
    route_device,
    route_slot,
    weight,
):
    devices = lax.axis_size("exp") * lax.axis_size("tile")
    image = exposure[0]
    tile_rows, width = image.shape
    per_tile = tile_rows * width // (BLOCK * BLOCK)
    slot_count = SLOT_ROWS * SLOT_COLS
    ident = warp_id.reshape(devices, per_tile)

    above, below = swap_rims(image[:RIM], image[tile_rows - RIM :])
    rows, columns = band_matrices(row_taps, column_taps)
    weighted = forward(
        ident,
        weight,
        basis_coef,
        above,
        image,
        below,
        rows,
        columns,
        warp_rows,
        warp_columns,
    )
    arrived = exchange(weighted, devices)

    owner = route_device.reshape(-1)
    place = route_slot.reshape(-1)
    block_weight = jnp.repeat(weight.reshape(-1), per_tile)
    by_owner = jnp.where(
        owner[None, :] == jnp.arange(devices, dtype=jnp.int32)[:, None], block_weight[None, :], 0.0
    )
    by_place = (place[:, None] == jnp.arange(slot_count, dtype=jnp.int32)[None, :]).astype(
        jnp.float32
    )
    total = jnp.dot(by_owner, by_place, precision=lax.Precision.HIGHEST)
    scale = 1.0 / jnp.maximum(total, 1.0)
    slots = (route_device * slot_count + route_slot).reshape(devices, per_tile)
    my_slots = lax.dynamic_slice_in_dim(slots, my_device(), 1, 0)
    block_scale = scale.reshape(-1)[my_slots]

    template_rows, coadd_rows = slot_sums(slots, arrived, block_scale)
    returned = exchange(template_rows, devices)
    owned = exchange(coadd_rows, devices)

    template, top, under_top, over_bottom, bottom = unwarp(
        ident, block_scale, returned, warp_rows, warp_columns, tile_rows
    )
    above, below = swap_rims(top, bottom)
    difference = subtract_inner(basis_coef, template, image, rows, columns)
    rims = (above, top, under_top, over_bottom, bottom, below)
    difference, order = subtract_outer(basis_coef, rims, image, rows, columns, difference)
    return patch(scale, owned, order), difference[None]


def solution(mesh):
    placed = (P("exp", "tile", None), P(), P(), P("exp", None), P(), P(), P(), P(), P(), P())
    return jax.shard_map(
        shards,
        mesh=mesh,
        in_specs=placed,
        out_specs=(P("exp", "tile"), P("exp", "tile", None)),
        check_vma=False,
    )
```

```python
import functools

import jax
import jax.numpy as jnp
from jax import lax
from jax.experimental import pallas as pl
from jax.experimental.pallas import tpu as pltpu
from jax.sharding import PartitionSpec as P

BLOCK = 128
HALF = 10
RIM = 16
CHUNK = 256
WIDE = 1024
SPAN = CHUNK + BLOCK
WINDOW = BLOCK + 2 * RIM
SLOT_ROWS = 8
SLOT_COLS = 8
LANES = 8
PAD = 8
VMEM = pl.BlockSpec(memory_space=pltpu.VMEM)
SMEM = pl.BlockSpec(memory_space=pltpu.SMEM)
ANY = pl.BlockSpec(memory_space=pl.ANY)
HBM = pl.BlockSpec(memory_space=pltpu.HBM)
GROUPS = 4


def grant(mebibytes):
    return pltpu.CompilerParams(vmem_limit_bytes=int(mebibytes * 1024 * 1024))


def bands_kernel(row_taps_ref, column_taps_ref, rows_ref, columns_ref):
    bases, taps = row_taps_ref.shape
    lead = RIM - HALF

    def banded(taps_ref, offsets):
        values = taps_ref[...].astype(jnp.float32)
        bands = [jnp.zeros(offsets.shape, jnp.float32) for _ in range(bases)]
        for tap in range(taps):
            hit = offsets == tap
            for base in range(bases):
                value = jnp.broadcast_to(values[base : base + 1, tap : tap + 1], offsets.shape)
                bands[base] = jnp.where(hit, value, bands[base])
        return [band.astype(jnp.bfloat16) for band in bands]

    shape = (BLOCK, WINDOW)
    across = lax.broadcasted_iota(jnp.int32, shape, 1) - lax.broadcasted_iota(jnp.int32, shape, 0)
    for base, band in enumerate(banded(row_taps_ref, across - lead)):
        rows_ref[base * BLOCK : (base + 1) * BLOCK, :] = band
    shape = (WINDOW, BLOCK)
    down = lax.broadcasted_iota(jnp.int32, shape, 0) - lax.broadcasted_iota(jnp.int32, shape, 1)
    columns_ref[...] = jnp.zeros_like(columns_ref)
    for base, band in enumerate(banded(column_taps_ref, down - lead)):
        top = base * CHUNK
        columns_ref[top : top + WINDOW - RIM, :BLOCK] = band[RIM:]
        columns_ref[top + BLOCK - RIM : top + CHUNK, BLOCK:] = band[: WINDOW - RIM]
        top = bases * CHUNK + base * BLOCK
        columns_ref[top : top + RIM, BLOCK:] = band[WINDOW - RIM :]
        columns_ref[top + BLOCK - RIM : top + BLOCK, :BLOCK] = band[:RIM]


def band_matrices(row_taps, column_taps):
    bases = row_taps.shape[0]
    return pl.pallas_call(
        bands_kernel,
        out_shape=(
            jax.ShapeDtypeStruct((bases * BLOCK, WINDOW), jnp.bfloat16),
            jax.ShapeDtypeStruct((bases * SPAN, CHUNK), jnp.bfloat16),
        ),
        in_specs=[VMEM, VMEM],
        out_specs=(VMEM, VMEM),
        compiler_params=grant(58),
        name="bands",
    )(row_taps, column_taps)


def swap_rims(top, bottom):
    count = lax.axis_size("tile")
    forward = [(i, i + 1) for i in range(count - 1)]
    backward = [(target, source) for source, target in forward]
    return lax.ppermute(bottom, "tile", forward), lax.ppermute(top, "tile", backward)


def clear(pass_ref, start):
    bases, height, _ = pass_ref.shape
    pass_ref[:, :, start : start + BLOCK] = jnp.zeros((bases, height, BLOCK), pass_ref.dtype)


def row_step(lanes, start, to, strips, coef_ref, rows_ref, pass_ref):
    bases = pass_ref.shape[0]
    for first_row, count, pieces in strips:
        window = [
            ref[first : first + size, pl.ds(pl.multiple_of(start + shift, BLOCK), lanes)]
            for ref, first, size, shift in pieces
        ]
        window = window[0] if len(window) == 1 else jnp.concatenate(window, axis=0)
        depth = window.shape[0]
        if count == BLOCK and depth == WINDOW:
            band = rows_ref[...]
        else:
            band = jnp.concatenate(
                [rows_ref[base * BLOCK : base * BLOCK + count, :depth] for base in range(bases)],
                axis=0,
            )
        summed = jnp.dot(band, window, preferred_element_type=jnp.float32)
        for base in range(bases):
            pass_ref[
                base, first_row : first_row + count, pl.ds(pl.multiple_of(to, BLOCK), lanes)
            ] = (coef_ref[0, base] * summed[base * count : (base + 1) * count]).astype(jnp.bfloat16)


def column_window(at, count, pass_ref):
    bases = pass_ref.shape[0]
    right = lax.broadcasted_iota(jnp.int32, (count, BLOCK), 1) < BLOCK // 2

    def columns(shift, size):
        return pl.ds(pl.multiple_of(at + shift, BLOCK), size)

    middle = [pass_ref[base, :count, columns(BLOCK, CHUNK)] for base in range(bases)]
    sides = [
        jnp.where(
            right,
            pass_ref[base, :count, columns(BLOCK + CHUNK, BLOCK)],
            pass_ref[base, :count, columns(0, BLOCK)],
        )
        for base in range(bases)
    ]
    return jnp.concatenate(middle + sides, axis=1)


def column_step(index, count, columns_ref, pass_ref):
    return [
        jnp.dot(
            column_window(index * WIDE + part * CHUNK, count, pass_ref),
            columns_ref[...],
            preferred_element_type=jnp.float32,
        )
        for part in range(WIDE // CHUNK)
    ]


def column_strip(count, columns_ref, pass_ref, consume):
    width = pass_ref.shape[2] - 2 * BLOCK
    chunks = width // CHUNK // 2
    for half in range(2):
        windows = [
            column_window((half * chunks + chunk) * CHUNK, count, pass_ref)
            for chunk in range(chunks)
        ]
        summed = jnp.dot(
            jnp.concatenate(windows, axis=0),
            columns_ref[...],
            preferred_element_type=jnp.float32,
        )
        for chunk in range(chunks):
            consume(
                pl.ds((half * chunks + chunk) * CHUNK, CHUNK),
                summed[chunk * count : (chunk + 1) * count],
            )


def my_device():
    return lax.axis_index("exp") * lax.axis_size("tile") + lax.axis_index("tile")


def wide_copy(source, target, sems, first_row, rows):
    def copy(index):
        at = pl.ds(pl.multiple_of(index * WIDE, WIDE), WIDE)
        return pltpu.make_async_copy(
            source.at[pl.ds(first_row, rows), at], target.at[:, at], sems.at[index]
        )

    return copy


def passes(fetch, step, consume, pass_ref, width, load=None):
    wides = width // WIDE

    def wide_step(index):
        fetch(index).wait()
        step(WIDE, index * WIDE, BLOCK + index * WIDE)

    clear(pass_ref, 0)
    clear(pass_ref, BLOCK + width)
    wide_step(0)
    wide_step(1)
    if load is not None:
        load.wait()

    @pl.loop(0, wides - 2)
    def _(index):
        consume(index)
        wide_step(index + 2)

    @pl.loop(wides - 2, wides)
    def _(index):
        consume(index)


def forward_kernel(
    ident_ref,
    weight_ref,
    coef_ref,
    above_ref,
    image_hbm,
    below_ref,
    rows_ref,
    columns_ref,
    bank_rows_ref,
    bank_columns_ref,
    out_hbm,
    image_ref,
    pass_ref,
    matched_ref,
    turned_ref,
    out_ref,
    warp_rows_ref,
    warp_columns_ref,
    fetch_sems,
    load_sems,
    store_sems,
):
    tile_rows, width = image_ref.shape
    parts = tile_rows // BLOCK
    across = width // BLOCK
    items = parts * across
    pitch = items + PAD
    myself = my_device()
    weight = weight_ref[lax.axis_index("exp"), lax.axis_index("tile")]
    fetch = wide_copy(image_hbm, image_ref, fetch_sems, 0, tile_rows)
    loads = [
        pltpu.make_async_copy(bank_rows_ref, warp_rows_ref, load_sems.at[0]),
        pltpu.make_async_copy(bank_columns_ref, warp_columns_ref, load_sems.at[1]),
    ]
    for index in range(width // WIDE):
        fetch(index).start()
    for load in loads:
        load.start()

    strips = [
        (0, BLOCK, [(above_ref, 0, RIM, 0), (image_ref, 0, BLOCK + RIM, 0)]),
        (BLOCK, BLOCK, [(image_ref, BLOCK - RIM, BLOCK + RIM, 0), (below_ref, 0, RIM, 0)]),
    ]
    step = functools.partial(
        row_step, strips=strips, coef_ref=coef_ref, rows_ref=rows_ref, pass_ref=pass_ref
    )

    def match_step(index):
        for inner, summed in enumerate(column_step(index, tile_rows, columns_ref, pass_ref)):
            matched_ref[:, pl.ds(pl.multiple_of(index * WIDE + inner * CHUNK, CHUNK), CHUNK)] = (
                summed.astype(jnp.bfloat16)
            )

    passes(fetch, step, match_step, pass_ref, width)
    for load in loads:
        load.wait()

    @pl.loop(0, across // 4)
    def _(quad):
        todo = []
        for part in range(parts):
            for inner in range(4):
                column = quad * 4 + inner
                ident = ident_ref[myself, part * across + column]
                piece = matched_ref[
                    part * BLOCK : (part + 1) * BLOCK,
                    pl.ds(pl.multiple_of(column * BLOCK, BLOCK), BLOCK),
                ]
                todo.append((part * across + column, ident, piece))
        todo = [
            (
                item,
                ident,
                jnp.dot(warp_rows_ref[ident], piece, preferred_element_type=jnp.float32).astype(
                    jnp.bfloat16
                ),
            )
            for item, ident, piece in todo
        ]
        todo = [
            (
                item,
                lax.dot_general(
                    first,
                    warp_columns_ref[ident],
                    (((1,), (1,)), ((), ())),
                    preferred_element_type=jnp.float32,
                ),
            )
            for item, ident, first in todo
        ]
        for item, second in todo:
            turned_ref[pl.ds(item, BLOCK, stride=pitch), :] = weight * second

    lines = out_ref.shape[0] // GROUPS

    def store(group):
        at = pl.ds(pl.multiple_of(group * lines, lines), lines)
        return pltpu.make_async_copy(out_ref.at[at], out_hbm.at[at], store_sems.at[group])

    for group in range(GROUPS):

        @pl.loop(group * BLOCK // GROUPS, (group + 1) * BLOCK // GROUPS, unroll=2)
        def _(row):
            to = pl.ds(pl.multiple_of(row * items, items), items)
            at = pl.ds(pl.multiple_of(row * pitch, PAD), items)
            out_ref[to, :] = turned_ref[at, :].astype(jnp.bfloat16)

        store(group).start()
    for group in range(GROUPS):
        store(group).wait()


def forward(
    ident, weight, coef, above, image, below, rows, columns, warp_rows, warp_columns
):
    tile_rows, width = image.shape
    bases = rows.shape[0] // BLOCK
    lines = tile_rows * width // BLOCK
    return pl.pallas_call(
        forward_kernel,
        out_shape=jax.ShapeDtypeStruct((lines, BLOCK), jnp.bfloat16),
        in_specs=[SMEM, SMEM, SMEM, VMEM, HBM, VMEM, VMEM, VMEM, HBM, HBM],
        out_specs=HBM,
        scratch_shapes=[
            pltpu.VMEM((tile_rows, width), jnp.bfloat16),
            pltpu.VMEM((bases, tile_rows, width + 2 * BLOCK), jnp.bfloat16),
            pltpu.VMEM((tile_rows, width), jnp.bfloat16),
            pltpu.VMEM((lines + BLOCK * PAD, BLOCK), jnp.float32),
            pltpu.VMEM((lines, BLOCK), jnp.bfloat16),
            pltpu.VMEM(warp_rows.shape, jnp.bfloat16),
            pltpu.VMEM(warp_columns.shape, jnp.bfloat16),
            pltpu.SemaphoreType.DMA((width // WIDE,)),
            pltpu.SemaphoreType.DMA((2,)),
            pltpu.SemaphoreType.DMA((GROUPS,)),
        ],
        compiler_params=grant(58),
        name="match_warp",
    )(ident, weight, coef, above, image, below, rows, columns, warp_rows, warp_columns)


def slots_kernel(slot_hbm, arrived_ref, scale_ref, template_ref, coadd_ref, wide_ref, *refs):
    del scale_ref
    items, _, sources = slot_hbm.shape
    sums, tables, sems = refs[:LANES], refs[LANES : LANES + items], refs[LANES + items]
    loads = [pltpu.make_async_copy(slot_hbm.at[k], tables[k], sems.at[k]) for k in range(items)]
    for load in loads:
        load.start()

    def at(source):
        return pl.ds(pl.multiple_of(source * items, items), items)

    @pl.loop(0, sources)
    def _(source):
        wide_ref[at(source), :] = arrived_ref[at(source), :].astype(jnp.float32)
        for sum_ref in sums:
            sum_ref[at(source), :] = jnp.zeros((items, BLOCK), jnp.float32)

    for load in loads:
        load.wait()

    @pl.loop(0, sources)
    def _(source):
        for first in range(0, items, LANES):
            slots = [tables[first + lane][0, source] for lane in range(LANES)]
            values = [
                sum_ref[pl.ds(slot, 1), :] + wide_ref[pl.ds(source * items + first + lane, 1), :]
                for lane, (slot, sum_ref) in enumerate(zip(slots, sums))
            ]
            for slot, sum_ref, value in zip(slots, sums, values):
                sum_ref[pl.ds(slot, 1), :] = value

    @pl.loop(0, sources, unroll=2)
    def _(source):
        value = sums[0][at(source), :]
        for sum_ref in sums[1:]:
            value = value + sum_ref[at(source), :]
        sums[0][at(source), :] = value
        coadd_ref[at(source), :] = value.astype(jnp.bfloat16)

    @pl.loop(0, sources)
    def _(source):
        for item in range(items):
            slot = tables[item][0, source]
            wide_ref[pl.ds(source * items + item, 1), :] = sums[0][pl.ds(slot, 1), :]

    @pl.loop(0, sources, unroll=4)
    def _(source):
        template_ref[at(source), :] = wide_ref[at(source), :].astype(jnp.bfloat16)


def slot_sums(slots, arrived, scale):
    shape = jax.ShapeDtypeStruct(arrived.shape, jnp.bfloat16)
    sources, items = slots.shape
    return pl.pallas_call(
        slots_kernel,
        out_shape=(shape, shape),
        in_specs=[ANY, VMEM, SMEM],
        out_specs=(VMEM, VMEM),
        scratch_shapes=[pltpu.VMEM(arrived.shape, jnp.float32)] * (1 + LANES)
        + [pltpu.SMEM((1, sources), jnp.int32)] * items
        + [pltpu.SemaphoreType.DMA((items,))],
        compiler_params=grant(44),
        name="slot_sums",
    )(slots.T.reshape(items, 1, sources), arrived, scale)


def unwarp_kernel(
    ident_ref,
    scale_ref,
    returned_ref,
    bank_rows_ref,
    bank_columns_ref,
    out_ref,
    top_ref,
    under_top_ref,
    over_bottom_ref,
    bottom_ref,
    wide_ref,
    warp_rows_ref,
    warp_columns_ref,
    sems,
):
    tile_rows, part_width = out_ref.shape
    across = part_width // BLOCK
    parts = tile_rows // BLOCK
    items = parts * across
    pitch = items + PAD
    myself = my_device()
    loads = [
        pltpu.make_async_copy(bank_rows_ref, warp_rows_ref, sems.at[0]),
        pltpu.make_async_copy(bank_columns_ref, warp_columns_ref, sems.at[1]),
    ]
    for load in loads:
        load.start()

    @pl.loop(0, BLOCK, unroll=4)
    def _(row):
        to = pl.ds(pl.multiple_of(row * pitch, PAD), items)
        at = pl.ds(pl.multiple_of(row * items, items), items)
        wide_ref[to, :] = returned_ref[at, :].astype(jnp.float32)

    for load in loads:
        load.wait()

    @pl.loop(0, across // 4)
    def _(quad):
        todo = []
        for part in range(parts):
            for inner in range(4):
                column = quad * 4 + inner
                item = part * across + column
                ident = ident_ref[myself, item]
                numerator = wide_ref[pl.ds(item, BLOCK, stride=pitch), :].astype(jnp.bfloat16)
                todo.append((part, column, item, ident, numerator))
        todo = [
            (
                part,
                column,
                ident,
                scale_ref[0, item]
                * lax.dot_general(
                    warp_rows_ref[ident],
                    numerator,
                    (((0,), (0,)), ((), ())),
                    preferred_element_type=jnp.float32,
                ),
            )
            for part, column, item, ident, numerator in todo
        ]
        for part, column, ident, first in todo:
            image = jnp.dot(
                first.astype(jnp.bfloat16),
                warp_columns_ref[ident],
                preferred_element_type=jnp.float32,
            ).astype(jnp.bfloat16)
            to = pl.ds(pl.multiple_of(column * BLOCK, BLOCK), BLOCK)
            out_ref[part * BLOCK : (part + 1) * BLOCK, to] = image
            if part == 0:
                top_ref[:, to] = image[:RIM]
                under_top_ref[:, to] = image[RIM : 2 * RIM]
            if part == parts - 1:
                over_bottom_ref[:, to] = image[BLOCK - 2 * RIM : BLOCK - RIM]
                bottom_ref[:, to] = image[BLOCK - RIM :]


def unwarp(ident, scale, returned, warp_rows, warp_columns, tile_rows):
    lines = returned.shape[0]
    part_width = lines * BLOCK // tile_rows
    rim = jax.ShapeDtypeStruct((RIM, part_width), jnp.bfloat16)
    return pl.pallas_call(
        unwarp_kernel,
        out_shape=(jax.ShapeDtypeStruct((tile_rows, part_width), jnp.bfloat16),) + (rim,) * 4,
        in_specs=[SMEM, SMEM, VMEM, ANY, ANY],
        out_specs=(VMEM,) * 5,
        scratch_shapes=[
            pltpu.VMEM((lines + BLOCK * PAD, BLOCK), jnp.float32),
            pltpu.VMEM(warp_rows.shape, jnp.bfloat16),
            pltpu.VMEM(warp_columns.shape, jnp.bfloat16),
            pltpu.SemaphoreType.DMA((2,)),
        ],
        compiler_params=grant(58),
        name="unwarp",
    )(ident, scale, returned, warp_rows, warp_columns)


def inner_strips(image_ref):
    tile_rows = image_ref.shape[0]
    return [
        (0, BLOCK, [(image_ref, 0, WINDOW, 0)]),
        (BLOCK, tile_rows - 2 * RIM - BLOCK, [(image_ref, BLOCK, tile_rows - BLOCK, 0)]),
    ]


def inner_kernel(
    coef_ref,
    image_hbm,
    exposure_hbm,
    rows_ref,
    columns_ref,
    out_ref,
    image_ref,
    exposure_ref,
    pass_ref,
    stage_ref,
    fetch_sems,
    load_sem,
    sems,
):
    tile_rows, width = image_ref.shape
    inner = tile_rows - 2 * RIM
    fetch = wide_copy(image_hbm, image_ref, fetch_sems, 0, tile_rows)
    load = pltpu.make_async_copy(exposure_hbm.at[pl.ds(RIM, inner)], exposure_ref, load_sem)
    for index in range(width // WIDE):
        fetch(index).start()
    load.start()
    step = functools.partial(
        row_step,
        strips=inner_strips(image_ref),
        coef_ref=coef_ref,
        rows_ref=rows_ref,
        pass_ref=pass_ref,
    )

    def store(index):
        at = pl.ds(pl.multiple_of(index * WIDE, WIDE), WIDE)
        return pltpu.make_async_copy(
            stage_ref.at[:, at], out_ref.at[pl.ds(RIM, inner), at], sems.at[index]
        )

    def subtract_step(index):
        for part, summed in enumerate(column_step(index, inner, columns_ref, pass_ref)):
            at = pl.ds(pl.multiple_of(index * WIDE + part * CHUNK, CHUNK), CHUNK)
            stage_ref[:, at] = exposure_ref[:, at].astype(jnp.float32) - summed
        store(index).start()

    passes(fetch, step, subtract_step, pass_ref, width, load)

    @pl.loop(0, width // WIDE)
    def _(index):
        store(index).wait()


def subtract_inner(coef, image, exposure, rows, columns):
    tile_rows, width = image.shape
    bases = rows.shape[0] // BLOCK
    inner = tile_rows - 2 * RIM
    return pl.pallas_call(
        inner_kernel,
        out_shape=jax.ShapeDtypeStruct((tile_rows, width), jnp.float32),
        in_specs=[SMEM, HBM, HBM, VMEM, VMEM],
        out_specs=HBM,
        scratch_shapes=[
            pltpu.VMEM((tile_rows, width), jnp.bfloat16),
            pltpu.VMEM((inner, width), jnp.bfloat16),
            pltpu.VMEM((bases, inner, width + 2 * BLOCK), jnp.bfloat16),
            pltpu.VMEM((inner, width), jnp.float32),
            pltpu.SemaphoreType.DMA((width // WIDE,)),
            pltpu.SemaphoreType.DMA,
            pltpu.SemaphoreType.DMA((width // WIDE,)),
        ],
        compiler_params=grant(58),
        name="subtract_inner",
    )(coef, image, exposure, rows, columns)


def outer_kernel(
    coef_ref,
    above_ref,
    top_ref,
    under_top_ref,
    over_bottom_ref,
    bottom_ref,
    below_ref,
    exposure_hbm,
    rows_ref,
    columns_ref,
    partial_hbm,
    out_hbm,
    order_ref,
    exposure_ref,
    pass_ref,
    stage_ref,
    fetch_sems,
    store_sems,
):
    del partial_hbm
    tile_rows, width = out_hbm.shape
    order_ref[...] = jnp.zeros_like(order_ref)

    def ends(index):
        first = index * (tile_rows - RIM)
        here, there = pl.ds(index * RIM, RIM), pl.ds(first, RIM)
        return (
            pltpu.make_async_copy(
                exposure_hbm.at[there], exposure_ref.at[here], fetch_sems.at[index]
            ),
            pltpu.make_async_copy(stage_ref.at[here], out_hbm.at[there], store_sems.at[index]),
        )

    fetches, stores = zip(*(ends(index) for index in range(2)))
    for fetch in fetches:
        fetch.start()
    strips = [
        (0, RIM, [(ref, 0, RIM, 0) for ref in (above_ref, top_ref, under_top_ref)]),
        (RIM, RIM, [(ref, 0, RIM, 0) for ref in (over_bottom_ref, bottom_ref, below_ref)]),
    ]
    clear(pass_ref, 0)
    clear(pass_ref, BLOCK + width)
    for index in range(width // WIDE):
        row_step(
            WIDE, index * WIDE, BLOCK + index * WIDE, strips, coef_ref, rows_ref, pass_ref
        )
    for fetch in fetches:
        fetch.wait()

    def subtract(at, summed):
        stage_ref[:, at] = exposure_ref[:, at].astype(jnp.float32) - summed

    column_strip(2 * RIM, columns_ref, pass_ref, subtract)
    for store in stores:
        store.start()
    for store in stores:
        store.wait()


def subtract_outer(coef, rims, exposure, rows, columns, partial):
    tile_rows, width = exposure.shape
    bases = rows.shape[0] // BLOCK
    operands = (coef, *rims, exposure, rows, columns, partial)
    return pl.pallas_call(
        outer_kernel,
        out_shape=(
            jax.ShapeDtypeStruct((tile_rows, width), jnp.float32),
            jax.ShapeDtypeStruct((SLOT_ROWS, BLOCK), jnp.float32),
        ),
        in_specs=[SMEM] + [VMEM] * len(rims) + [HBM, VMEM, VMEM, HBM],
        out_specs=(HBM, VMEM),
        scratch_shapes=[
            pltpu.VMEM((2 * RIM, width), jnp.bfloat16),
            pltpu.VMEM((bases, 2 * RIM, width + 2 * BLOCK), jnp.bfloat16),
            pltpu.VMEM((2 * RIM, width), jnp.float32),
            pltpu.SemaphoreType.DMA((2,)),
            pltpu.SemaphoreType.DMA((2,)),
        ],
        input_output_aliases={len(operands) - 1: 0},
        compiler_params=grant(16),
        name="subtract_outer",
    )(*operands)


def patch_kernel(scale_ref, owned_ref, order_ref, out_hbm, wide_ref, stage_ref, store_sems):
    del order_ref
    slots = SLOT_ROWS * SLOT_COLS
    pitch = slots + PAD
    myself = my_device()

    @pl.loop(0, BLOCK, unroll=4)
    def _(row):
        to = pl.ds(pl.multiple_of(row * pitch, PAD), slots)
        at = pl.ds(pl.multiple_of(row * slots, slots), slots)
        wide_ref[to, :] = owned_ref[at, :].astype(jnp.float32)

    def store(down):
        at = pl.ds(pl.multiple_of(down * BLOCK, BLOCK), BLOCK)
        return pltpu.make_async_copy(stage_ref.at[at], out_hbm.at[at], store_sems.at[down])

    @pl.loop(0, SLOT_ROWS)
    def _(down):
        to = pl.ds(pl.multiple_of(down * BLOCK, BLOCK), BLOCK)
        for across in range(SLOT_COLS):
            slot = down * SLOT_COLS + across
            stage_ref[to, across * BLOCK : (across + 1) * BLOCK] = (
                scale_ref[myself, slot] * wide_ref[pl.ds(slot, BLOCK, stride=pitch), :]
            )
        store(down).start()

    @pl.loop(0, SLOT_ROWS)
    def _(down):
        store(down).wait()


def patch(scale, owned, order):
    shape = (SLOT_ROWS * BLOCK, SLOT_COLS * BLOCK)
    return pl.pallas_call(
        patch_kernel,
        out_shape=jax.ShapeDtypeStruct(shape, jnp.float32),
        in_specs=[SMEM, VMEM, VMEM],
        out_specs=HBM,
        scratch_shapes=[
            pltpu.VMEM((owned.shape[0] + BLOCK * PAD, BLOCK), jnp.float32),
            pltpu.VMEM(shape, jnp.float32),
            pltpu.SemaphoreType.DMA((SLOT_ROWS,)),
        ],
        compiler_params=grant(12),
        name="patch",
    )(scale, owned, order)


def exchange(rows, devices):
    shaped = rows.reshape(devices, -1, BLOCK)
    moved = lax.all_to_all(shaped, ("exp", "tile"), split_axis=0, concat_axis=0, tiled=True)
    return moved.reshape(rows.shape)


def shards(
    exposure,
    row_taps,
    column_taps,
    basis_coef,
    warp_rows,
    warp_columns,
    warp_id,
    route_device,
    route_slot,
    weight,
):
    devices = lax.axis_size("exp") * lax.axis_size("tile")
    image = exposure[0]
    tile_rows, width = image.shape
    per_tile = tile_rows * width // (BLOCK * BLOCK)
    slot_count = SLOT_ROWS * SLOT_COLS
    ident = warp_id.reshape(devices, per_tile)

    above, below = swap_rims(image[:RIM], image[tile_rows - RIM :])
    rows, columns = band_matrices(row_taps, column_taps)
    weighted = forward(
        ident,
        weight,
        basis_coef,
        above,
        image,
        below,
        rows,
        columns,
        warp_rows,
        warp_columns,
    )
    arrived = exchange(weighted, devices)

    owner = route_device.reshape(-1)
    place = route_slot.reshape(-1)
    block_weight = jnp.repeat(weight.reshape(-1), per_tile)
    by_owner = jnp.where(
        owner[None, :] == jnp.arange(devices, dtype=jnp.int32)[:, None], block_weight[None, :], 0.0
    )
    by_place = (place[:, None] == jnp.arange(slot_count, dtype=jnp.int32)[None, :]).astype(
        jnp.float32
    )
    total = jnp.dot(by_owner, by_place, precision=lax.Precision.HIGHEST)
    scale = 1.0 / jnp.maximum(total, 1.0)
    slots = (route_device * slot_count + route_slot).reshape(devices, per_tile)
    my_slots = lax.dynamic_slice_in_dim(slots, my_device(), 1, 0)
    block_scale = scale.reshape(-1)[my_slots]

    template_rows, coadd_rows = slot_sums(slots, arrived, block_scale)
    returned = exchange(template_rows, devices)
    owned = exchange(coadd_rows, devices)

    template, top, under_top, over_bottom, bottom = unwarp(
        ident, block_scale, returned, warp_rows, warp_columns, tile_rows
    )
    above, below = swap_rims(top, bottom)
    difference = subtract_inner(basis_coef, template, image, rows, columns)
    rims = (above, top, under_top, over_bottom, bottom, below)
    difference, order = subtract_outer(basis_coef, rims, image, rows, columns, difference)
    return patch(scale, owned, order), difference[None]


def solution(mesh):
    placed = (P("exp", "tile", None), P(), P(), P("exp", None), P(), P(), P(), P(), P(), P())
    return jax.shard_map(
        shards,
        mesh=mesh,
        in_specs=placed,
        out_specs=(P("exp", "tile"), P("exp", "tile", None)),
        check_vma=False,
    )
```

```python
import functools

import jax
import jax.numpy as jnp
from jax import lax
from jax.experimental import pallas as pl
from jax.experimental.pallas import tpu as pltpu
from jax.sharding import PartitionSpec as P

BLOCK = 128
HALF = 10
RIM = 16
CHUNK = 256
WIDE = 1024
SPAN = CHUNK + BLOCK
WINDOW = BLOCK + 2 * RIM
SLOT_ROWS = 8
SLOT_COLS = 8
LANES = 8
SUMS = 2
PAD = 8
VMEM = pl.BlockSpec(memory_space=pltpu.VMEM)
SMEM = pl.BlockSpec(memory_space=pltpu.SMEM)
ANY = pl.BlockSpec(memory_space=pl.ANY)
HBM = pl.BlockSpec(memory_space=pltpu.HBM)
GROUPS = 4


def grant(mebibytes):
    return pltpu.CompilerParams(vmem_limit_bytes=int(mebibytes * 1024 * 1024))


def bands_kernel(row_taps_ref, column_taps_ref, rows_ref, columns_ref):
    bases, taps = row_taps_ref.shape
    lead = RIM - HALF

    def banded(taps_ref, offsets):
        values = taps_ref[...].astype(jnp.float32)
        bands = [jnp.zeros(offsets.shape, jnp.float32) for _ in range(bases)]
        for tap in range(taps):
            hit = offsets == tap
            for base in range(bases):
                value = jnp.broadcast_to(values[base : base + 1, tap : tap + 1], offsets.shape)
                bands[base] = jnp.where(hit, value, bands[base])
        return [band.astype(jnp.bfloat16) for band in bands]

    shape = (BLOCK, WINDOW)
    across = lax.broadcasted_iota(jnp.int32, shape, 1) - lax.broadcasted_iota(jnp.int32, shape, 0)
    for base, band in enumerate(banded(row_taps_ref, across - lead)):
        rows_ref[base * BLOCK : (base + 1) * BLOCK, :] = band
    shape = (WINDOW, BLOCK)
    down = lax.broadcasted_iota(jnp.int32, shape, 0) - lax.broadcasted_iota(jnp.int32, shape, 1)
    columns_ref[...] = jnp.zeros_like(columns_ref)
    for base, band in enumerate(banded(column_taps_ref, down - lead)):
        top = base * CHUNK
        columns_ref[top : top + WINDOW - RIM, :BLOCK] = band[RIM:]
        columns_ref[top + BLOCK - RIM : top + CHUNK, BLOCK:] = band[: WINDOW - RIM]
        top = bases * CHUNK + base * BLOCK
        columns_ref[top : top + RIM, BLOCK:] = band[WINDOW - RIM :]
        columns_ref[top + BLOCK - RIM : top + BLOCK, :BLOCK] = band[:RIM]


def band_matrices(row_taps, column_taps):
    bases = row_taps.shape[0]
    return pl.pallas_call(
        bands_kernel,
        out_shape=(
            jax.ShapeDtypeStruct((bases * BLOCK, WINDOW), jnp.bfloat16),
            jax.ShapeDtypeStruct((bases * SPAN, CHUNK), jnp.bfloat16),
        ),
        in_specs=[VMEM, VMEM],
        out_specs=(VMEM, VMEM),
        compiler_params=grant(58),
        name="bands",
    )(row_taps, column_taps)


def swap_rims(top, bottom):
    count = lax.axis_size("tile")
    forward = [(i, i + 1) for i in range(count - 1)]
    backward = [(target, source) for source, target in forward]
    return lax.ppermute(bottom, "tile", forward), lax.ppermute(top, "tile", backward)


def clear(pass_ref, start):
    bases, height, _ = pass_ref.shape
    pass_ref[:, :, start : start + BLOCK] = jnp.zeros((bases, height, BLOCK), pass_ref.dtype)


def row_step(lanes, start, to, strips, coef_ref, rows_ref, pass_ref):
    bases = pass_ref.shape[0]
    for first_row, count, pieces in strips:
        window = [
            ref[first : first + size, pl.ds(pl.multiple_of(start + shift, BLOCK), lanes)]
            for ref, first, size, shift in pieces
        ]
        window = window[0] if len(window) == 1 else jnp.concatenate(window, axis=0)
        depth = window.shape[0]
        if count == BLOCK and depth == WINDOW:
            band = rows_ref[...]
        else:
            band = jnp.concatenate(
                [rows_ref[base * BLOCK : base * BLOCK + count, :depth] for base in range(bases)],
                axis=0,
            )
        summed = jnp.dot(band, window, preferred_element_type=jnp.float32)
        for base in range(bases):
            pass_ref[
                base, first_row : first_row + count, pl.ds(pl.multiple_of(to, BLOCK), lanes)
            ] = (coef_ref[0, base] * summed[base * count : (base + 1) * count]).astype(jnp.bfloat16)


def column_window(at, count, pass_ref):
    bases = pass_ref.shape[0]
    right = lax.broadcasted_iota(jnp.int32, (count, BLOCK), 1) < BLOCK // 2

    def columns(shift, size):
        return pl.ds(pl.multiple_of(at + shift, BLOCK), size)

    middle = [pass_ref[base, :count, columns(BLOCK, CHUNK)] for base in range(bases)]
    sides = [
        jnp.where(
            right,
            pass_ref[base, :count, columns(BLOCK + CHUNK, BLOCK)],
            pass_ref[base, :count, columns(0, BLOCK)],
        )
        for base in range(bases)
    ]
    return jnp.concatenate(middle + sides, axis=1)


def column_step(index, count, columns_ref, pass_ref):
    return [
        jnp.dot(
            column_window(index * WIDE + part * CHUNK, count, pass_ref),
            columns_ref[...],
            preferred_element_type=jnp.float32,
        )
        for part in range(WIDE // CHUNK)
    ]


def column_strip(count, columns_ref, pass_ref, consume):
    width = pass_ref.shape[2] - 2 * BLOCK
    chunks = width // CHUNK // 2
    for half in range(2):
        windows = [
            column_window((half * chunks + chunk) * CHUNK, count, pass_ref)
            for chunk in range(chunks)
        ]
        summed = jnp.dot(
            jnp.concatenate(windows, axis=0),
            columns_ref[...],
            preferred_element_type=jnp.float32,
        )
        for chunk in range(chunks):
            consume(
                pl.ds((half * chunks + chunk) * CHUNK, CHUNK),
                summed[chunk * count : (chunk + 1) * count],
            )


def my_device():
    return lax.axis_index("exp") * lax.axis_size("tile") + lax.axis_index("tile")


def wide_copy(source, target, sems, first_row, rows):
    def copy(index):
        at = pl.ds(pl.multiple_of(index * WIDE, WIDE), WIDE)
        return pltpu.make_async_copy(
            source.at[pl.ds(first_row, rows), at], target.at[:, at], sems.at[index]
        )

    return copy


def passes(fetch, step, consume, pass_ref, width, load=None):
    wides = width // WIDE

    def wide_step(index):
        fetch(index).wait()
        step(WIDE, index * WIDE, BLOCK + index * WIDE)

    clear(pass_ref, 0)
    clear(pass_ref, BLOCK + width)
    wide_step(0)
    wide_step(1)
    if load is not None:
        load.wait()

    @pl.loop(0, wides - 2)
    def _(index):
        consume(index)
        wide_step(index + 2)

    @pl.loop(wides - 2, wides)
    def _(index):
        consume(index)


def forward_kernel(
    ident_ref,
    weight_ref,
    coef_ref,
    above_ref,
    image_hbm,
    below_ref,
    rows_ref,
    columns_ref,
    bank_rows_ref,
    bank_columns_ref,
    out_hbm,
    image_ref,
    pass_ref,
    matched_ref,
    turned_ref,
    out_ref,
    warp_rows_ref,
    warp_columns_ref,
    fetch_sems,
    load_sems,
    store_sems,
):
    tile_rows, width = image_ref.shape
    parts = tile_rows // BLOCK
    across = width // BLOCK
    items = parts * across
    pitch = items + PAD
    myself = my_device()
    weight = weight_ref[lax.axis_index("exp"), lax.axis_index("tile")]
    fetch = wide_copy(image_hbm, image_ref, fetch_sems, 0, tile_rows)
    loads = [
        pltpu.make_async_copy(bank_rows_ref, warp_rows_ref, load_sems.at[0]),
        pltpu.make_async_copy(bank_columns_ref, warp_columns_ref, load_sems.at[1]),
    ]
    for index in range(width // WIDE):
        fetch(index).start()
    for load in loads:
        load.start()

    strips = [
        (0, BLOCK, [(above_ref, 0, RIM, 0), (image_ref, 0, BLOCK + RIM, 0)]),
        (BLOCK, BLOCK, [(image_ref, BLOCK - RIM, BLOCK + RIM, 0), (below_ref, 0, RIM, 0)]),
    ]
    step = functools.partial(
        row_step, strips=strips, coef_ref=coef_ref, rows_ref=rows_ref, pass_ref=pass_ref
    )

    def match_step(index):
        for inner, summed in enumerate(column_step(index, tile_rows, columns_ref, pass_ref)):
            matched_ref[:, pl.ds(pl.multiple_of(index * WIDE + inner * CHUNK, CHUNK), CHUNK)] = (
                summed.astype(jnp.bfloat16)
            )

    passes(fetch, step, match_step, pass_ref, width)
    for load in loads:
        load.wait()

    @pl.loop(0, across // 4)
    def _(quad):
        todo = []
        for part in range(parts):
            for inner in range(4):
                column = quad * 4 + inner
                ident = ident_ref[myself, part * across + column]
                piece = matched_ref[
                    part * BLOCK : (part + 1) * BLOCK,
                    pl.ds(pl.multiple_of(column * BLOCK, BLOCK), BLOCK),
                ]
                todo.append((part * across + column, ident, piece))
        todo = [
            (
                item,
                ident,
                jnp.dot(warp_rows_ref[ident], piece, preferred_element_type=jnp.float32).astype(
                    jnp.bfloat16
                ),
            )
            for item, ident, piece in todo
        ]
        todo = [
            (
                item,
                lax.dot_general(
                    first,
                    warp_columns_ref[ident],
                    (((1,), (1,)), ((), ())),
                    preferred_element_type=jnp.float32,
                ),
            )
            for item, ident, first in todo
        ]
        for item, second in todo:
            turned_ref[pl.ds(item, BLOCK, stride=pitch), :] = weight * second

    lines = out_ref.shape[0] // GROUPS

    def store(group):
        at = pl.ds(pl.multiple_of(group * lines, lines), lines)
        return pltpu.make_async_copy(out_ref.at[at], out_hbm.at[at], store_sems.at[group])

    for group in range(GROUPS):

        @pl.loop(group * BLOCK // GROUPS, (group + 1) * BLOCK // GROUPS, unroll=2)
        def _(row):
            to = pl.ds(pl.multiple_of(row * items, items), items)
            at = pl.ds(pl.multiple_of(row * pitch, PAD), items)
            out_ref[to, :] = turned_ref[at, :].astype(jnp.bfloat16)

        store(group).start()
    for group in range(GROUPS):
        store(group).wait()


def forward(
    ident, weight, coef, above, image, below, rows, columns, warp_rows, warp_columns
):
    tile_rows, width = image.shape
    bases = rows.shape[0] // BLOCK
    lines = tile_rows * width // BLOCK
    return pl.pallas_call(
        forward_kernel,
        out_shape=jax.ShapeDtypeStruct((lines, BLOCK), jnp.bfloat16),
        in_specs=[SMEM, SMEM, SMEM, VMEM, HBM, VMEM, VMEM, VMEM, HBM, HBM],
        out_specs=HBM,
        scratch_shapes=[
            pltpu.VMEM((tile_rows, width), jnp.bfloat16),
            pltpu.VMEM((bases, tile_rows, width + 2 * BLOCK), jnp.bfloat16),
            pltpu.VMEM((tile_rows, width), jnp.bfloat16),
            pltpu.VMEM((lines + BLOCK * PAD, BLOCK), jnp.float32),
            pltpu.VMEM((lines, BLOCK), jnp.bfloat16),
            pltpu.VMEM(warp_rows.shape, jnp.bfloat16),
            pltpu.VMEM(warp_columns.shape, jnp.bfloat16),
            pltpu.SemaphoreType.DMA((width // WIDE,)),
            pltpu.SemaphoreType.DMA((2,)),
            pltpu.SemaphoreType.DMA((GROUPS,)),
        ],
        compiler_params=grant(58),
        name="match_warp",
    )(ident, weight, coef, above, image, below, rows, columns, warp_rows, warp_columns)


def slots_kernel(
    slot_hbm, repeat_ref, arrived_ref, scale_ref, template_ref, coadd_ref, wide_ref, *refs
):
    del scale_ref
    items, _, sources = slot_hbm.shape
    sums, tables, sems = refs[:SUMS], refs[SUMS : SUMS + items], refs[SUMS + items]
    loads = [pltpu.make_async_copy(slot_hbm.at[k], tables[k], sems.at[k]) for k in range(items)]
    for load in loads:
        load.start()

    def at(source):
        return pl.ds(pl.multiple_of(source * items, items), items)

    @pl.loop(0, sources, unroll=2)
    def _(source):
        wide_ref[at(source), :] = arrived_ref[at(source), :].astype(jnp.float32)
        for sum_ref in sums:
            sum_ref[at(source), :] = jnp.zeros((items, BLOCK), jnp.float32)

    for load in loads:
        load.wait()

    def add(source, blocks, sum_ref):
        slots = [tables[block][0, source] for block in blocks]
        values = [
            sum_ref[pl.ds(slot, 1), :] + wide_ref[pl.ds(source * items + block, 1), :]
            for slot, block in zip(slots, blocks)
        ]
        for slot, value in zip(slots, values):
            sum_ref[pl.ds(slot, 1), :] = value

    groups = [list(range(first, first + LANES)) for first in range(0, items, LANES)]

    @pl.loop(0, sources)
    def _(source):
        repeats = repeat_ref[0, source]

        @pl.when(repeats == 0)
        def _():
            for index, blocks in enumerate(groups):
                add(source, blocks, sums[index % SUMS])

        @pl.when(repeats != 0)
        def _():
            for index, blocks in enumerate(groups):
                repeated = (repeats // 2**index) % 2

                @pl.when(repeated == 0)
                def _():
                    add(source, blocks, sums[index % SUMS])

                @pl.when(repeated != 0)
                def _():
                    for lane, block in enumerate(blocks):
                        add(source, [block], sums[lane % SUMS])

    @pl.loop(0, sources, unroll=2)
    def _(source):
        value = sums[0][at(source), :]
        for sum_ref in sums[1:]:
            value = value + sum_ref[at(source), :]
        sums[0][at(source), :] = value
        coadd_ref[at(source), :] = value.astype(jnp.bfloat16)

    @pl.loop(0, sources)
    def _(source):
        for item in range(items):
            slot = tables[item][0, source]
            wide_ref[pl.ds(source * items + item, 1), :] = sums[0][pl.ds(slot, 1), :]

    @pl.loop(0, sources, unroll=4)
    def _(source):
        template_ref[at(source), :] = wide_ref[at(source), :].astype(jnp.bfloat16)


def group_repeats(slots):
    grouped = slots.T.reshape(-1, LANES, slots.shape[0])
    repeated = jnp.zeros(grouped[:, 0].shape, jnp.bool_)
    for later in range(1, LANES):
        for earlier in range(later):
            repeated = repeated | (grouped[:, later] == grouped[:, earlier])
    bits = 2 ** jnp.arange(grouped.shape[0], dtype=jnp.int32)
    return jnp.sum(jnp.where(repeated, bits[:, None], 0), axis=0, keepdims=True)


def slot_sums(slots, arrived, scale):
    shape = jax.ShapeDtypeStruct(arrived.shape, jnp.bfloat16)
    sources, items = slots.shape
    return pl.pallas_call(
        slots_kernel,
        out_shape=(shape, shape),
        in_specs=[ANY, SMEM, VMEM, SMEM],
        out_specs=(VMEM, VMEM),
        scratch_shapes=[pltpu.VMEM(arrived.shape, jnp.float32)] * (1 + SUMS)
        + [pltpu.SMEM((1, sources), jnp.int32)] * items
        + [pltpu.SemaphoreType.DMA((items,))],
        compiler_params=grant(28),
        name="slot_sums",
    )(slots.T.reshape(items, 1, sources), group_repeats(slots), arrived, scale)


def unwarp_kernel(
    ident_ref,
    scale_ref,
    returned_ref,
    bank_rows_ref,
    bank_columns_ref,
    out_ref,
    top_ref,
    under_top_ref,
    over_bottom_ref,
    bottom_ref,
    wide_ref,
    warp_rows_ref,
    warp_columns_ref,
    sems,
):
    tile_rows, part_width = out_ref.shape
    across = part_width // BLOCK
    parts = tile_rows // BLOCK
    items = parts * across
    pitch = items + PAD
    myself = my_device()
    loads = [
        pltpu.make_async_copy(bank_rows_ref, warp_rows_ref, sems.at[0]),
        pltpu.make_async_copy(bank_columns_ref, warp_columns_ref, sems.at[1]),
    ]
    for load in loads:
        load.start()

    @pl.loop(0, BLOCK, unroll=4)
    def _(row):
        to = pl.ds(pl.multiple_of(row * pitch, PAD), items)
        at = pl.ds(pl.multiple_of(row * items, items), items)
        wide_ref[to, :] = returned_ref[at, :].astype(jnp.float32)

    for load in loads:
        load.wait()

    @pl.loop(0, across // 4)
    def _(quad):
        todo = []
        for part in range(parts):
            for inner in range(4):
                column = quad * 4 + inner
                item = part * across + column
                ident = ident_ref[myself, item]
                numerator = wide_ref[pl.ds(item, BLOCK, stride=pitch), :].astype(jnp.bfloat16)
                todo.append((part, column, item, ident, numerator))
        todo = [
            (
                part,
                column,
                ident,
                scale_ref[0, item]
                * lax.dot_general(
                    warp_rows_ref[ident],
                    numerator,
                    (((0,), (0,)), ((), ())),
                    preferred_element_type=jnp.float32,
                ),
            )
            for part, column, item, ident, numerator in todo
        ]
        for part, column, ident, first in todo:
            image = jnp.dot(
                first.astype(jnp.bfloat16),
                warp_columns_ref[ident],
                preferred_element_type=jnp.float32,
            ).astype(jnp.bfloat16)
            to = pl.ds(pl.multiple_of(column * BLOCK, BLOCK), BLOCK)
            out_ref[part * BLOCK : (part + 1) * BLOCK, to] = image
            if part == 0:
                top_ref[:, to] = image[:RIM]
                under_top_ref[:, to] = image[RIM : 2 * RIM]
            if part == parts - 1:
                over_bottom_ref[:, to] = image[BLOCK - 2 * RIM : BLOCK - RIM]
                bottom_ref[:, to] = image[BLOCK - RIM :]


def unwarp(ident, scale, returned, warp_rows, warp_columns, tile_rows):
    lines = returned.shape[0]
    part_width = lines * BLOCK // tile_rows
    rim = jax.ShapeDtypeStruct((RIM, part_width), jnp.bfloat16)
    return pl.pallas_call(
        unwarp_kernel,
        out_shape=(jax.ShapeDtypeStruct((tile_rows, part_width), jnp.bfloat16),) + (rim,) * 4,
        in_specs=[SMEM, SMEM, VMEM, ANY, ANY],
        out_specs=(VMEM,) * 5,
        scratch_shapes=[
            pltpu.VMEM((lines + BLOCK * PAD, BLOCK), jnp.float32),
            pltpu.VMEM(warp_rows.shape, jnp.bfloat16),
            pltpu.VMEM(warp_columns.shape, jnp.bfloat16),
            pltpu.SemaphoreType.DMA((2,)),
        ],
        compiler_params=grant(58),
        name="unwarp",
    )(ident, scale, returned, warp_rows, warp_columns)


def inner_strips(image_ref):
    tile_rows = image_ref.shape[0]
    return [
        (0, BLOCK, [(image_ref, 0, WINDOW, 0)]),
        (BLOCK, tile_rows - 2 * RIM - BLOCK, [(image_ref, BLOCK, tile_rows - BLOCK, 0)]),
    ]


def inner_kernel(
    coef_ref,
    image_hbm,
    exposure_hbm,
    rows_ref,
    columns_ref,
    out_ref,
    image_ref,
    exposure_ref,
    pass_ref,
    stage_ref,
    fetch_sems,
    load_sem,
    sems,
):
    tile_rows, width = image_ref.shape
    inner = tile_rows - 2 * RIM
    fetch = wide_copy(image_hbm, image_ref, fetch_sems, 0, tile_rows)
    load = pltpu.make_async_copy(exposure_hbm.at[pl.ds(RIM, inner)], exposure_ref, load_sem)
    for index in range(width // WIDE):
        fetch(index).start()
    load.start()
    step = functools.partial(
        row_step,
        strips=inner_strips(image_ref),
        coef_ref=coef_ref,
        rows_ref=rows_ref,
        pass_ref=pass_ref,
    )

    def store(index):
        at = pl.ds(pl.multiple_of(index * WIDE, WIDE), WIDE)
        return pltpu.make_async_copy(
            stage_ref.at[:, at], out_ref.at[pl.ds(RIM, inner), at], sems.at[index]
        )

    def subtract_step(index):
        for part, summed in enumerate(column_step(index, inner, columns_ref, pass_ref)):
            at = pl.ds(pl.multiple_of(index * WIDE + part * CHUNK, CHUNK), CHUNK)
            stage_ref[:, at] = exposure_ref[:, at].astype(jnp.float32) - summed
        store(index).start()

    passes(fetch, step, subtract_step, pass_ref, width, load)

    @pl.loop(0, width // WIDE)
    def _(index):
        store(index).wait()


def subtract_inner(coef, image, exposure, rows, columns):
    tile_rows, width = image.shape
    bases = rows.shape[0] // BLOCK
    inner = tile_rows - 2 * RIM
    return pl.pallas_call(
        inner_kernel,
        out_shape=jax.ShapeDtypeStruct((tile_rows, width), jnp.float32),
        in_specs=[SMEM, HBM, HBM, VMEM, VMEM],
        out_specs=HBM,
        scratch_shapes=[
            pltpu.VMEM((tile_rows, width), jnp.bfloat16),
            pltpu.VMEM((inner, width), jnp.bfloat16),
            pltpu.VMEM((bases, inner, width + 2 * BLOCK), jnp.bfloat16),
            pltpu.VMEM((inner, width), jnp.float32),
            pltpu.SemaphoreType.DMA((width // WIDE,)),
            pltpu.SemaphoreType.DMA,
            pltpu.SemaphoreType.DMA((width // WIDE,)),
        ],
        compiler_params=grant(58),
        name="subtract_inner",
    )(coef, image, exposure, rows, columns)


def outer_kernel(
    coef_ref,
    above_ref,
    top_ref,
    under_top_ref,
    over_bottom_ref,
    bottom_ref,
    below_ref,
    exposure_hbm,
    rows_ref,
    columns_ref,
    partial_hbm,
    out_hbm,
    order_ref,
    exposure_ref,
    pass_ref,
    stage_ref,
    fetch_sems,
    store_sems,
):
    del partial_hbm
    tile_rows, width = out_hbm.shape
    order_ref[...] = jnp.zeros_like(order_ref)

    def ends(index):
        first = index * (tile_rows - RIM)
        here, there = pl.ds(index * RIM, RIM), pl.ds(first, RIM)
        return (
            pltpu.make_async_copy(
                exposure_hbm.at[there], exposure_ref.at[here], fetch_sems.at[index]
            ),
            pltpu.make_async_copy(stage_ref.at[here], out_hbm.at[there], store_sems.at[index]),
        )

    fetches, stores = zip(*(ends(index) for index in range(2)))
    for fetch in fetches:
        fetch.start()
    strips = [
        (0, RIM, [(ref, 0, RIM, 0) for ref in (above_ref, top_ref, under_top_ref)]),
        (RIM, RIM, [(ref, 0, RIM, 0) for ref in (over_bottom_ref, bottom_ref, below_ref)]),
    ]
    clear(pass_ref, 0)
    clear(pass_ref, BLOCK + width)
    for index in range(width // WIDE):
        row_step(
            WIDE, index * WIDE, BLOCK + index * WIDE, strips, coef_ref, rows_ref, pass_ref
        )
    for fetch in fetches:
        fetch.wait()

    def subtract(at, summed):
        stage_ref[:, at] = exposure_ref[:, at].astype(jnp.float32) - summed

    column_strip(2 * RIM, columns_ref, pass_ref, subtract)
    for store in stores:
        store.start()
    for store in stores:
        store.wait()


def subtract_outer(coef, rims, exposure, rows, columns, partial):
    tile_rows, width = exposure.shape
    bases = rows.shape[0] // BLOCK
    operands = (coef, *rims, exposure, rows, columns, partial)
    return pl.pallas_call(
        outer_kernel,
        out_shape=(
            jax.ShapeDtypeStruct((tile_rows, width), jnp.float32),
            jax.ShapeDtypeStruct((SLOT_ROWS, BLOCK), jnp.float32),
        ),
        in_specs=[SMEM] + [VMEM] * len(rims) + [HBM, VMEM, VMEM, HBM],
        out_specs=(HBM, VMEM),
        scratch_shapes=[
            pltpu.VMEM((2 * RIM, width), jnp.bfloat16),
            pltpu.VMEM((bases, 2 * RIM, width + 2 * BLOCK), jnp.bfloat16),
            pltpu.VMEM((2 * RIM, width), jnp.float32),
            pltpu.SemaphoreType.DMA((2,)),
            pltpu.SemaphoreType.DMA((2,)),
        ],
        input_output_aliases={len(operands) - 1: 0},
        compiler_params=grant(16),
        name="subtract_outer",
    )(*operands)


def patch_kernel(scale_ref, owned_ref, order_ref, out_hbm, wide_ref, stage_ref, store_sems):
    del order_ref
    slots = SLOT_ROWS * SLOT_COLS
    pitch = slots + PAD
    myself = my_device()

    @pl.loop(0, BLOCK, unroll=4)
    def _(row):
        to = pl.ds(pl.multiple_of(row * pitch, PAD), slots)
        at = pl.ds(pl.multiple_of(row * slots, slots), slots)
        wide_ref[to, :] = owned_ref[at, :].astype(jnp.float32)

    def store(down):
        at = pl.ds(pl.multiple_of(down * BLOCK, BLOCK), BLOCK)
        return pltpu.make_async_copy(stage_ref.at[at], out_hbm.at[at], store_sems.at[down])

    @pl.loop(0, SLOT_ROWS)
    def _(down):
        to = pl.ds(pl.multiple_of(down * BLOCK, BLOCK), BLOCK)
        for across in range(SLOT_COLS):
            slot = down * SLOT_COLS + across
            stage_ref[to, across * BLOCK : (across + 1) * BLOCK] = (
                scale_ref[myself, slot] * wide_ref[pl.ds(slot, BLOCK, stride=pitch), :]
            )
        store(down).start()

    @pl.loop(0, SLOT_ROWS)
    def _(down):
        store(down).wait()


def patch(scale, owned, order):
    shape = (SLOT_ROWS * BLOCK, SLOT_COLS * BLOCK)
    return pl.pallas_call(
        patch_kernel,
        out_shape=jax.ShapeDtypeStruct(shape, jnp.float32),
        in_specs=[SMEM, VMEM, VMEM],
        out_specs=HBM,
        scratch_shapes=[
            pltpu.VMEM((owned.shape[0] + BLOCK * PAD, BLOCK), jnp.float32),
            pltpu.VMEM(shape, jnp.float32),
            pltpu.SemaphoreType.DMA((SLOT_ROWS,)),
        ],
        compiler_params=grant(12),
        name="patch",
    )(scale, owned, order)


def exchange(rows, devices):
    shaped = rows.reshape(devices, -1, BLOCK)
    moved = lax.all_to_all(shaped, ("exp", "tile"), split_axis=0, concat_axis=0, tiled=True)
    return moved.reshape(rows.shape)


def shards(
    exposure,
    row_taps,
    column_taps,
    basis_coef,
    warp_rows,
    warp_columns,
    warp_id,
    route_device,
    route_slot,
    weight,
):
    devices = lax.axis_size("exp") * lax.axis_size("tile")
    image = exposure[0]
    tile_rows, width = image.shape
    per_tile = tile_rows * width // (BLOCK * BLOCK)
    slot_count = SLOT_ROWS * SLOT_COLS
    ident = warp_id.reshape(devices, per_tile)

    above, below = swap_rims(image[:RIM], image[tile_rows - RIM :])
    rows, columns = band_matrices(row_taps, column_taps)
    weighted = forward(
        ident,
        weight,
        basis_coef,
        above,
        image,
        below,
        rows,
        columns,
        warp_rows,
        warp_columns,
    )
    arrived = exchange(weighted, devices)

    owner = route_device.reshape(-1)
    place = route_slot.reshape(-1)
    block_weight = jnp.repeat(weight.reshape(-1), per_tile)
    by_owner = jnp.where(
        owner[None, :] == jnp.arange(devices, dtype=jnp.int32)[:, None], block_weight[None, :], 0.0
    )
    by_place = (place[:, None] == jnp.arange(slot_count, dtype=jnp.int32)[None, :]).astype(
        jnp.float32
    )
    total = jnp.dot(by_owner, by_place, precision=lax.Precision.HIGHEST)
    scale = 1.0 / jnp.maximum(total, 1.0)
    slots = (route_device * slot_count + route_slot).reshape(devices, per_tile)
    my_slots = lax.dynamic_slice_in_dim(slots, my_device(), 1, 0)
    block_scale = scale.reshape(-1)[my_slots]

    template_rows, coadd_rows = slot_sums(slots, arrived, block_scale)
    returned = exchange(template_rows, devices)
    owned = exchange(coadd_rows, devices)

    template, top, under_top, over_bottom, bottom = unwarp(
        ident, block_scale, returned, warp_rows, warp_columns, tile_rows
    )
    above, below = swap_rims(top, bottom)
    difference = subtract_inner(basis_coef, template, image, rows, columns)
    rims = (above, top, under_top, over_bottom, bottom, below)
    difference, order = subtract_outer(basis_coef, rims, image, rows, columns, difference)
    return patch(scale, owned, order), difference[None]


def solution(mesh):
    placed = (P("exp", "tile", None), P(), P(), P("exp", None), P(), P(), P(), P(), P(), P())
    return jax.shard_map(
        shards,
        mesh=mesh,
        in_specs=placed,
        out_specs=(P("exp", "tile"), P("exp", "tile", None)),
        check_vma=False,
    )
```
